128 devices in a mesh: dp: 16 (over y, x), head: 8 (over z, core).
Axes of the slice: x: 4, y: 4, z: 4, core: 2. Of those that a mesh axis runs over, the one named last changes fastest.
Arguments:
- slot_token_ids: int32 [128, 512], P('dp'), may hold values from 0 to 50264
- lengths: int32 [128], P('dp'), may hold values from 64 to 512, as said below
- labels: int32 [128], P('dp'), may hold values from 0 to 2
- optimizer_step_count: int32 [], replicated, may hold values from 2 to 20
- token_embedding_table: bfloat16 [50304, 1024], P('dp', 'head'), may hold values from -6 to 6
- positions: bfloat16 [512, 1024], replicated, may hold values from -4 to 4
- query_key_value_weight: bfloat16 [3, 1024, 1024], P(None, None, 'head'), may hold values from -0.1875 to 0.1875
- attention_output_weight: bfloat16 [1024, 1024], P('head'), may hold values from -0.8 to 0.8
- feedforward_input_weight: bfloat16 [1024, 4096], P(None, 'head'), may hold values from -0.1875 to 0.1875
- feedforward_output_weight: bfloat16 [4096, 1024], P('head'), may hold values from -0.09375 to 0.09375
- layer_norm_gains: float32 [3, 1024], replicated, may hold values from 0.5 to 1.5
- layer_norm_biases: float32 [3, 1024], replicated, may hold values from -2 to 2
- classifier: bfloat16 [3, 1024], replicated, may hold values from -0.75 to 0.75
- adapter_down_maps: float32 [2, 1024, 16], replicated, may hold values from -0.1875 to 0.1875
- adapter_up_maps: float32 [2, 16, 1024], P(None, None, 'head'), may hold values from -1.5 to 1.5
- down_first_moment: float32 [2, 1024, 16], P(None, 'dp'), may hold values from -0.0078125 to 0.0078125
- down_second_moment: float32 [2, 1024, 16], P(None, 'dp'), may hold values from 2.1972657e-08 to 9.1552735e-08
- up_first_moment: float32 [2, 16, 1024], P(None, None, ('head', 'dp')), may hold values from -0.0078125 to 0.0078125
- up_second_moment: float32 [2, 16, 1024], P(None, None, ('head', 'dp')), may hold values from 2.1972657e-08 to 9.1552735e-08
- down_privacy_noise: float32 [2, 1024, 16], P(None, 'dp'), may hold values from -6 to 6
- up_privacy_noise: float32 [2, 16, 1024], P(None, None, ('head', 'dp')), may hold values from -6 to 6
Outputs:
- loss: float32 [], replicated
- example_norms: float32 [128], P(('dp', 'head'))
- a_moment1: float32 [2, 1024, 16], P(None, 'dp')
- a_moment2: float32 [2, 1024, 16], P(None, 'dp')
- a_weight: float32 [2, 1024, 16], P(None, 'dp')
- b_moment1: float32 [2, 16, 1024], P(None, None, ('head', 'dp'))
- b_moment2: float32 [2, 16, 1024], P(None, None, ('head', 'dp'))
- b_weight: float32 [2, 16, 1024], P(None, None, ('head', 'dp'))
- lamb_norms: float32 [4, 2], replicated
The draws below stay inside these ranges and needn't reach their ends.
Inputs may be any that keep to these rules, and one draw needn't show every extreme that they name: `lengths`: valid tokens of each example; some example has exactly 512.
All inputs are finite; a program needn't handle non-finite values.
Results may differ from the reference program's by a relative error of at most 0.0059.
Values may be sent and summed in bfloat16 or wider, within the bound.
No kernel may reach another device: no remote copies, remote signals or barrier semaphores. Data moves between devices by JAX's collectives and lax.ppermute only.
A program may use at most 256 MiB of HBM per device.

```python
import math
import jax
import jax.numpy as jnp
import numpy as np
from jax import lax

MODEL_WIDTH = 1024
HEADS = 16
HDIM = 64
FF = 4096
VOCAB = 50265
ADAPTER_RANK = 16
CLASSES = 3
SEQ = 512
EXAMPLES = 128
VOCAB_ROWS = 50304


def draw_lengths(key, part):
    raw = jax.random.randint(key, (EXAMPLES,), SEQ // 8, SEQ + 1)
    return raw.at[0].set(SEQ).astype(jnp.int32)


def draw_attention_output_weight(key, part):
    row_place = jnp.arange(MODEL_WIDTH, dtype=jnp.float32) / MODEL_WIDTH
    row_scale = jnp.power(10.0, row_place) / 4.64
    entries = jax.random.normal(key, (MODEL_WIDTH, MODEL_WIDTH), jnp.float32)
    values = entries * (8.0 / MODEL_WIDTH) ** 0.5 * row_scale[:, None]
    return jnp.clip(values, -0.796875, 0.796875).astype(jnp.bfloat16)


def set_ends(values, key, least, top_value):
    dims = values.shape
    index_at = [jax.random.randint(jax.random.fold_in(key, axis), (), 0, dims[axis]) for axis in range(len(dims))]
    values = values.at[tuple(index_at)].set(least)
    longest = dims.index(max(dims))
    index_at[longest] = (index_at[longest] + 1) % dims[longest]
    return values.at[tuple(index_at)].set(top_value)


def steps_of(stream_key, dims, pieces, least, high):
    def one(axis_at, parts):
        steps = jax.random.uniform(jax.random.fold_in(jax.random.fold_in(stream_key, 6), axis_at), (parts,), jnp.float32, least / len(pieces), high / len(pieces))
        return jnp.repeat(jnp.exp(steps), dims[axis_at] // parts).reshape((-1,) + (1,) * (len(dims) - axis_at - 1))

    level = one(*pieces[0])
    for cut in pieces[1:]:
        level = level * one(*cut)
    return level


def rank_bounds(amount, lean):
    weights = [(1 << 20) // math.isqrt(rank ** lean) + 1 for rank in range(1, amount + 1)]
    spread = 1 + sum(weights) // (1 << 30)
    return np.cumsum(np.array([max(1, weight // spread) for weight in weights]))


def ranked(stream_key, shape, amount, slope):
    grid = rank_bounds(amount, slope)
    pick = jax.random.randint(jax.random.fold_in(stream_key, 1), shape, 0, int(grid[amount - 1]))
    rank = jnp.searchsorted(jnp.asarray(grid, jnp.int32), pick, side="right")
    return jax.random.permutation(jax.random.fold_in(stream_key, 2), amount)[rank].astype(jnp.int32)


def scatter_about(own_key, extent, deviation, most, pieces=(), kind=jnp.bfloat16):
    level = steps_of(own_key, extent, pieces, -0.22, 0.18) if pieces else 1.0
    array = jax.random.normal(own_key, extent, jnp.float32) * deviation * level
    return jnp.minimum(jnp.maximum(array, -most), most).astype(kind)


def setup_inputs(seed: int = 0) -> dict:
    seeds = jax.random.split(jax.random.key(seed), 22)
    slot_token_ids = set_ends(ranked(seeds[0], (EXAMPLES, SEQ), VOCAB, 2), jax.random.fold_in(seeds[0], 3), 0, VOCAB - 1).astype(jnp.int32)
    lengths = draw_lengths(jax.random.fold_in(seeds[21], 71), 0)
    labels = set_ends(jax.random.randint(seeds[2], (EXAMPLES,), 0, 3), jax.random.fold_in(seeds[2], 1), 0, 2).astype(jnp.int32)
    optimizer_step_count = jax.random.randint(seeds[3], (), 2, 21).astype(jnp.int32)
    token_embedding_table = scatter_about(seeds[4], (VOCAB_ROWS, MODEL_WIDTH), 1.0, 6.0, ((0, 16), (1, 8)))
    positions = scatter_about(seeds[5], (SEQ, MODEL_WIDTH), 0.5, 4.0)
    query_key_value_weight = scatter_about(seeds[6], (3, MODEL_WIDTH, MODEL_WIDTH), MODEL_WIDTH ** -0.5, 0.1875, ((2, 8),))
    attention_output_weight = draw_attention_output_weight(jax.random.fold_in(seeds[21], 71), 0)
    feedforward_input_weight = scatter_about(seeds[8], (MODEL_WIDTH, FF), MODEL_WIDTH ** -0.5, 0.1875, ((1, 8),))
    feedforward_output_weight = scatter_about(seeds[9], (FF, MODEL_WIDTH), FF ** -0.5, 0.09375, ((0, 8),))
    layer_norm_gains = jnp.clip(1.0 + 0.1 * jax.random.normal(seeds[10], (3, MODEL_WIDTH), jnp.float32), 0.5, 1.5)
    layer_norm_biases = scatter_about(seeds[11], (3, MODEL_WIDTH), 0.3, 2.0, (), jnp.float32)
    classifier = scatter_about(seeds[12], (CLASSES, MODEL_WIDTH), (MODEL_WIDTH // 16) ** -0.5, 0.75)
    adapter_down_maps = scatter_about(seeds[13], (2, MODEL_WIDTH, ADAPTER_RANK), MODEL_WIDTH ** -0.5, 0.1875, (), jnp.float32)
    adapter_up_maps = scatter_about(seeds[14], (2, ADAPTER_RANK, MODEL_WIDTH), ADAPTER_RANK ** -0.5, 1.5, ((2, 8),), jnp.float32)
    down_first_moment = scatter_about(seeds[15], (2, MODEL_WIDTH, ADAPTER_RANK), (0.07 / EXAMPLES), 0.0078125, ((1, 16),), jnp.float32)
    down_second_moment = jnp.clip(jnp.exp(math.log(9.155273517080786e-08) - 1.42711635 * jax.random.uniform(seeds[16], (2, MODEL_WIDTH, ADAPTER_RANK), jnp.float32) ** steps_of(seeds[16], (2, MODEL_WIDTH, ADAPTER_RANK), ((1, 16),), -0.2, 0.2)), 2.1972656583102435e-08, 9.155273517080786e-08)
    up_first_moment = scatter_about(seeds[17], (2, ADAPTER_RANK, MODEL_WIDTH), (0.07 / EXAMPLES), 0.0078125, ((2, 128),), jnp.float32)
    up_second_moment = jnp.clip(jnp.exp(math.log(9.155273517080786e-08) - 1.42711635 * jax.random.uniform(seeds[18], (2, ADAPTER_RANK, MODEL_WIDTH), jnp.float32) ** steps_of(seeds[18], (2, ADAPTER_RANK, MODEL_WIDTH), ((2, 128),), -0.2, 0.2)), 2.1972656583102435e-08, 9.155273517080786e-08)
    down_privacy_noise = scatter_about(seeds[19], (2, MODEL_WIDTH, ADAPTER_RANK), 1.0, 6.0, ((1, 16),), jnp.float32)
    up_privacy_noise = scatter_about(seeds[20], (2, ADAPTER_RANK, MODEL_WIDTH), 1.0, 6.0, ((2, 128),), jnp.float32)
    return {"slot_token_ids": slot_token_ids, "lengths": lengths, "labels": labels, "optimizer_step_count": optimizer_step_count, "token_embedding_table": token_embedding_table, "positions": positions, "query_key_value_weight": query_key_value_weight, "attention_output_weight": attention_output_weight, "feedforward_input_weight": feedforward_input_weight, "feedforward_output_weight": feedforward_output_weight, "layer_norm_gains": layer_norm_gains, "layer_norm_biases": layer_norm_biases, "classifier": classifier, "adapter_down_maps": adapter_down_maps, "adapter_up_maps": adapter_up_maps, "down_first_moment": down_first_moment, "down_second_moment": down_second_moment, "up_first_moment": up_first_moment, "up_second_moment": up_second_moment, "down_privacy_noise": down_privacy_noise, "up_privacy_noise": up_privacy_noise}


@jax.custom_vjp
def reduced_rows(v):
    return lax.optimization_barrier(v.astype(jnp.bfloat16)).astype(jnp.float32)

@jax.custom_vjp
def reduced_backward(v):
    return v

def low_keep(v):
    return (reduced_rows(v), None)

def low_pass(kept, grad):
    return (grad,)

def back_keep(v):
    return (v, None)

def back_low(kept, grad):
    return (reduced_rows(grad),)
reduced_rows.defvjp(low_keep, low_pass)
reduced_backward.defvjp(back_keep, back_low)
precise = lax.Precision.HIGHEST
adapter_scale = 2.0
clip_bound = 1.0
noise_mult = 0.6
smooth_rate = 0.1
beta_one = 0.9
beta_two = 0.999
adam_eps = 1e-06
decay_rate = 0.01
learn_rate = 0.25
norm_eps = 1e-05

def precise_product(left, right):
    return jnp.dot(left, right, precision=precise)

def layer_norm(inputs, gain, bias):
    centre = inputs - lax.optimization_barrier(jnp.mean(inputs, -1, keepdims=True))
    return centre * lax.rsqrt(lax.optimization_barrier(jnp.mean(centre * centre, -1, keepdims=True)) + norm_eps) * gain + bias

def single_example_loss(adapter_down, adapter_up, hidden_initial, example_length, class_label, frozen_params):
    query_weight, w_k, value_weight, w_o, w_in, w_out, gains, biases, class_w = frozen_params
    hidden_reduced = reduced_rows(hidden_initial)
    down_reduced = reduced_rows(adapter_down)
    up_reduced = reduced_rows(adapter_up)
    adapter_activation = reduced_rows(reduced_backward(precise_product(hidden_reduced, jnp.concatenate([down_reduced[0], down_reduced[1]], 1))))
    query_rows = reduced_rows(reduced_backward(precise_product(hidden_reduced, query_weight) + adapter_scale * precise_product(adapter_activation[:, :ADAPTER_RANK], up_reduced[0])))
    keys = reduced_rows(precise_product(hidden_reduced, w_k))
    value_rows = reduced_rows(reduced_backward(precise_product(hidden_reduced, value_weight) + adapter_scale * precise_product(adapter_activation[:, ADAPTER_RANK:], up_reduced[1])))
    shape3 = (SEQ, HEADS, HDIM)
    valid_mask = jnp.arange(SEQ) < example_length
    scores = jnp.einsum('qhd,khd->hqk', query_rows.reshape(shape3), keys.reshape(shape3), precision=precise) * HDIM ** (-0.5)
    scores = reduced_backward(jnp.where(valid_mask[None, None, :], scores, -1e+30))
    attn_prob = jax.nn.softmax(scores, -1)
    context = jnp.einsum('hqk,khd->qhd', reduced_rows(attn_prob), value_rows.reshape(shape3), precision=precise)
    context = reduced_rows(reduced_backward(context.reshape(SEQ, MODEL_WIDTH)))
    attn_out = reduced_backward(precise_product(context, w_o))
    hidden_one = layer_norm(hidden_initial + attn_out, gains[1], biases[1])
    ffn_pre = reduced_backward(precise_product(reduced_rows(hidden_one), w_in))
    ffn_branch = reduced_backward(precise_product(reduced_rows(jax.nn.gelu(ffn_pre, approximate=False)), w_out))
    hidden_two = layer_norm(hidden_one + ffn_branch, gains[2], biases[2])
    valid_f = valid_mask.astype(jnp.float32)
    pooled = lax.optimization_barrier(jnp.sum(hidden_two * valid_f[:, None], 0)) / example_length.astype(jnp.float32)
    logits = precise_product(reduced_rows(pooled), class_w.T)
    log_prob = jax.nn.log_softmax(logits)
    target = (1.0 - smooth_rate) * jax.nn.one_hot(class_label, CLASSES, dtype=jnp.float32) + smooth_rate / CLASSES
    return -jnp.sum(target * log_prob)

def layerwise_adaptive_step(weight, grad, first, second, step_number):
    first_new = beta_one * first + (1.0 - beta_one) * grad
    second_new = beta_two * second + (1.0 - beta_two) * grad * grad
    direction = first_new / (1.0 - jnp.power(beta_one, step_number)) / (jnp.sqrt(second_new / (1.0 - jnp.power(beta_two, step_number))) + adam_eps) + decay_rate * weight
    weight_norm = jnp.sqrt(lax.optimization_barrier(jnp.sum(weight * weight, (1, 2))))
    dir_norm = jnp.sqrt(lax.optimization_barrier(jnp.sum(direction * direction, (1, 2))))
    new_weight = weight - learn_rate * (weight_norm / dir_norm)[:, None, None] * direction
    return (first_new, second_new, new_weight, jnp.stack([weight_norm, dir_norm], 1))

def reference(slot_token_ids, lengths, labels, optimizer_step_count, token_embedding_table, positions, query_key_value_weight, attention_output_weight, feedforward_input_weight, feedforward_output_weight, layer_norm_gains, layer_norm_biases, classifier, adapter_down_maps, adapter_up_maps, down_first_moment, down_second_moment, up_first_moment, up_second_moment, down_privacy_noise, up_privacy_noise):
    as_f = jnp.float32
    frozen_params = (query_key_value_weight[0].astype(as_f), query_key_value_weight[1].astype(as_f), query_key_value_weight[2].astype(as_f), attention_output_weight.astype(as_f), feedforward_input_weight.astype(as_f), feedforward_output_weight.astype(as_f), layer_norm_gains, layer_norm_biases, classifier.astype(as_f))
    pos_f = positions.astype(as_f)

    def one_example(inputs):
        ids_row, example_length, class_label = inputs
        hidden_initial = layer_norm(token_embedding_table[ids_row].astype(as_f) + pos_f, layer_norm_gains[0], layer_norm_biases[0])
        loss_amount, gather_rows = jax.vjp(lambda down_matrix, up_matrix: single_example_loss(down_matrix, up_matrix, hidden_initial, example_length, class_label, frozen_params), adapter_down_maps, adapter_up_maps)
        down_gradient, up_gradient = gather_rows(jnp.ones((), as_f))
        return (loss_amount, down_gradient, up_gradient)
    losses, grads_down, grads_up = lax.map(one_example, (slot_token_ids, lengths, labels))
    example_norms = jnp.sqrt(lax.optimization_barrier(jnp.sum(grads_down * grads_down, (1, 2, 3))) + lax.optimization_barrier(jnp.sum(grads_up * grads_up, (1, 2, 3))))
    factors = clip_bound / jnp.maximum(example_norms, clip_bound)
    sum_down = jnp.einsum('e,eabc->abc', factors, grads_down, precision=precise)
    sum_up = jnp.einsum('e,eabc->abc', factors, grads_up, precision=precise)
    down_gradient = (sum_down + noise_mult * clip_bound * down_privacy_noise) / EXAMPLES
    up_gradient = (sum_up + noise_mult * clip_bound * up_privacy_noise) / EXAMPLES
    step_number = optimizer_step_count.astype(as_f)
    down_momentum, down_velocity, updated_down, down_norms = layerwise_adaptive_step(adapter_down_maps, down_gradient, down_first_moment, down_second_moment, step_number)
    up_momentum, up_velocity, updated_up, up_norms = layerwise_adaptive_step(adapter_up_maps, up_gradient, up_first_moment, up_second_moment, step_number)
    loss = jnp.mean(losses)
    return (loss, example_norms, down_momentum, down_velocity, updated_down, up_momentum, up_velocity, updated_up, jnp.concatenate([down_norms, up_norms], 0))
```

```python
import functools

import jax
import jax.numpy as jnp
from jax import lax
from jax.experimental import pallas as pl
from jax.experimental.pallas import tpu as pltpu
from jax.sharding import PartitionSpec as P

HDIM = 64
CAP = 48
LANES = 128
MIB = 1 << 20

adapter_scale = 2.0
clip_bound = 1.0
noise_mult = 0.6
smooth_rate = 0.1
beta_one = 0.9
beta_two = 0.999
adam_eps = 1e-06
decay_rate = 0.01
learn_rate = 0.25
norm_eps = 1e-05

f32 = jnp.float32
bf16 = jnp.bfloat16
i32 = jnp.int32
LAST = (((1,), (1,)), ((), ()))
ALL = ("dp", "head")
VM = pl.BlockSpec(memory_space=pltpu.VMEM)
SM = pl.BlockSpec(memory_space=pltpu.SMEM)
ANY = pl.BlockSpec(memory_space=pl.ANY)


def iota(shape, axis):
    return lax.broadcasted_iota(i32, shape, axis)


def mm(a, b):
    return jnp.dot(a, b, preferred_element_type=f32)


def mm_last(a, b):
    return lax.dot_general(a, b, LAST, preferred_element_type=f32)


def call(kernel, outs, in_specs, out_specs, scratch=(), vmem=32, flops=0, moved=0, exps=0):
    return pl.pallas_call(
        kernel,
        out_shape=outs,
        in_specs=in_specs,
        out_specs=out_specs,
        scratch_shapes=list(scratch),
        compiler_params=pltpu.CompilerParams(vmem_limit_bytes=vmem * MIB),
        cost_estimate=pl.CostEstimate(flops=flops, bytes_accessed=moved, transcendentals=exps),
    )


def request_kernel(owners, peers, owned, sc_ref, len_ref, ids_ref, req_ref, slot_ref):
    me = sc_ref[0]
    base = (sc_ref[1] * CAP).astype(f32)
    count = len_ref[me]
    ids = ids_ref[...].astype(f32)
    examples, slots = ids.shape
    row = jnp.sum(jnp.where(iota(ids.shape, 0) == me, ids, 0.0), 0, keepdims=True)
    flipped = ids.T
    col = jnp.sum(jnp.where(iota(flipped.shape, 1) == me, flipped, 0.0), 1, keepdims=True)
    t_col = iota((slots, slots), 0)
    t_row = iota((slots, slots), 1)
    valid_col = (iota((slots, 1), 0) < count).astype(f32)
    valid_row = (iota((1, slots), 1) < count).astype(f32)
    own_col = sum((col >= k * owned).astype(f32) for k in range(1, owners))
    own_row = sum((row >= k * owned).astype(f32) for k in range(1, owners))
    same = (col == row) & (t_row < count) & (t_col < count)
    before = t_row < t_col
    after = t_col < t_row
    seen_col = jnp.sum(jnp.where(same & before, 1.0, 0.0), 1, keepdims=True)
    seen_row = jnp.sum(jnp.where(same & after, 1.0, 0.0), 0, keepdims=True)
    first_col = jnp.where(seen_col == 0.0, valid_col, 0.0)
    first_row = jnp.where(seen_row == 0.0, valid_row, 0.0)
    shared = own_col == own_row
    place_col = jnp.sum(jnp.where(shared & before, first_row, 0.0), 1, keepdims=True)
    place_row = jnp.sum(jnp.where(shared & after, first_col, 0.0), 0, keepdims=True)
    rank = jnp.sum(jnp.where(same, first_row * place_row, 0.0), 1, keepdims=True)
    local = rank - base
    here = (local >= 0.0) & (local < CAP) & (valid_col > 0.0)
    slot = jnp.where(here, own_col * CAP + local, -1.0)
    slot_ref[...] = jnp.broadcast_to(slot, slot_ref.shape).astype(i32)
    rounds = jnp.floor(jnp.max(rank, 0, keepdims=True) * (1.0 / CAP) + 0.5 / CAP) + 1.0
    lane = iota((slots, LANES), 1)
    lane_f = lane.astype(f32)
    wanted = jnp.where(first_col > 0.0, place_col - base, -1.0)
    hit = (wanted == lane_f) & (lane < CAP)
    lane_row = iota((1, LANES), 1)
    for owner in range(owners):
        chosen = jnp.where(hit & (own_col == float(owner)), col - float(owner * owned), 0.0)
        line = jnp.sum(chosen, 0, keepdims=True)
        line = jnp.where(lane_row == LANES - 1, rounds, line).astype(i32)
        for peer in range(peers):
            req_ref[owner * peers + peer] = line


def lookup_kernel(want_ref, table_ref, out_ref, wide_ref, stage_ref):
    wide_ref[...] = table_ref[...].astype(f32)

    def one(src, carry):
        for p in range(CAP):
            stage_ref[p : p + 1, :] = wide_ref[pl.ds(want_ref[src, 0, p], 1), :]
        out_ref[src] = stage_ref[...].astype(bf16)
        return carry

    lax.fori_loop(0, want_ref.shape[0], one, 0)


def assemble_kernel(owners, peers, got_ref, slot_ref, emb_ref, rows_ref):
    for owner in range(owners):
        for peer in range(peers):
            rows_ref[owner * CAP : (owner + 1) * CAP, peer * LANES : (peer + 1) * LANES] = got_ref[
                owner * peers + peer
            ]
    slot = slot_ref[...]
    lane = iota(slot.shape, 1)
    picks = [
        (slot == lane + first).astype(f32).astype(bf16)
        for first in range(0, owners * CAP, LANES)
    ]
    emb_ref[...] = mm(jnp.concatenate(picks, 1), rows_ref[...]).astype(bf16)


def normalize(inputs):
    centre = inputs - jnp.mean(inputs, -1, keepdims=True)
    inv_std = lax.rsqrt(jnp.mean(centre * centre, -1, keepdims=True) + norm_eps)
    return centre * inv_std, inv_std


def norm_back(scaled, x_hat, inv_std):
    return inv_std * (
        scaled
        - jnp.mean(scaled, -1, keepdims=True)
        - x_hat * jnp.mean(scaled * x_hat, -1, keepdims=True)
    )


def halves(pair):
    low = iota(pair.shape, 1) < HDIM
    zero = jnp.zeros_like(pair)
    return jnp.where(low, pair, zero), jnp.where(low, zero, pair)


def flip(x):
    return x.astype(f32).T


def attend_kernel(
    shards, len_ref, emb_ref, pos_ref, gain_ref, bias_ref, down_ref, w_ref,
    x_ref, xb_ref, xa_ref, q_ref, k_ref, v_ref, lse_ref, ctx_ref,
    w_buf, up_buf, sems,
):
    slots, width = emb_ref.shape
    rank2 = down_ref.shape[1]
    rank = rank2 // 2
    stride = 3 * width + rank2
    copies = []
    for pair in range(shards // 2):
        mine = []
        for side in range(2):
            base = (2 * pair + side) * stride
            for part in range(3):
                mine.append(
                    pltpu.make_async_copy(
                        w_ref.at[pl.ds(base + part * width, width), :],
                        w_buf.at[pair, :, pl.ds((part * 2 + side) * LANES, LANES)],
                        sems.at[pair, side * 4 + part],
                    )
                )
            mine.append(
                pltpu.make_async_copy(
                    w_ref.at[pl.ds(base + 3 * width, rank2), :],
                    up_buf.at[pair, :, pl.ds(side * LANES, LANES)],
                    sems.at[pair, side * 4 + 3],
                )
            )
        copies.append(mine)
    for mine in copies:
        for one in mine:
            one.start()
    count = len_ref[0]
    x_hat, unused_std = normalize(emb_ref[...].astype(f32) + pos_ref[...].astype(f32))
    x0 = x_hat * gain_ref[0:1, :] + bias_ref[0:1, :]
    x_ref[...] = x0
    xb_ref[...] = x0.astype(bf16)
    xa = mm(xb_ref[...], down_ref[...]).astype(bf16)
    xa_ref[...] = xa
    low = iota(xa.shape, 1) < rank
    zero = jnp.zeros_like(xa)
    twice = xa * jnp.asarray(adapter_scale, bf16)
    twice_q = jnp.where(low, twice, zero)
    twice_v = jnp.where(low, zero, twice)
    for pair in range(shards // 2):
        for one in copies[pair]:
            one.wait()
        total = mm(xb_ref[...], w_buf[pair])
        two = 2 * LANES
        q2 = ((total[:, :two] + mm(twice_q, up_buf[pair])) * (HDIM**-0.5)).astype(bf16)
        k2 = total[:, two : 2 * two].astype(bf16)
        v2 = (total[:, 2 * two :] + mm(twice_v, up_buf[pair])).astype(bf16)
        for side in range(2):
            cut = slice(side * LANES, (side + 1) * LANES)
            q_ref[2 * pair + side] = q2[:, cut]
            k_ref[2 * pair + side] = k2[:, cut]
            v_ref[2 * pair + side] = v2[:, cut]
    block = slots // 2
    keep = iota((slots, block), 0) < count

    def one_pair(j, carry):
        k_sides = halves(k_ref[j])
        v_flip = flip(v_ref[j]).astype(bf16)
        for first in range(0, slots, block):
            q = q_ref[j, first : first + block, :]
            parts = []
            for side in range(2):
                s = jnp.where(keep, mm_last(k_sides[side], q), -1e30)
                top = jnp.max(s, 0, keepdims=True)
                e = jnp.exp(s - top)
                total = jnp.sum(e, 0, keepdims=True)
                prob = (e * (1.0 / total)).astype(bf16)
                lse_ref[j, side : side + 1, first : first + block] = top + jnp.log(total)
                parts.append(mm(v_flip[side * HDIM : (side + 1) * HDIM, :], prob))
            both = jnp.concatenate(parts, 0).T
            ctx_ref[first : first + block, pl.ds(pl.multiple_of(j * LANES, LANES), LANES)] = (
                both.astype(bf16)
            )
        return carry

    lax.fori_loop(0, shards, one_pair, 0)


def gelu_parts(x):
    z = jnp.abs(x) * (0.5**0.5)
    t = 1.0 / (1.0 + 0.3275911 * z)
    poly = t * (
        0.254829592
        + t * (-0.284496736 + t * (1.421413741 + t * (-1.453152027 + t * 1.061405429)))
    )
    bell = jnp.exp(-0.5 * x * x)
    tail = 0.5 * poly * bell
    cdf = jnp.where(x < 0.0, tail, 1.0 - tail)
    return x * cdf, cdf + x * bell * 0.3989422804014327


def middle_kernel(
    shards, len_ref, label_ref, x_ref, ctx_ref, gain_ref, bias_ref, class_ref, wo_ref, wi_ref, wf_ref,
    dctx_ref, loss_ref,
    wo_buf, wi_buf, wf_buf, slope_buf, acc_ref, h_ref, hb_ref, hat_ref, df_ref, wo_sem, wi_sem, wf_sem,
):
    slots, width = x_ref.shape
    classes = class_ref.shape[0]
    unit = wf_buf.shape[1]
    wo_copy = pltpu.make_async_copy(wo_ref, wo_buf, wo_sem.at[0])
    wo_copy.start()
    wi_copies = []
    wf_copies = []
    for f in range(shards):
        wi_copies.append(
            pltpu.make_async_copy(wi_ref.at[pl.ds(f * width, width), :], wi_buf.at[f], wi_sem.at[f])
        )
        wf_copies.append(
            pltpu.make_async_copy(wf_ref.at[pl.ds(f * unit, unit), :], wf_buf.at[f], wf_sem.at[f])
        )
        wi_copies[-1].start()
        wf_copies[-1].start()
    count = len_ref[0]
    count_f = count.astype(f32)
    label = label_ref[0]
    wo_copy.wait()
    hat1, std1 = normalize(x_ref[...] + mm(ctx_ref[...], wo_buf[...]))
    hat_ref[...] = hat1
    h1 = hat1 * gain_ref[1:2, :] + bias_ref[1:2, :]
    h_ref[...] = h1
    hb_ref[...] = h1.astype(bf16)
    for f in range(shards):
        wi_copies[f].wait()
        g, slope = gelu_parts(mm(hb_ref[...], wi_buf[f]))
        slope_buf[f] = slope
        wf_copies[f].wait()
        part = mm(g.astype(bf16), wf_buf[f])
        if f == 0:
            acc_ref[...] = part
        else:
            acc_ref[...] += part
    hat2, std2 = normalize(h_ref[...] + acc_ref[...])
    gain2 = gain_ref[2:3, :]
    valid = (iota((slots, 1), 0) < count).astype(f32)
    pooled = jnp.sum((hat2 * gain2 + bias_ref[2:3, :]) * valid, 0, keepdims=True) / count_f
    weights = class_ref[...].astype(f32)
    logits = jnp.sum(pooled.astype(bf16).astype(f32) * weights, 1, keepdims=True)
    shifted = logits - jnp.max(logits, 0, keepdims=True)
    log_prob = shifted - jnp.log(jnp.sum(jnp.exp(shifted), 0, keepdims=True))
    target = (1.0 - smooth_rate) * (iota((classes, 1), 0) == label).astype(f32) + smooth_rate / classes
    loss_ref[...] = jnp.broadcast_to(-jnp.sum(target * log_prob, 0, keepdims=True), loss_ref.shape)
    d_pooled = jnp.sum((jnp.exp(log_prob) - target) * weights, 0, keepdims=True) / count_f
    d_two = norm_back((d_pooled * gain2) * valid, hat2, std2)
    acc_ref[...] = d_two
    df_ref[...] = d_two.astype(bf16)
    for f in range(shards):
        d_pre = (mm_last(df_ref[...], wf_buf[f]) * slope_buf[f]).astype(bf16)
        acc_ref[...] += mm_last(d_pre, wi_buf[f])
    d_attn = norm_back(acc_ref[...] * gain_ref[1:2, :], hat_ref[...], std1).astype(bf16)
    dctx_ref[...] = mm_last(d_attn, wo_buf[...]).astype(bf16)


def gradient_kernel(
    shards, groups, len_ref, xb_ref, xa_ref, q_ref, k_ref, v_ref, lse_ref, dctx_ref, w_ref,
    send_ref, norm_ref,
    up_buf, up_grad, inner_ref, sems,
):
    slots, width = xb_ref.shape
    rank2 = xa_ref.shape[1]
    rank = rank2 // 2
    stride = 3 * width + rank2
    copies = [
        pltpu.make_async_copy(
            w_ref.at[pl.ds(j * stride + 3 * width, rank2), :], up_buf.at[j], sems.at[j]
        )
        for j in range(shards)
    ]
    for one in copies:
        one.start()
    for one in copies:
        one.wait()
    count = len_ref[0]
    block = slots // 2
    keep = iota((slots, block), 0) < count
    xa = xa_ref[...]
    low = iota((LANES, rank2), 1) < rank
    inner_ref[...] = jnp.zeros_like(inner_ref)

    def one_pair(j, carry):
        k = k_ref[j]
        k_sides = halves(k)
        v_sides = halves(v_ref[j])
        k_flip = flip(k).astype(bf16)
        dv = jnp.zeros((slots, LANES), f32)
        flips = []
        for first in range(0, slots, block):
            q = q_ref[j, first : first + block, :]
            dctx = dctx_ref[first : first + block, pl.ds(pl.multiple_of(j * LANES, LANES), LANES)]
            dctx_sides = halves(dctx)
            parts = []
            for side in range(2):
                s = jnp.where(keep, mm_last(k_sides[side], q), -1e30)
                prob = jnp.exp(s - lse_ref[j, side : side + 1, first : first + block])
                d_prob = mm_last(v_sides[side], dctx)
                weighted = jnp.sum(prob * d_prob, 0, keepdims=True)
                d_s = (prob * (d_prob - weighted)).astype(bf16)
                dv = dv + mm(prob.astype(bf16), dctx_sides[side])
                parts.append(mm(k_flip[side * HDIM : (side + 1) * HDIM, :], d_s))
            flips.append(jnp.concatenate(parts, 0))
        dq_flip = (jnp.concatenate(flips, 1) * (HDIM**-0.5)).astype(bf16)
        dv_flip = flip(dv.astype(bf16)).astype(bf16)
        up_grad[pl.ds(pl.multiple_of(j * LANES, LANES), LANES), :] = adapter_scale * jnp.where(
            low, mm(dq_flip, xa), mm(dv_flip, xa)
        )
        inner_ref[0:rank, :] += adapter_scale * mm(up_buf[j, 0:rank, :], dq_flip)
        inner_ref[rank:rank2, :] += adapter_scale * mm(up_buf[j, rank:rank2, :], dv_flip)
        return carry

    lax.fori_loop(0, shards, one_pair, 0)
    down_grad = mm(inner_ref[...].astype(bf16), xb_ref[...]).T
    both = jnp.concatenate([up_grad[...], down_grad], 1)
    squares = jnp.sum(jnp.sum(both * both, 1, keepdims=True), 0, keepdims=True)
    norm = jnp.sqrt(squares)
    norm_ref[...] = jnp.broadcast_to(norm, norm_ref.shape)
    both = both * (clip_bound / jnp.maximum(norm, clip_bound))
    rows = width // (groups * shards)
    for i in range(groups):
        for j in range(shards):
            to = i * shards + j
            at_up = (j * groups + i) * rows
            at_down = to * rows
            send_ref[to, :, 0:rank2] = both[at_up : at_up + rows, 0:rank2]
            send_ref[to, :, rank2:] = both[at_down : at_down + rows, rank2:]


def lamb(weight, grad, first, second, fix_one, fix_two):
    first_new = beta_one * first + (1.0 - beta_one) * grad
    second_new = beta_two * second + (1.0 - beta_two) * grad * grad
    direction = first_new / fix_one / (jnp.sqrt(second_new / fix_two) + adam_eps) + decay_rate * weight
    return first_new, second_new, direction


def side_by_side(ref, at, rows):
    return jnp.concatenate([ref[0, pl.ds(at, rows), :], ref[1, pl.ds(at, rows), :]], 1)


def flip_up(ref):
    maps, rank, cols = ref.shape
    return ref[...].reshape(maps * rank, cols).T


def direction_kernel(
    examples, sc_ref, fix_ref, got_ref, loss_ref, down_ref, up_ref, dm1_ref, dm2_ref, um1_ref, um2_ref,
    dn_ref, un_ref,
    tile_ref, um1_out, um2_out, dir_ref, w_out, turned,
):
    dp_at, head_at = sc_ref[0], sc_ref[1]
    rows = got_ref.shape[1]
    rank2 = got_ref.shape[2] // 2
    at = pl.multiple_of(head_at * rows, rows)
    whole_at = pl.multiple_of(dp_at * dm1_ref.shape[1] + head_at * rows, rows)
    turned[...] = flip_up(up_ref)
    up_at = pl.multiple_of(dp_at * rows, rows)
    weight = jnp.concatenate([turned[pl.ds(up_at, rows), :], side_by_side(down_ref, whole_at, rows)], 1)
    noise = jnp.concatenate([flip_up(un_ref), side_by_side(dn_ref, at, rows)], 1)
    first = jnp.concatenate([flip_up(um1_ref), side_by_side(dm1_ref, at, rows)], 1)
    second = jnp.concatenate([flip_up(um2_ref), side_by_side(dm2_ref, at, rows)], 1)
    total = jnp.sum(got_ref[...], 0)
    grad = (total + noise_mult * clip_bound * noise) / examples
    first_new, second_new, direction = lamb(weight, grad, first, second, fix_ref[0], fix_ref[1])
    um1_out[...] = first_new
    um2_out[...] = second_new
    dir_ref[...] = direction
    w_out[...] = weight
    line = iota((rows, 2 * rank2), 0)
    stats = jnp.where(
        line == 0,
        jnp.sum(direction * direction, 0, keepdims=True),
        jnp.where(
            line == 1,
            jnp.sum(weight * weight, 0, keepdims=True),
            jnp.where(line == 2, loss_ref[0:1, 0 : 2 * rank2], 0.0),
        ),
    )
    tile = jnp.concatenate([grad, stats], 1)
    for to in range(tile_ref.shape[0]):
        tile_ref[to] = tile


def update_kernel(
    examples, shards, sc_ref, fix_ref, got_ref, down_ref, dm1_ref, dm2_ref, um1_ref, um2_ref, dir_ref, w_ref,
    loss_ref, dm1_out, dm2_out, dw_out, um1_out, um2_out, uw_out, table_ref,
):
    dp_at = sc_ref[0]
    rows = got_ref.shape[1]
    rank2 = w_ref.shape[1] // 2
    rank = rank2 // 2
    total = jnp.sum(got_ref[...], 0)
    stats = total[:, 2 * rank2 :]
    loss_ref[...] = stats[2:3, 0:1] / examples
    lane = iota((1, 2 * rank2), 1)

    def part(line, group):
        inside = (lane >= group * rank) & (lane < (group + 1) * rank)
        return jnp.sqrt(jnp.sum(jnp.where(inside, stats[line : line + 1, :], 0.0), 1, keepdims=True))

    norms = [(part(1, group), part(0, group)) for group in range(4)]
    for out_row, group in enumerate((2, 3, 0, 1)):
        table_ref[out_row : out_row + 1, :] = jnp.concatenate(norms[group], 1)

    def rate(a, b):
        wide = iota((1, rank2), 1) < rank
        return learn_rate * jnp.where(
            wide, norms[a][0] / norms[a][1], norms[b][0] / norms[b][1]
        )

    up_new = w_ref[:, :rank2] - rate(0, 1) * dir_ref[:, :rank2]

    def put_up(ref, value):
        ref[...] = value.T.reshape(ref.shape)

    put_up(uw_out, up_new)
    put_up(um1_out, um1_ref[:, :rank2])
    put_up(um2_out, um2_ref[:, :rank2])
    grad = jnp.concatenate(
        [got_ref[dp_at * shards + j, :, rank2 : 2 * rank2] for j in range(shards)], 0
    )
    many = dm1_ref.shape[1]
    at = pl.multiple_of(dp_at * many, many)
    weight = side_by_side(down_ref, at, many)
    first = side_by_side(dm1_ref, 0, many)
    second = side_by_side(dm2_ref, 0, many)
    first_new, second_new, direction = lamb(weight, grad, first, second, fix_ref[0], fix_ref[1])
    new = weight - rate(2, 3) * direction
    for ref, value in ((dm1_out, first_new), (dm2_out, second_new), (dw_out, new)):
        ref[0] = value[:, :rank]
        ref[1] = value[:, rank:]


def per_device(
    slot_token_ids,
    lengths,
    labels,
    optimizer_step_count,
    token_embedding_table,
    positions,
    query_key_value_weight,
    attention_output_weight,
    feedforward_input_weight,
    feedforward_output_weight,
    layer_norm_gains,
    layer_norm_biases,
    classifier,
    adapter_down_maps,
    adapter_up_maps,
    down_first_moment,
    down_second_moment,
    up_first_moment,
    up_second_moment,
    down_privacy_noise,
    up_privacy_noise,
):
    shards = lax.axis_size("head")
    groups = lax.axis_size("dp")
    devices = shards * groups
    dp_at = lax.axis_index("dp")
    head_at = lax.axis_index("head")
    slots, width = positions.shape
    rank = adapter_down_maps.shape[2]
    rank2 = 2 * rank
    units = feedforward_output_weight.shape[0]
    local_w = attention_output_weight.shape[0]
    owned = token_embedding_table.shape[0]
    shape = jax.ShapeDtypeStruct

    packed = jnp.concatenate(
        [
            query_key_value_weight.reshape(3 * width, local_w),
            adapter_up_maps.astype(bf16).reshape(rank2, local_w),
        ],
        0,
    )
    w_all = lax.all_gather(packed, "head", axis=0, tiled=True)
    wo_all = lax.all_gather(attention_output_weight, "head", axis=0, tiled=True)
    wi_all = lax.all_gather(feedforward_input_weight, "head", axis=0, tiled=True)
    wf_all = lax.all_gather(feedforward_output_weight, "head", axis=0, tiled=True)

    def fetch(which):
        requests, slot = call(
            functools.partial(request_kernel, groups, shards, owned),
            (shape((devices, 1, LANES), i32), shape((slots, LANES), i32)),
            [SM, SM, VM],
            (VM, VM),
            flops=40 * slots * slots,
            moved=slots * 1024,
        )(jnp.stack([head_at, which]).astype(i32), lengths, slot_token_ids)
        wanted = lax.all_to_all(requests, ALL, 0, 0, tiled=True)
        found = call(
            lookup_kernel,
            shape((devices, CAP, LANES), bf16),
            [SM, VM],
            VM,
            [pltpu.VMEM((owned, LANES), f32), pltpu.VMEM((CAP, LANES), f32)],
            flops=devices * CAP * LANES,
            moved=devices * CAP * LANES * 4,
        )(wanted, token_embedding_table)
        got = lax.all_to_all(found, ALL, 0, 0, tiled=True)
        emb = call(
            functools.partial(assemble_kernel, groups, shards),
            shape((slots, width), bf16),
            [VM, VM],
            VM,
            [pltpu.VMEM((groups * CAP, width), bf16)],
            flops=2 * slots * groups * CAP * width,
            moved=4 * slots * width,
        )(got, slot)
        return emb, jnp.max(wanted[:, 0, LANES - 1])

    emb, rounds = fetch(jnp.zeros((), i32))
    unused_at, emb = lax.while_loop(
        lambda state: state[0] < rounds,
        lambda state: (state[0] + 1, state[1] + fetch(state[0])[0]),
        (jnp.ones((), i32), emb),
    )

    down_pair = jnp.concatenate([adapter_down_maps[0], adapter_down_maps[1]], 1).astype(bf16)
    own_len = lax.dynamic_slice_in_dim(lengths, head_at, 1)
    own_label = lax.dynamic_slice_in_dim(labels, head_at, 1)
    quarter = 2 * slots * slots * width
    x0, x0b, xa, q, k, v, lse, ctx = call(
        functools.partial(attend_kernel, shards),
        (
            shape((slots, width), f32),
            shape((slots, width), bf16),
            shape((slots, rank2), bf16),
            shape((shards, slots, LANES), bf16),
            shape((shards, slots, LANES), bf16),
            shape((shards, slots, LANES), bf16),
            shape((shards, 2, slots), f32),
            shape((slots, width), bf16),
        ),
        [SM, VM, VM, VM, VM, VM, ANY],
        (VM,) * 8,
        [
            pltpu.VMEM((shards // 2, width, 6 * LANES), bf16),
            pltpu.VMEM((shards // 2, rank2, 2 * LANES), bf16),
            pltpu.SemaphoreType.DMA((shards // 2, 8)),
        ],
        vmem=50,
        flops=6 * slots * width * width + 2 * quarter,
        moved=12 * MIB,
        exps=16 * slots * slots,
    )(own_len, emb, positions, layer_norm_gains, layer_norm_biases, down_pair, w_all)

    dctx, loss = call(
        functools.partial(middle_kernel, shards),
        (shape((slots, width), bf16), shape((1, LANES), f32)),
        [SM, SM, VM, VM, VM, VM, VM, ANY, ANY, ANY],
        (VM, VM),
        [
            pltpu.VMEM((width, width), bf16),
            pltpu.VMEM((shards, width, units), bf16),
            pltpu.VMEM((shards, units, width), bf16),
            pltpu.VMEM((shards, slots, units), f32),
            pltpu.VMEM((slots, width), f32),
            pltpu.VMEM((slots, width), f32),
            pltpu.VMEM((slots, width), bf16),
            pltpu.VMEM((slots, width), f32),
            pltpu.VMEM((slots, width), bf16),
            pltpu.SemaphoreType.DMA((1,)),
            pltpu.SemaphoreType.DMA((shards,)),
            pltpu.SemaphoreType.DMA((shards,)),
        ],
        vmem=60,
        flops=8 * slots * width * units * shards + 4 * slots * width * width,
        moved=24 * MIB,
        exps=2 * slots * units * shards,
    )(
        own_len, own_label, x0, ctx, layer_norm_gains, layer_norm_biases, classifier, wo_all, wi_all, wf_all
    )

    send, norm = call(
        functools.partial(gradient_kernel, shards, groups),
        (shape((devices, width // devices, 2 * rank2), f32), shape((1, LANES), f32)),
        [SM, VM, VM, VM, VM, VM, VM, VM, ANY],
        (VM, VM),
        [
            pltpu.VMEM((shards, rank2, LANES), bf16),
            pltpu.VMEM((width, rank2), f32),
            pltpu.VMEM((rank2, slots), f32),
            pltpu.SemaphoreType.DMA((shards,)),
        ],
        vmem=50,
        flops=4 * quarter,
        moved=8 * MIB,
        exps=16 * slots * slots,
    )(own_len, x0b, xa, q, k, v, lse, dctx, w_all)

    got = lax.all_to_all(send, ALL, 0, 0, tiled=True)
    examples = float(devices)
    step_number = optimizer_step_count.astype(f32)
    fixes = jnp.stack([1.0 - jnp.power(beta_one, step_number), 1.0 - jnp.power(beta_two, step_number)])
    where = jnp.stack([dp_at, head_at]).astype(i32)
    rows = width // devices
    small = shape((rows, 2 * rank2), f32)
    tile, um1, um2, direction, weight = call(
        functools.partial(direction_kernel, examples),
        (shape((devices, rows, LANES), f32), small, small, small, small),
        [SM, SM] + [VM] * 10,
        (VM,) * 5,
        [pltpu.VMEM((local_w, rank2), f32)],
    )(
        where, fixes, got, loss, adapter_down_maps, adapter_up_maps, down_first_moment, down_second_moment,
        up_first_moment, up_second_moment, down_privacy_noise, up_privacy_noise,
    )
    spread = lax.all_to_all(tile, ALL, 0, 0, tiled=True)
    down_shape = shape(down_first_moment.shape, f32)
    up_shape = shape(up_first_moment.shape, f32)
    loss_mean, dm1, dm2, dw, bm1, bm2, bw, table = call(
        functools.partial(update_kernel, examples, shards),
        (
            shape((1, 1), f32), down_shape, down_shape, down_shape, up_shape, up_shape, up_shape,
            shape((4, 2), f32),
        ),
        [SM, SM] + [VM] * 8,
        (VM,) * 8,
    )(
        where, fixes, spread, adapter_down_maps, down_first_moment, down_second_moment, um1, um2, direction,
        weight,
    )
    return (
        loss_mean.reshape(()),
        norm[0, 0:1],
        dm1,
        dm2,
        dw,
        bm1,
        bm2,
        bw,
        table,
    )


def solution(mesh):
    placed = (
        P("dp", None),
        P("dp"),
        P("dp"),
        P(),
        P("dp", "head"),
        P(),
        P(None, None, "head"),
        P("head", None),
        P(None, "head"),
        P("head", None),
        P(),
        P(),
        P(),
        P(),
        P(None, None, "head"),
        P(None, "dp", None),
        P(None, "dp", None),
        P(None, None, ("head", "dp")),
        P(None, None, ("head", "dp")),
        P(None, "dp", None),
        P(None, None, ("head", "dp")),
    )
    return jax.shard_map(
        per_device,
        mesh=mesh,
        in_specs=placed,
        out_specs=(
            P(),
            P(("dp", "head")),
            P(None, "dp", None),
            P(None, "dp", None),
            P(None, "dp", None),
            P(None, None, ("head", "dp")),
            P(None, None, ("head", "dp")),
            P(None, None, ("head", "dp")),
            P(),
        ),
        check_vma=False,
    )
```

```python
import functools

import jax
import jax.numpy as jnp
from jax import lax
from jax.experimental import pallas as pl
from jax.experimental.pallas import tpu as pltpu
from jax.sharding import PartitionSpec as P

HDIM = 64
CAP = 48
QUARTERS = 4
LANES = 128
MIB = 1 << 20

adapter_scale = 2.0
clip_bound = 1.0
noise_mult = 0.6
smooth_rate = 0.1
beta_one = 0.9
beta_two = 0.999
adam_eps = 1e-06
decay_rate = 0.01
learn_rate = 0.25
norm_eps = 1e-05

f32 = jnp.float32
bf16 = jnp.bfloat16
i32 = jnp.int32
LAST = (((1,), (1,)), ((), ()))
ALL = ("dp", "head")
VM = pl.BlockSpec(memory_space=pltpu.VMEM)
SM = pl.BlockSpec(memory_space=pltpu.SMEM)
ANY = pl.BlockSpec(memory_space=pl.ANY)


def iota(shape, axis):
    return lax.broadcasted_iota(i32, shape, axis)


def mm(a, b):
    return jnp.dot(a, b, preferred_element_type=f32)


def mm_last(a, b):
    return lax.dot_general(a, b, LAST, preferred_element_type=f32)


def call(kernel, outs, in_specs, out_specs, scratch=(), vmem=32, flops=0, moved=0, exps=0):
    return pl.pallas_call(
        kernel,
        out_shape=outs,
        in_specs=in_specs,
        out_specs=out_specs,
        scratch_shapes=list(scratch),
        compiler_params=pltpu.CompilerParams(vmem_limit_bytes=vmem * MIB),
        cost_estimate=pl.CostEstimate(flops=flops, bytes_accessed=moved, transcendentals=exps),
    )


def request_kernel(owners, peers, owned, sc_ref, len_ref, ids_ref, req_ref, slot_ref):
    me = sc_ref[0]
    base = (sc_ref[1] * CAP).astype(f32)
    count = len_ref[me]
    ids = ids_ref[...].astype(f32)
    examples, slots = ids.shape
    row = jnp.sum(jnp.where(iota(ids.shape, 0) == me, ids, 0.0), 0, keepdims=True)
    flipped = ids.T
    col = jnp.sum(jnp.where(iota(flipped.shape, 1) == me, flipped, 0.0), 1, keepdims=True)
    t_col = iota((slots, slots), 0)
    t_row = iota((slots, slots), 1)
    valid_col = (iota((slots, 1), 0) < count).astype(f32)
    valid_row = (iota((1, slots), 1) < count).astype(f32)
    own_col = sum((col >= k * owned).astype(f32) for k in range(1, owners))
    own_row = sum((row >= k * owned).astype(f32) for k in range(1, owners))
    same = (col == row) & (t_row < count) & (t_col < count)
    before = t_row < t_col
    after = t_col < t_row
    seen_col = jnp.sum(jnp.where(same & before, 1.0, 0.0), 1, keepdims=True)
    seen_row = jnp.sum(jnp.where(same & after, 1.0, 0.0), 0, keepdims=True)
    first_col = jnp.where(seen_col == 0.0, valid_col, 0.0)
    first_row = jnp.where(seen_row == 0.0, valid_row, 0.0)
    shared = own_col == own_row
    place_col = jnp.sum(jnp.where(shared & before, first_row, 0.0), 1, keepdims=True)
    place_row = jnp.sum(jnp.where(shared & after, first_col, 0.0), 0, keepdims=True)
    rank = jnp.sum(jnp.where(same, first_row * place_row, 0.0), 1, keepdims=True)
    local = rank - base
    here = (local >= 0.0) & (local < CAP) & (valid_col > 0.0)
    slot = jnp.where(here, own_col * CAP + local, -1.0)
    slot_ref[...] = jnp.broadcast_to(slot, slot_ref.shape).astype(i32)
    rounds = jnp.floor(jnp.max(rank, 0, keepdims=True) * (1.0 / CAP) + 0.5 / CAP) + 1.0
    lane = iota((slots, LANES), 1)
    lane_f = lane.astype(f32)
    wanted = jnp.where(first_col > 0.0, place_col - base, -1.0)
    hit = (wanted == lane_f) & (lane < CAP)
    lane_row = iota((1, LANES), 1)
    for owner in range(owners):
        chosen = jnp.where(hit & (own_col == float(owner)), col - float(owner * owned), 0.0)
        line = jnp.sum(chosen, 0, keepdims=True)
        line = jnp.where(lane_row == LANES - 1, rounds, line).astype(i32)
        for peer in range(peers):
            req_ref[owner * peers + peer] = line


def lookup_kernel(want_ref, table_ref, out_ref, wide_ref, stage_ref):
    wide_ref[...] = table_ref[...].astype(f32)

    def one(src, carry):
        for p in range(CAP):
            stage_ref[p : p + 1, :] = wide_ref[pl.ds(want_ref[src, 0, p], 1), :]
        out_ref[src] = stage_ref[...].astype(bf16)
        return carry

    lax.fori_loop(0, want_ref.shape[0], one, 0)


def assemble_kernel(owners, peers, got_ref, slot_ref, emb_ref, rows_ref):
    for owner in range(owners):
        for peer in range(peers):
            rows_ref[owner * CAP : (owner + 1) * CAP, peer * LANES : (peer + 1) * LANES] = got_ref[
                owner * peers + peer
            ]
    slot = slot_ref[...]
    lane = iota(slot.shape, 1)
    picks = [
        (slot == lane + first).astype(f32).astype(bf16)
        for first in range(0, owners * CAP, LANES)
    ]
    emb_ref[...] = mm(jnp.concatenate(picks, 1), rows_ref[...]).astype(bf16)


def normalize(inputs):
    centre = inputs - jnp.mean(inputs, -1, keepdims=True)
    inv_std = lax.rsqrt(jnp.mean(centre * centre, -1, keepdims=True) + norm_eps)
    return centre * inv_std, inv_std


def norm_back(scaled, x_hat, inv_std):
    return inv_std * (
        scaled
        - jnp.mean(scaled, -1, keepdims=True)
        - x_hat * jnp.mean(scaled * x_hat, -1, keepdims=True)
    )


def halves(pair):
    low = iota(pair.shape, 1) < HDIM
    zero = jnp.zeros_like(pair)
    return jnp.where(low, pair, zero), jnp.where(low, zero, pair)


def flip(x):
    return x.astype(f32).T


def attend_kernel(
    shards, len_ref, emb_ref, pos_ref, gain_ref, bias_ref, down_ref, w_ref,
    x_ref, xb_ref, xa_ref, q_ref, k_ref, v_ref, lse_ref, ctx_ref,
    w_buf, up_buf, sems,
):
    slots, width = emb_ref.shape
    rank2 = down_ref.shape[1]
    rank = rank2 // 2
    stride = 3 * width + rank2
    copies = []
    for pair in range(shards // 2):
        mine = []
        for side in range(2):
            base = (2 * pair + side) * stride
            for part in range(3):
                mine.append(
                    pltpu.make_async_copy(
                        w_ref.at[pl.ds(base + part * width, width), :],
                        w_buf.at[pair, :, pl.ds((part * 2 + side) * LANES, LANES)],
                        sems.at[pair, side * 4 + part],
                    )
                )
            mine.append(
                pltpu.make_async_copy(
                    w_ref.at[pl.ds(base + 3 * width, rank2), :],
                    up_buf.at[pair, :, pl.ds(side * LANES, LANES)],
                    sems.at[pair, side * 4 + 3],
                )
            )
        copies.append(mine)
    for mine in copies:
        for one in mine:
            one.start()
    count = len_ref[0]
    x_hat, unused_std = normalize(emb_ref[...].astype(f32) + pos_ref[...].astype(f32))
    x0 = x_hat * gain_ref[0:1, :] + bias_ref[0:1, :]
    x_ref[...] = x0
    xb_ref[...] = x0.astype(bf16)
    xa = mm(xb_ref[...], down_ref[...]).astype(bf16)
    xa_ref[...] = xa
    low = iota(xa.shape, 1) < rank
    zero = jnp.zeros_like(xa)
    twice = xa * jnp.asarray(adapter_scale, bf16)
    twice_q = jnp.where(low, twice, zero)
    twice_v = jnp.where(low, zero, twice)
    for pair in range(shards // 2):
        for one in copies[pair]:
            one.wait()
        total = mm(xb_ref[...], w_buf[pair])
        two = 2 * LANES
        q2 = ((total[:, :two] + mm(twice_q, up_buf[pair])) * (HDIM**-0.5)).astype(bf16)
        k2 = total[:, two : 2 * two].astype(bf16)
        v2 = (total[:, 2 * two :] + mm(twice_v, up_buf[pair])).astype(bf16)
        for side in range(2):
            cut = slice(side * LANES, (side + 1) * LANES)
            q_ref[2 * pair + side] = q2[:, cut]
            k_ref[2 * pair + side] = k2[:, cut]
            v_ref[2 * pair + side] = v2[:, cut]
    block = slots // 2
    keep = iota((slots, block), 0) < count

    def one_pair(j, carry):
        k_sides = halves(k_ref[j])
        v_flip = flip(v_ref[j]).astype(bf16)
        for first in range(0, slots, block):
            q = q_ref[j, first : first + block, :]
            parts = []
            for side in range(2):
                s = jnp.where(keep, mm_last(k_sides[side], q), -1e30)
                top = jnp.max(s, 0, keepdims=True)
                e = jnp.exp(s - top)
                total = jnp.sum(e, 0, keepdims=True)
                prob = (e * (1.0 / total)).astype(bf16)
                lse_ref[j, side : side + 1, first : first + block] = top + jnp.log(total)
                parts.append(mm(v_flip[side * HDIM : (side + 1) * HDIM, :], prob))
            both = jnp.concatenate(parts, 0).T
            ctx_ref[first : first + block, pl.ds(pl.multiple_of(j * LANES, LANES), LANES)] = (
                both.astype(bf16)
            )
        return carry

    lax.fori_loop(0, shards, one_pair, 0)


def gelu_parts(x):
    z = jnp.abs(x) * (0.5**0.5)
    t = 1.0 / (1.0 + 0.3275911 * z)
    poly = t * (
        0.254829592
        + t * (-0.284496736 + t * (1.421413741 + t * (-1.453152027 + t * 1.061405429)))
    )
    bell = jnp.exp(-0.5 * x * x)
    tail = 0.5 * poly * bell
    cdf = jnp.where(x < 0.0, tail, 1.0 - tail)
    return x * cdf, cdf + x * bell * 0.3989422804014327


def middle_kernel(
    shards, len_ref, label_ref, turn_ref, x_ref, ctx_ref, gain_ref, bias_ref, class_ref, wo_ref,
    wi_own, wi_up, wi_down, wi_low, wi_high, wf_own, wf_up, wf_down, wf_low, wf_high,
    dctx_ref, loss_ref,
    wo_buf, wi_buf, wf_buf, slope_buf, acc_ref, h_ref, hb_ref, hat_ref, df_ref, wo_sem, wi_sem, wf_sem,
):
    slots, width = x_ref.shape
    classes = class_ref.shape[0]
    wo_copy = pltpu.make_async_copy(wo_ref, wo_buf, wo_sem.at[0])
    wo_copy.start()

    def quarters(f, turn, buf, sem, own, up, down, low, high):
        rows = own.shape[0] // shards
        half = shards // 2
        opposite = low if f < half else high
        found = []
        for step, (ref, at) in enumerate(((own, f), (up, f), (opposite, f % half), (down, f))):
            place = pl.multiple_of(lax.rem(turn + step, QUARTERS) * rows, rows)
            found.append(
                pltpu.make_async_copy(
                    ref.at[pl.ds(at * rows, rows), :], buf.at[f, pl.ds(place, rows), :], sem.at[f, step]
                )
            )
            found[-1].start()
        return found

    wi_copies = []
    wf_copies = []
    for f in range(shards):
        wi_copies.append(quarters(f, turn_ref[0], wi_buf, wi_sem, wi_own, wi_up, wi_down, wi_low, wi_high))
        wf_copies.append(quarters(f, turn_ref[1], wf_buf, wf_sem, wf_own, wf_up, wf_down, wf_low, wf_high))
    count = len_ref[0]
    count_f = count.astype(f32)
    label = label_ref[0]
    wo_copy.wait()
    hat1, std1 = normalize(x_ref[...] + mm(ctx_ref[...], wo_buf[...]))
    hat_ref[...] = hat1
    h1 = hat1 * gain_ref[1:2, :] + bias_ref[1:2, :]
    h_ref[...] = h1
    hb_ref[...] = h1.astype(bf16)
    for f in range(shards):
        for one in wi_copies[f]:
            one.wait()
        g, slope = gelu_parts(mm(hb_ref[...], wi_buf[f]))
        slope_buf[f] = slope
        for one in wf_copies[f]:
            one.wait()
        part = mm(g.astype(bf16), wf_buf[f])
        if f == 0:
            acc_ref[...] = part
        else:
            acc_ref[...] += part
    hat2, std2 = normalize(h_ref[...] + acc_ref[...])
    gain2 = gain_ref[2:3, :]
    valid = (iota((slots, 1), 0) < count).astype(f32)
    pooled = jnp.sum((hat2 * gain2 + bias_ref[2:3, :]) * valid, 0, keepdims=True) / count_f
    weights = class_ref[...].astype(f32)
    logits = jnp.sum(pooled.astype(bf16).astype(f32) * weights, 1, keepdims=True)
    shifted = logits - jnp.max(logits, 0, keepdims=True)
    log_prob = shifted - jnp.log(jnp.sum(jnp.exp(shifted), 0, keepdims=True))
    target = (1.0 - smooth_rate) * (iota((classes, 1), 0) == label).astype(f32) + smooth_rate / classes
    loss_ref[...] = jnp.broadcast_to(-jnp.sum(target * log_prob, 0, keepdims=True), loss_ref.shape)
    d_pooled = jnp.sum((jnp.exp(log_prob) - target) * weights, 0, keepdims=True) / count_f
    d_two = norm_back((d_pooled * gain2) * valid, hat2, std2)
    acc_ref[...] = d_two
    df_ref[...] = d_two.astype(bf16)
    for f in range(shards):
        d_pre = (mm_last(df_ref[...], wf_buf[f]) * slope_buf[f]).astype(bf16)
        acc_ref[...] += mm_last(d_pre, wi_buf[f])
    d_attn = norm_back(acc_ref[...] * gain_ref[1:2, :], hat_ref[...], std1).astype(bf16)
    dctx_ref[...] = mm_last(d_attn, wo_buf[...]).astype(bf16)


def gradient_kernel(
    shards, groups, len_ref, xb_ref, xa_ref, q_ref, k_ref, v_ref, lse_ref, dctx_ref, w_ref,
    send_ref, norm_ref,
    up_buf, up_grad, inner_ref, sems,
):
    slots, width = xb_ref.shape
    rank2 = xa_ref.shape[1]
    rank = rank2 // 2
    stride = 3 * width + rank2
    copies = [
        pltpu.make_async_copy(
            w_ref.at[pl.ds(j * stride + 3 * width, rank2), :], up_buf.at[j], sems.at[j]
        )
        for j in range(shards)
    ]
    for one in copies:
        one.start()
    for one in copies:
        one.wait()
    count = len_ref[0]
    block = slots // 2
    keep = iota((slots, block), 0) < count
    xa = xa_ref[...]
    low = iota((LANES, rank2), 1) < rank
    inner_ref[...] = jnp.zeros_like(inner_ref)

    def one_pair(j, carry):
        k = k_ref[j]
        k_sides = halves(k)
        v_sides = halves(v_ref[j])
        k_flip = flip(k).astype(bf16)
        dv = jnp.zeros((slots, LANES), f32)
        flips = []
        for first in range(0, slots, block):
            q = q_ref[j, first : first + block, :]
            dctx = dctx_ref[first : first + block, pl.ds(pl.multiple_of(j * LANES, LANES), LANES)]
            dctx_sides = halves(dctx)
            parts = []
            for side in range(2):
                s = jnp.where(keep, mm_last(k_sides[side], q), -1e30)
                prob = jnp.exp(s - lse_ref[j, side : side + 1, first : first + block])
                d_prob = mm_last(v_sides[side], dctx)
                weighted = jnp.sum(prob * d_prob, 0, keepdims=True)
                d_s = (prob * (d_prob - weighted)).astype(bf16)
                dv = dv + mm(prob.astype(bf16), dctx_sides[side])
                parts.append(mm(k_flip[side * HDIM : (side + 1) * HDIM, :], d_s))
            flips.append(jnp.concatenate(parts, 0))
        dq_flip = (jnp.concatenate(flips, 1) * (HDIM**-0.5)).astype(bf16)
        dv_flip = flip(dv.astype(bf16)).astype(bf16)
        up_grad[pl.ds(pl.multiple_of(j * LANES, LANES), LANES), :] = adapter_scale * jnp.where(
            low, mm(dq_flip, xa), mm(dv_flip, xa)
        )
        inner_ref[0:rank, :] += adapter_scale * mm(up_buf[j, 0:rank, :], dq_flip)
        inner_ref[rank:rank2, :] += adapter_scale * mm(up_buf[j, rank:rank2, :], dv_flip)
        return carry

    lax.fori_loop(0, shards, one_pair, 0)
    down_grad = mm(inner_ref[...].astype(bf16), xb_ref[...]).T
    both = jnp.concatenate([up_grad[...], down_grad], 1)
    squares = jnp.sum(jnp.sum(both * both, 1, keepdims=True), 0, keepdims=True)
    norm = jnp.sqrt(squares)
    norm_ref[...] = jnp.broadcast_to(norm, norm_ref.shape)
    both = both * (clip_bound / jnp.maximum(norm, clip_bound))
    rows = width // (groups * shards)
    for i in range(groups):
        for j in range(shards):
            to = i * shards + j
            at_up = (j * groups + i) * rows
            at_down = to * rows
            send_ref[to, :, 0:rank2] = both[at_up : at_up + rows, 0:rank2]
            send_ref[to, :, rank2:] = both[at_down : at_down + rows, rank2:]


def lamb(weight, grad, first, second, fix_one, fix_two):
    first_new = beta_one * first + (1.0 - beta_one) * grad
    second_new = beta_two * second + (1.0 - beta_two) * grad * grad
    direction = first_new / fix_one / (jnp.sqrt(second_new / fix_two) + adam_eps) + decay_rate * weight
    return first_new, second_new, direction


def side_by_side(ref, at, rows):
    return jnp.concatenate([ref[0, pl.ds(at, rows), :], ref[1, pl.ds(at, rows), :]], 1)


def flip_up(ref):
    maps, rank, cols = ref.shape
    return ref[...].reshape(maps * rank, cols).T


def direction_kernel(
    examples, sc_ref, fix_ref, got_ref, loss_ref, down_ref, up_ref, dm1_ref, dm2_ref, um1_ref, um2_ref,
    dn_ref, un_ref,
    tile_ref, um1_out, um2_out, dir_ref, w_out, turned,
):
    dp_at, head_at = sc_ref[0], sc_ref[1]
    rows = got_ref.shape[1]
    rank2 = got_ref.shape[2] // 2
    at = pl.multiple_of(head_at * rows, rows)
    whole_at = pl.multiple_of(dp_at * dm1_ref.shape[1] + head_at * rows, rows)
    turned[...] = flip_up(up_ref)
    up_at = pl.multiple_of(dp_at * rows, rows)
    weight = jnp.concatenate([turned[pl.ds(up_at, rows), :], side_by_side(down_ref, whole_at, rows)], 1)
    noise = jnp.concatenate([flip_up(un_ref), side_by_side(dn_ref, at, rows)], 1)
    first = jnp.concatenate([flip_up(um1_ref), side_by_side(dm1_ref, at, rows)], 1)
    second = jnp.concatenate([flip_up(um2_ref), side_by_side(dm2_ref, at, rows)], 1)
    total = jnp.sum(got_ref[...], 0)
    grad = (total + noise_mult * clip_bound * noise) / examples
    first_new, second_new, direction = lamb(weight, grad, first, second, fix_ref[0], fix_ref[1])
    um1_out[...] = first_new
    um2_out[...] = second_new
    dir_ref[...] = direction
    w_out[...] = weight
    line = iota((rows, 2 * rank2), 0)
    stats = jnp.where(
        line == 0,
        jnp.sum(direction * direction, 0, keepdims=True),
        jnp.where(
            line == 1,
            jnp.sum(weight * weight, 0, keepdims=True),
            jnp.where(line == 2, loss_ref[0:1, 0 : 2 * rank2], 0.0),
        ),
    )
    tile = jnp.concatenate([grad, stats], 1)
    for to in range(tile_ref.shape[0]):
        tile_ref[to] = tile


def update_kernel(
    examples, shards, sc_ref, fix_ref, got_ref, down_ref, dm1_ref, dm2_ref, um1_ref, um2_ref, dir_ref, w_ref,
    loss_ref, dm1_out, dm2_out, dw_out, um1_out, um2_out, uw_out, table_ref,
):
    dp_at = sc_ref[0]
    rows = got_ref.shape[1]
    rank2 = w_ref.shape[1] // 2
    rank = rank2 // 2
    total = jnp.sum(got_ref[...], 0)
    stats = total[:, 2 * rank2 :]
    loss_ref[...] = stats[2:3, 0:1] / examples
    lane = iota((1, 2 * rank2), 1)

    def part(line, group):
        inside = (lane >= group * rank) & (lane < (group + 1) * rank)
        return jnp.sqrt(jnp.sum(jnp.where(inside, stats[line : line + 1, :], 0.0), 1, keepdims=True))

    norms = [(part(1, group), part(0, group)) for group in range(4)]
    for out_row, group in enumerate((2, 3, 0, 1)):
        table_ref[out_row : out_row + 1, :] = jnp.concatenate(norms[group], 1)

    def rate(a, b):
        wide = iota((1, rank2), 1) < rank
        return learn_rate * jnp.where(
            wide, norms[a][0] / norms[a][1], norms[b][0] / norms[b][1]
        )

    up_new = w_ref[:, :rank2] - rate(0, 1) * dir_ref[:, :rank2]

    def put_up(ref, value):
        ref[...] = value.T.reshape(ref.shape)

    put_up(uw_out, up_new)
    put_up(um1_out, um1_ref[:, :rank2])
    put_up(um2_out, um2_ref[:, :rank2])
    grad = jnp.concatenate(
        [got_ref[dp_at * shards + j, :, rank2 : 2 * rank2] for j in range(shards)], 0
    )
    many = dm1_ref.shape[1]
    at = pl.multiple_of(dp_at * many, many)
    weight = side_by_side(down_ref, at, many)
    first = side_by_side(dm1_ref, 0, many)
    second = side_by_side(dm2_ref, 0, many)
    first_new, second_new, direction = lamb(weight, grad, first, second, fix_ref[0], fix_ref[1])
    new = weight - rate(2, 3) * direction
    for ref, value in ((dm1_out, first_new), (dm2_out, second_new), (dw_out, new)):
        ref[0] = value[:, :rank]
        ref[1] = value[:, rank:]


def per_device(
    slot_token_ids,
    lengths,
    labels,
    optimizer_step_count,
    token_embedding_table,
    positions,
    query_key_value_weight,
    attention_output_weight,
    feedforward_input_weight,
    feedforward_output_weight,
    layer_norm_gains,
    layer_norm_biases,
    classifier,
    adapter_down_maps,
    adapter_up_maps,
    down_first_moment,
    down_second_moment,
    up_first_moment,
    up_second_moment,
    down_privacy_noise,
    up_privacy_noise,
):
    shards = lax.axis_size("head")
    groups = lax.axis_size("dp")
    devices = shards * groups
    dp_at = lax.axis_index("dp")
    head_at = lax.axis_index("head")
    slots, width = positions.shape
    rank = adapter_down_maps.shape[2]
    rank2 = 2 * rank
    units = feedforward_output_weight.shape[0]
    local_w = attention_output_weight.shape[0]
    owned = token_embedding_table.shape[0]
    shape = jax.ShapeDtypeStruct

    packed = jnp.concatenate(
        [
            query_key_value_weight.reshape(3 * width, local_w),
            adapter_up_maps.astype(bf16).reshape(rank2, local_w),
        ],
        0,
    )
    side = QUARTERS
    y_at, x_at = dp_at // side, dp_at % side
    wi_turn = (x_at + 2 * y_at) % QUARTERS
    wf_turn = (y_at + 2 * x_at) % QUARTERS

    def gathered_quarter(weight, turn):
        rows = weight.shape[0] // QUARTERS
        return lax.all_gather(
            lax.dynamic_slice_in_dim(weight, turn * rows, rows, 0), "head", axis=0, tiled=True
        )

    def neighbour(x, dy, dx):
        pairs = [
            (((y + dy) % side) * side + (c + dx) % side, y * side + c) for y in range(side) for c in range(side)
        ]
        return lax.ppermute(x, "dp", pairs)

    wi_own = gathered_quarter(feedforward_input_weight, wi_turn)
    wf_own = gathered_quarter(feedforward_output_weight, wf_turn)
    w_all = lax.all_gather(packed, "head", axis=0, tiled=True)
    wo_all = lax.all_gather(attention_output_weight, "head", axis=0, tiled=True)
    def spread_quarters(wi_own, wf_own):
        wi_half = wi_own.shape[0] // 2
        wf_half = wf_own.shape[0] // 2
        wi_parts = (
            wi_own,
            neighbour(wi_own, 0, 1),
            neighbour(wi_own, 0, -1),
            neighbour(wi_own[:wi_half], 1, 0),
            neighbour(wi_own[wi_half:], -1, 0),
        )
        wf_parts = (
            wf_own,
            neighbour(wf_own, 1, 0),
            neighbour(wf_own, -1, 0),
            neighbour(wf_own[:wf_half], 0, 1),
            neighbour(wf_own[wf_half:], 0, -1),
        )
        return wi_parts, wf_parts

    def ask(which):
        requests, slot = call(
            functools.partial(request_kernel, groups, shards, owned),
            (shape((devices, 1, LANES), i32), shape((slots, LANES), i32)),
            [SM, SM, VM],
            (VM, VM),
            flops=40 * slots * slots,
            moved=slots * 1024,
        )(jnp.stack([head_at, which]).astype(i32), lengths, slot_token_ids)
        return lax.all_to_all(requests, ALL, 0, 0, tiled=True), slot

    def fetch(wanted, slot):
        found = call(
            lookup_kernel,
            shape((devices, CAP, LANES), bf16),
            [SM, VM],
            VM,
            [pltpu.VMEM((owned, LANES), f32), pltpu.VMEM((CAP, LANES), f32)],
            flops=devices * CAP * LANES,
            moved=devices * CAP * LANES * 4,
        )(wanted, token_embedding_table)
        got = lax.all_to_all(found, ALL, 0, 0, tiled=True)
        emb = call(
            functools.partial(assemble_kernel, groups, shards),
            shape((slots, width), bf16),
            [VM, VM],
            VM,
            [pltpu.VMEM((groups * CAP, width), bf16)],
            flops=2 * slots * groups * CAP * width,
            moved=4 * slots * width,
        )(got, slot)
        return emb

    wanted, slot = ask(jnp.zeros((), i32))
    wanted, wi_own, wf_own = lax.optimization_barrier((wanted, wi_own, wf_own))
    wi_parts, wf_parts = spread_quarters(wi_own, wf_own)
    rounds = jnp.max(wanted[:, 0, LANES - 1])
    emb = fetch(wanted, slot)
    unused_at, emb = lax.while_loop(
        lambda state: state[0] < rounds,
        lambda state: (state[0] + 1, state[1] + fetch(*ask(state[0]))),
        (jnp.ones((), i32), emb),
    )

    down_pair = jnp.concatenate([adapter_down_maps[0], adapter_down_maps[1]], 1).astype(bf16)
    own_len = lax.dynamic_slice_in_dim(lengths, head_at, 1)
    own_label = lax.dynamic_slice_in_dim(labels, head_at, 1)
    quarter = 2 * slots * slots * width
    x0, x0b, xa, q, k, v, lse, ctx = call(
        functools.partial(attend_kernel, shards),
        (
            shape((slots, width), f32),
            shape((slots, width), bf16),
            shape((slots, rank2), bf16),
            shape((shards, slots, LANES), bf16),
            shape((shards, slots, LANES), bf16),
            shape((shards, slots, LANES), bf16),
            shape((shards, 2, slots), f32),
            shape((slots, width), bf16),
        ),
        [SM, VM, VM, VM, VM, VM, ANY],
        (VM,) * 8,
        [
            pltpu.VMEM((shards // 2, width, 6 * LANES), bf16),
            pltpu.VMEM((shards // 2, rank2, 2 * LANES), bf16),
            pltpu.SemaphoreType.DMA((shards // 2, 8)),
        ],
        vmem=50,
        flops=6 * slots * width * width + 2 * quarter,
        moved=12 * MIB,
        exps=16 * slots * slots,
    )(own_len, emb, positions, layer_norm_gains, layer_norm_biases, down_pair, w_all)

    dctx, loss = call(
        functools.partial(middle_kernel, shards),
        (shape((slots, width), bf16), shape((1, LANES), f32)),
        [SM, SM, SM, VM, VM, VM, VM, VM] + [ANY] * 11,
        (VM, VM),
        [
            pltpu.VMEM((width, width), bf16),
            pltpu.VMEM((shards, width, units), bf16),
            pltpu.VMEM((shards, units, width), bf16),
            pltpu.VMEM((shards, slots, units), f32),
            pltpu.VMEM((slots, width), f32),
            pltpu.VMEM((slots, width), f32),
            pltpu.VMEM((slots, width), bf16),
            pltpu.VMEM((slots, width), f32),
            pltpu.VMEM((slots, width), bf16),
            pltpu.SemaphoreType.DMA((1,)),
            pltpu.SemaphoreType.DMA((shards, QUARTERS)),
            pltpu.SemaphoreType.DMA((shards, QUARTERS)),
        ],
        vmem=60,
        flops=8 * slots * width * units * shards + 4 * slots * width * width,
        moved=24 * MIB,
        exps=2 * slots * units * shards,
    )(
        own_len, own_label, jnp.stack([wi_turn, wf_turn]).astype(i32), x0, ctx, layer_norm_gains,
        layer_norm_biases, classifier, wo_all, *wi_parts, *wf_parts,
    )

    send, norm = call(
        functools.partial(gradient_kernel, shards, groups),
        (shape((devices, width // devices, 2 * rank2), f32), shape((1, LANES), f32)),
        [SM, VM, VM, VM, VM, VM, VM, VM, ANY],
        (VM, VM),
        [
            pltpu.VMEM((shards, rank2, LANES), bf16),
            pltpu.VMEM((width, rank2), f32),
            pltpu.VMEM((rank2, slots), f32),
            pltpu.SemaphoreType.DMA((shards,)),
        ],
        vmem=50,
        flops=4 * quarter,
        moved=8 * MIB,
        exps=16 * slots * slots,
    )(own_len, x0b, xa, q, k, v, lse, dctx, w_all)

    got = lax.all_to_all(send, ALL, 0, 0, tiled=True)
    examples = float(devices)
    step_number = optimizer_step_count.astype(f32)
    fixes = jnp.stack([1.0 - jnp.power(beta_one, step_number), 1.0 - jnp.power(beta_two, step_number)])
    where = jnp.stack([dp_at, head_at]).astype(i32)
    rows = width // devices
    small = shape((rows, 2 * rank2), f32)
    tile, um1, um2, direction, weight = call(
        functools.partial(direction_kernel, examples),
        (shape((devices, rows, LANES), f32), small, small, small, small),
        [SM, SM] + [VM] * 10,
        (VM,) * 5,
        [pltpu.VMEM((local_w, rank2), f32)],
    )(
        where, fixes, got, loss, adapter_down_maps, adapter_up_maps, down_first_moment, down_second_moment,
        up_first_moment, up_second_moment, down_privacy_noise, up_privacy_noise,
    )
    spread = lax.all_to_all(tile, ALL, 0, 0, tiled=True)
    down_shape = shape(down_first_moment.shape, f32)
    up_shape = shape(up_first_moment.shape, f32)
    loss_mean, dm1, dm2, dw, bm1, bm2, bw, table = call(
        functools.partial(update_kernel, examples, shards),
        (
            shape((1, 1), f32), down_shape, down_shape, down_shape, up_shape, up_shape, up_shape,
            shape((4, 2), f32),
        ),
        [SM, SM] + [VM] * 8,
        (VM,) * 8,
    )(
        where, fixes, spread, adapter_down_maps, down_first_moment, down_second_moment, um1, um2, direction,
        weight,
    )
    return (
        loss_mean.reshape(()),
        norm[0, 0:1],
        dm1,
        dm2,
        dw,
        bm1,
        bm2,
        bw,
        table,
    )


def solution(mesh):
    placed = (
        P("dp", None),
        P("dp"),
        P("dp"),
        P(),
        P("dp", "head"),
        P(),
        P(None, None, "head"),
        P("head", None),
        P(None, "head"),
        P("head", None),
        P(),
        P(),
        P(),
        P(),
        P(None, None, "head"),
        P(None, "dp", None),
        P(None, "dp", None),
        P(None, None, ("head", "dp")),
        P(None, None, ("head", "dp")),
        P(None, "dp", None),
        P(None, None, ("head", "dp")),
    )
    return jax.shard_map(
        per_device,
        mesh=mesh,
        in_specs=placed,
        out_specs=(
            P(),
            P(("dp", "head")),
            P(None, "dp", None),
            P(None, "dp", None),
            P(None, "dp", None),
            P(None, None, ("head", "dp")),
            P(None, None, ("head", "dp")),
            P(None, None, ("head", "dp")),
            P(),
        ),
        check_vma=False,
    )
```

```python
import functools

import jax
import jax.numpy as jnp
from jax import lax
from jax.experimental import pallas as pl
from jax.experimental.pallas import tpu as pltpu
from jax.sharding import PartitionSpec as P

HDIM = 64
CAP = 48
QUARTERS = 4
LANES = 128
MIB = 1 << 20

adapter_scale = 2.0
clip_bound = 1.0
noise_mult = 0.6
smooth_rate = 0.1
beta_one = 0.9
beta_two = 0.999
adam_eps = 1e-06
decay_rate = 0.01
learn_rate = 0.25
norm_eps = 1e-05

f32 = jnp.float32
bf16 = jnp.bfloat16
i32 = jnp.int32
LAST = (((1,), (1,)), ((), ()))
ALL = ("dp", "head")
VM = pl.BlockSpec(memory_space=pltpu.VMEM)
SM = pl.BlockSpec(memory_space=pltpu.SMEM)
ANY = pl.BlockSpec(memory_space=pl.ANY)


def iota(shape, axis):
    return lax.broadcasted_iota(i32, shape, axis)


def mm(a, b):
    return jnp.dot(a, b, preferred_element_type=f32)


def mm_last(a, b):
    return lax.dot_general(a, b, LAST, preferred_element_type=f32)


def call(kernel, outs, in_specs, out_specs, scratch=(), vmem=32, flops=10**10):
    return pl.pallas_call(
        kernel,
        out_shape=outs,
        in_specs=in_specs,
        out_specs=out_specs,
        scratch_shapes=list(scratch),
        compiler_params=pltpu.CompilerParams(vmem_limit_bytes=vmem * MIB),
        cost_estimate=pl.CostEstimate(flops=flops, bytes_accessed=1, transcendentals=0),
    )


def request_kernel(owners, peers, owned, sc_ref, len_ref, ids_ref, req_ref, slot_ref):
    me = sc_ref[0]
    base = (sc_ref[1] * CAP).astype(f32)
    count = len_ref[me]
    ids = ids_ref[...].astype(f32)
    examples, slots = ids.shape
    row = jnp.sum(jnp.where(iota(ids.shape, 0) == me, ids, 0.0), 0, keepdims=True)
    flipped = ids.T
    col = jnp.sum(jnp.where(iota(flipped.shape, 1) == me, flipped, 0.0), 1, keepdims=True)
    t_col = iota((slots, slots), 0)
    t_row = iota((slots, slots), 1)
    valid_col = (iota((slots, 1), 0) < count).astype(f32)
    valid_row = (iota((1, slots), 1) < count).astype(f32)
    own_col = sum((col >= k * owned).astype(f32) for k in range(1, owners))
    own_row = sum((row >= k * owned).astype(f32) for k in range(1, owners))
    same = (col == row) & (t_row < count) & (t_col < count)
    before = t_row < t_col
    after = t_col < t_row
    seen_col = jnp.sum(jnp.where(same & before, 1.0, 0.0), 1, keepdims=True)
    seen_row = jnp.sum(jnp.where(same & after, 1.0, 0.0), 0, keepdims=True)
    first_col = jnp.where(seen_col == 0.0, valid_col, 0.0)
    first_row = jnp.where(seen_row == 0.0, valid_row, 0.0)
    shared = own_col == own_row
    place_col = jnp.sum(jnp.where(shared & before, first_row, 0.0), 1, keepdims=True)
    place_row = jnp.sum(jnp.where(shared & after, first_col, 0.0), 0, keepdims=True)
    rank = jnp.sum(jnp.where(same, first_row * place_row, 0.0), 1, keepdims=True)
    local = rank - base
    here = (local >= 0.0) & (local < CAP) & (valid_col > 0.0)
    slot = jnp.where(here, own_col * CAP + local, -1.0)
    slot_ref[...] = jnp.broadcast_to(slot, slot_ref.shape).astype(i32)
    rounds = jnp.floor(jnp.max(rank, 0, keepdims=True) * (1.0 / CAP) + 0.5 / CAP) + 1.0
    lane = iota((slots, LANES), 1)
    lane_f = lane.astype(f32)
    wanted = jnp.where(first_col > 0.0, place_col - base, -1.0)
    hit = (wanted == lane_f) & (lane < CAP)
    lane_row = iota((1, LANES), 1)
    for owner in range(owners):
        chosen = jnp.where(hit & (own_col == float(owner)), col - float(owner * owned), 0.0)
        line = jnp.sum(chosen, 0, keepdims=True)
        line = jnp.where(lane_row == LANES - 1, rounds, line).astype(i32)
        for peer in range(peers):
            req_ref[owner * peers + peer] = line


def lookup_kernel(want_ref, table_ref, out_ref, wide_ref, stage_ref):
    wide_ref[...] = table_ref[...].astype(f32)

    def one(src, carry):
        for p in range(CAP):
            stage_ref[p : p + 1, :] = wide_ref[pl.ds(want_ref[src, 0, p], 1), :]
        out_ref[src] = stage_ref[...].astype(bf16)
        return carry

    lax.fori_loop(0, want_ref.shape[0], one, 0)


def assemble_kernel(owners, peers, got_ref, slot_ref, emb_ref, rows_ref):
    for owner in range(owners):
        for peer in range(peers):
            rows_ref[owner * CAP : (owner + 1) * CAP, peer * LANES : (peer + 1) * LANES] = got_ref[
                owner * peers + peer
            ]
    slot = slot_ref[...]
    lane = iota(slot.shape, 1)
    picks = [
        (slot == lane + first).astype(f32).astype(bf16)
        for first in range(0, owners * CAP, LANES)
    ]
    emb_ref[...] = mm(jnp.concatenate(picks, 1), rows_ref[...]).astype(bf16)


def stack_kernel(count, *refs):
    parts, whole, sems = refs[:count], refs[count], refs[count + 1]
    copies = [pltpu.make_async_copy(ref, whole.at[n], sems.at[n]) for n, ref in enumerate(parts)]
    for one in copies:
        one.start()
    for one in copies:
        one.wait()


def stack(parts):
    count = len(parts)
    return call(
        functools.partial(stack_kernel, count),
        jax.ShapeDtypeStruct((count, *parts[0].shape), parts[0].dtype),
        [ANY] * count,
        ANY,
        [pltpu.SemaphoreType.DMA((count,))],
        flops=1,
    )(*parts)


def pack_kernel(turn_ref, qkv_ref, up_ref, in_ref, out_ref, att_ref, packed_ref, dense_ref, up_low, sems):
    heads, rank2 = qkv_ref.shape[0], up_ref.shape[0]
    turn = turn_ref[0]
    half = in_ref.shape[1]
    moves = []
    at = 0
    for ref in (in_ref, out_ref, att_ref):
        rows = ref.shape[0] // QUARTERS
        here = pl.ds(pl.multiple_of(turn * rows, rows), rows)
        for first in range(0, ref.shape[1], half):
            moves.append((ref.at[here, pl.ds(first, half)], dense_ref.at[pl.ds(at, rows), :]))
            at += rows
    moves.append((qkv_ref, packed_ref.at[pl.ds(0, heads), :]))
    up_low[...] = up_ref[...].astype(bf16)
    moves.append((up_low, packed_ref.at[pl.ds(heads, rank2), :]))
    copies = [pltpu.make_async_copy(source, target, sems.at[n]) for n, (source, target) in enumerate(moves)]
    for one in copies:
        one.start()
    for one in copies:
        one.wait()


def normalize(inputs):
    centre = inputs - jnp.mean(inputs, -1, keepdims=True)
    inv_std = lax.rsqrt(jnp.mean(centre * centre, -1, keepdims=True) + norm_eps)
    return centre * inv_std, inv_std


def norm_back(scaled, x_hat, inv_std):
    return inv_std * (
        scaled
        - jnp.mean(scaled, -1, keepdims=True)
        - x_hat * jnp.mean(scaled * x_hat, -1, keepdims=True)
    )


def halves(pair):
    low = iota(pair.shape, 1) < HDIM
    zero = jnp.zeros_like(pair)
    return jnp.where(low, pair, zero), jnp.where(low, zero, pair)


def flip(x):
    return x.astype(f32).T


def project_kernel(
    shards, emb_ref, pos_ref, gain_ref, bias_ref, down_ref, w_own, w_peer,
    x_ref, xb_ref, xa_ref, q_ref, k_ref, v_ref,
    w_buf, up_buf, sems,
):
    slots, width = emb_ref.shape
    rank = down_ref.shape[1]
    rank2 = 2 * rank
    copies = []
    for pair in range(shards // 2):
        mine = []
        for side, w_ref in enumerate((w_own, w_peer)):
            for part in range(3):
                mine.append(
                    pltpu.make_async_copy(
                        w_ref.at[pair, pl.ds(part * width, width), :],
                        w_buf.at[pair, :, pl.ds((part * 2 + side) * LANES, LANES)],
                        sems.at[pair, side * 4 + part],
                    )
                )
            mine.append(
                pltpu.make_async_copy(
                    w_ref.at[pair, pl.ds(3 * width, rank2), :],
                    up_buf.at[pair, :, pl.ds(side * LANES, LANES)],
                    sems.at[pair, side * 4 + 3],
                )
            )
        copies.append(mine)
    for mine in copies:
        for one in mine:
            one.start()
    x_hat, unused_std = normalize(emb_ref[...].astype(f32) + pos_ref[...].astype(f32))
    x0 = x_hat * gain_ref[0:1, :] + bias_ref[0:1, :]
    x_ref[...] = x0
    xb_ref[...] = x0.astype(bf16)
    xa = mm_last(xb_ref[...], down_ref[...].reshape(rank2, width).astype(bf16)).astype(bf16)
    xa_ref[...] = xa
    low = iota(xa.shape, 1) < rank
    zero = jnp.zeros_like(xa)
    twice = xa * jnp.asarray(adapter_scale, bf16)
    twice_q = jnp.where(low, twice, zero)
    twice_v = jnp.where(low, zero, twice)
    for pair in range(shards // 2):
        for one in copies[pair]:
            one.wait()
        total = mm(xb_ref[...], w_buf[pair])
        two = 2 * LANES
        q2 = ((total[:, :two] + mm(twice_q, up_buf[pair])) * (HDIM**-0.5)).astype(bf16)
        k2 = total[:, two : 2 * two].astype(bf16)
        v2 = (total[:, 2 * two :] + mm(twice_v, up_buf[pair])).astype(bf16)
        for side in range(2):
            cut = slice(side * LANES, (side + 1) * LANES)
            q_ref[2 * pair + side] = q2[:, cut]
            k_ref[2 * pair + side] = k2[:, cut]
            v_ref[2 * pair + side] = v2[:, cut]


def attend_kernel(shards, len_ref, q_ref, k_ref, v_ref, lse_ref, ctx_ref):
    slots = q_ref.shape[1]
    count = len_ref[0]
    block = slots // 2
    keep = iota((slots, block), 0) < count

    def one_pair(j, carry):
        k_sides = halves(k_ref[j])
        v_flip = flip(v_ref[j]).astype(bf16)
        for first in range(0, slots, block):
            q = q_ref[j, first : first + block, :]
            parts = []
            for side in range(2):
                s = jnp.where(keep, mm_last(k_sides[side], q), -1e30)
                top = jnp.max(s, 0, keepdims=True)
                e = jnp.exp(s - top)
                total = jnp.sum(e, 0, keepdims=True)
                prob = (e * (1.0 / total)).astype(bf16)
                lse_ref[j, side : side + 1, first : first + block] = top + jnp.log(total)
                parts.append(mm(v_flip[side * HDIM : (side + 1) * HDIM, :], prob))
            both = jnp.concatenate(parts, 0).T
            ctx_ref[first : first + block, pl.ds(pl.multiple_of(j * LANES, LANES), LANES)] = (
                both.astype(bf16)
            )
        return carry

    lax.fori_loop(0, shards, one_pair, 0)


def gelu_parts(x):
    z = jnp.abs(x) * (0.5**0.5)
    t = 1.0 / (1.0 + 0.3275911 * z)
    poly = t * (
        0.254829592
        + t * (-0.284496736 + t * (1.421413741 + t * (-1.453152027 + t * 1.061405429)))
    )
    bell = jnp.exp(-0.5 * x * x)
    tail = 0.5 * poly * bell
    cdf = jnp.where(x < 0.0, tail, 1.0 - tail)
    return x * cdf, cdf + x * bell * 0.3989422804014327


def middle_kernel(
    shards, len_ref, label_ref, turn_ref, x_ref, ctx_ref, gain_ref, bias_ref, class_ref,
    own_0, own_1, own_2, own_3, peer_0, peer_1, peer_2, peer_3,
    dctx_ref, loss_ref,
    wo_buf, wi_buf, wf_buf, slope_buf, acc_ref, h_ref, hb_ref, hat_ref, df_ref, sems,
):
    slots, width = x_ref.shape
    classes = class_ref.shape[0]
    unit = wf_buf.shape[1]
    planes = shards // 2
    in_rows, out_rows, att_rows = width // QUARTERS, unit // QUARTERS, width // shards // QUARTERS
    half = width // 2
    wo_copies, wi_copies, wf_copies = [], [[], []], [[], []]
    for column, refs in enumerate(((own_0, own_1, own_2, own_3), (peer_0, peer_1, peer_2, peer_3))):
        for step, ref in enumerate(refs):
            turn = lax.rem(turn_ref[0] + step, QUARTERS)
            for side in range(2):
                wo_copies.append(
                    pltpu.make_async_copy(
                        ref.at[:, pl.ds(in_rows + 2 * out_rows + side * att_rows, att_rows), :],
                        wo_buf.at[
                            :,
                            pl.ds(pl.multiple_of(column * (width // shards) + turn * att_rows, att_rows), att_rows),
                            pl.ds(side * half, half),
                        ],
                        sems.at[column, step, side],
                    )
                )
                wf_copies[column].append(
                    pltpu.make_async_copy(
                        ref.at[:, pl.ds(in_rows + side * out_rows, out_rows), :],
                        wf_buf.at[
                            pl.ds(column * planes, planes),
                            pl.ds(pl.multiple_of(turn * out_rows, out_rows), out_rows),
                            pl.ds(side * half, half),
                        ],
                        sems.at[column, step, 2 + side],
                    )
                )
            wi_copies[column].append(
                pltpu.make_async_copy(
                    ref.at[:, pl.ds(0, in_rows), :],
                    wi_buf.at[
                        pl.ds(column * planes, planes),
                        pl.ds(pl.multiple_of(turn * in_rows, in_rows), in_rows),
                        :,
                    ],
                    sems.at[column, step, 4],
                )
            )
    for one in wo_copies:
        one.start()
    for column in range(2):
        for one in wi_copies[column] + wf_copies[column]:
            one.start()
    count = len_ref[0]
    count_f = count.astype(f32)
    label = label_ref[0]
    for one in wo_copies:
        one.wait()
    hat1, std1 = normalize(x_ref[...] + mm(ctx_ref[...], wo_buf[...].reshape(width, width)))
    hat_ref[...] = hat1
    h1 = hat1 * gain_ref[1:2, :] + bias_ref[1:2, :]
    h_ref[...] = h1
    hb_ref[...] = h1.astype(bf16)
    for f in range(shards):
        if f % planes == 0:
            for one in wi_copies[f // planes]:
                one.wait()
        g, slope = gelu_parts(mm(hb_ref[...], wi_buf[f]))
        slope_buf[f] = slope
        if f % planes == 0:
            for one in wf_copies[f // planes]:
                one.wait()
        part = mm(g.astype(bf16), wf_buf[f])
        if f == 0:
            acc_ref[...] = part
        else:
            acc_ref[...] += part
    hat2, std2 = normalize(h_ref[...] + acc_ref[...])
    gain2 = gain_ref[2:3, :]
    valid = (iota((slots, 1), 0) < count).astype(f32)
    pooled = jnp.sum((hat2 * gain2 + bias_ref[2:3, :]) * valid, 0, keepdims=True) / count_f
    weights = class_ref[...].astype(f32)
    logits = jnp.sum(pooled.astype(bf16).astype(f32) * weights, 1, keepdims=True)
    shifted = logits - jnp.max(logits, 0, keepdims=True)
    log_prob = shifted - jnp.log(jnp.sum(jnp.exp(shifted), 0, keepdims=True))
    target = (1.0 - smooth_rate) * (iota((classes, 1), 0) == label).astype(f32) + smooth_rate / classes
    loss_ref[...] = jnp.broadcast_to(-jnp.sum(target * log_prob, 0, keepdims=True), loss_ref.shape)
    d_pooled = jnp.sum((jnp.exp(log_prob) - target) * weights, 0, keepdims=True) / count_f
    d_two = norm_back((d_pooled * gain2) * valid, hat2, std2)
    acc_ref[...] = d_two
    df_ref[...] = d_two.astype(bf16)
    for f in range(shards):
        d_pre = (mm_last(df_ref[...], wf_buf[f]) * slope_buf[f]).astype(bf16)
        acc_ref[...] += mm_last(d_pre, wi_buf[f])
    d_attn = norm_back(acc_ref[...] * gain_ref[1:2, :], hat_ref[...], std1).astype(bf16)
    dctx_ref[...] = mm_last(d_attn, wo_buf[...].reshape(width, width)).astype(bf16)


def gradient_kernel(
    shards, groups, len_ref, order_ref, xb_ref, xa_ref, q_ref, k_ref, v_ref, lse_ref, dctx_ref, w_own, w_peer,
    send_ref, norm_ref,
    up_buf, up_grad, inner_ref, sems,
):
    slots, width = xb_ref.shape
    rank2 = xa_ref.shape[1]
    rank = rank2 // 2
    copies = [
        pltpu.make_async_copy(
            (w_own, w_peer)[j % 2].at[j // 2, pl.ds(3 * width, rank2), :], up_buf.at[j], sems.at[j]
        )
        for j in range(shards)
    ]
    for one in copies:
        one.start()
    for one in copies:
        one.wait()
    count = len_ref[0]
    block = slots // 2
    keep = iota((slots, block), 0) < count
    xa = xa_ref[...]
    low = iota((LANES, rank2), 1) < rank
    inner_ref[...] = jnp.zeros_like(inner_ref)

    def one_pair(j, carry):
        k = k_ref[j]
        k_sides = halves(k)
        v_sides = halves(v_ref[j])
        k_flip = flip(k).astype(bf16)
        dv = jnp.zeros((slots, LANES), f32)
        flips = []
        for first in range(0, slots, block):
            q = q_ref[j, first : first + block, :]
            dctx = dctx_ref[first : first + block, pl.ds(pl.multiple_of(j * LANES, LANES), LANES)]
            dctx_sides = halves(dctx)
            parts = []
            for side in range(2):
                s = jnp.where(keep, mm_last(k_sides[side], q), -1e30)
                prob = jnp.exp(s - lse_ref[j, side : side + 1, first : first + block])
                d_prob = mm_last(v_sides[side], dctx)
                weighted = jnp.sum(prob * d_prob, 0, keepdims=True)
                d_s = (prob * (d_prob - weighted)).astype(bf16)
                dv = dv + mm(prob.astype(bf16), dctx_sides[side])
                parts.append(mm(k_flip[side * HDIM : (side + 1) * HDIM, :], d_s))
            flips.append(jnp.concatenate(parts, 0))
        dq_flip = (jnp.concatenate(flips, 1) * (HDIM**-0.5)).astype(bf16)
        dv_flip = flip(dv.astype(bf16)).astype(bf16)
        up_grad[pl.ds(pl.multiple_of(order_ref[j] * LANES, LANES), LANES), :] = adapter_scale * jnp.where(
            low, mm(dq_flip, xa), mm(dv_flip, xa)
        )
        inner_ref[0:rank, :] += adapter_scale * mm(up_buf[j, 0:rank, :], dq_flip)
        inner_ref[rank:rank2, :] += adapter_scale * mm(up_buf[j, rank:rank2, :], dv_flip)
        return carry

    lax.fori_loop(0, shards, one_pair, 0)
    down_grad = mm(inner_ref[...].astype(bf16), xb_ref[...]).T
    both = jnp.concatenate([up_grad[...], down_grad], 1)
    squares = jnp.sum(jnp.sum(both * both, 1, keepdims=True), 0, keepdims=True)
    norm = jnp.sqrt(squares)
    norm_ref[...] = jnp.broadcast_to(norm, norm_ref.shape)
    both = both * (clip_bound / jnp.maximum(norm, clip_bound))
    rows = width // (groups * shards)
    send_ref[...] = jnp.zeros_like(send_ref)
    for i in range(groups):
        for j in range(shards):
            to = i * shards + j
            at_up = (j * groups + i) * rows
            at_down = to * rows
            send_ref[to, :, 0:rank2] = both[at_up : at_up + rows, 0:rank2]
            send_ref[to, :, rank2 : 2 * rank2] = both[at_down : at_down + rows, rank2:]


def lamb(weight, grad, first, second, fix_one, fix_two):
    first_new = beta_one * first + (1.0 - beta_one) * grad
    second_new = beta_two * second + (1.0 - beta_two) * grad * grad
    direction = first_new / fix_one / (jnp.sqrt(second_new / fix_two) + adam_eps) + decay_rate * weight
    return first_new, second_new, direction


def side_by_side(ref):
    return jnp.concatenate([ref[0], ref[1]], 1)


def flipped(ref):
    maps, rank, cols = ref.shape
    return ref[...].reshape(maps * rank, cols).T


def direction_kernel(
    examples, sc_ref, fix_ref, got_ref, loss_ref, down_ref, up_ref, dm1_ref, dm2_ref, um1_ref, um2_ref,
    dn_ref, un_ref,
    tile_ref, um1_out, um2_out, dir_ref, w_out, up_turn, down_turn, part_turn,
):
    dp_at, head_at = sc_ref[0], sc_ref[1]
    rows = got_ref.shape[1]
    rank2 = up_turn.shape[1]
    up_at = pl.multiple_of(dp_at * rows, rows)
    at = pl.multiple_of(head_at * rows, rows)
    down_at = pl.multiple_of(dp_at * dm1_ref.shape[2] + head_at * rows, rows)
    up_turn[...] = flipped(up_ref)
    down_turn[...] = flipped(down_ref)
    for n, ref in enumerate((dn_ref, dm1_ref, dm2_ref)):
        part_turn[n] = flipped(ref)
    here = pl.ds(at, rows)
    weight = jnp.concatenate([up_turn[pl.ds(up_at, rows), :], down_turn[pl.ds(down_at, rows), :]], 1)
    noise = jnp.concatenate([side_by_side(un_ref), part_turn[0, here, :]], 1)
    first = jnp.concatenate([side_by_side(um1_ref), part_turn[1, here, :]], 1)
    second = jnp.concatenate([side_by_side(um2_ref), part_turn[2, here, :]], 1)
    total = jnp.sum(got_ref[...], 0)[:, : 2 * rank2]
    grad = (total + noise_mult * clip_bound * noise) / examples
    first_new, second_new, direction = lamb(weight, grad, first, second, fix_ref[0], fix_ref[1])
    um1_out[...] = first_new
    um2_out[...] = second_new
    dir_ref[...] = direction
    w_out[...] = weight
    down_grad = grad[:, rank2:]
    per_line = LANES // rank2
    lines = [
        jnp.concatenate([down_grad[k : k + 1] for k in range(line, line + per_line)], 1)
        for line in range(0, rows, per_line)
    ]
    lines.append(
        jnp.concatenate(
            [jnp.sum(direction * direction, 0, keepdims=True), jnp.sum(weight * weight, 0, keepdims=True)], 1
        )
    )
    lines.append(loss_ref[...])
    tile = jnp.concatenate(lines, 0)
    for to in range(tile_ref.shape[0]):
        tile_ref[to] = tile


def update_kernel(
    examples, shards, sc_ref, fix_ref, got_ref, down_ref, dm1_ref, dm2_ref, um1_ref, um2_ref, dir_ref, w_ref,
    loss_ref, dm1_out, dm2_out, dw_out, um1_out, um2_out, uw_out, table_ref, down_turn,
):
    dp_at = sc_ref[0]
    rows = w_ref.shape[0]
    rank2 = w_ref.shape[1] // 2
    rank = rank2 // 2
    per_line = LANES // rank2
    lines = rows // per_line
    total = jnp.sum(got_ref[...], 0)
    loss_ref[...] = total[lines + 1 : lines + 2, 0:1] / examples
    stats = total[lines : lines + 1, :]
    lane = iota(stats.shape, 1)

    def part(group):
        inside = (lane >= group * rank) & (lane < (group + 1) * rank)
        return jnp.sqrt(jnp.sum(jnp.where(inside, stats, 0.0), 1, keepdims=True))

    norms = [(part(group + 4), part(group)) for group in range(4)]
    for out_col, group in enumerate((2, 3, 0, 1)):
        table_ref[:, out_col : out_col + 1] = jnp.concatenate(norms[group], 0)

    def rate(a, b):
        wide = iota((1, rank2), 1) < rank
        return learn_rate * jnp.where(wide, norms[a][0] / norms[a][1], norms[b][0] / norms[b][1])

    up_new = w_ref[:, :rank2] - rate(0, 1) * dir_ref[:, :rank2]
    for ref, value in ((uw_out, up_new), (um1_out, um1_ref[...]), (um2_out, um2_ref[...])):
        ref[0] = value[:, :rank]
        ref[1] = value[:, rank:rank2]
    grad = jnp.concatenate(
        [
            got_ref[dp_at * shards + j, k // per_line, (k % per_line) * rank2 : (k % per_line + 1) * rank2]
            .reshape(1, rank2)
            for j in range(shards)
            for k in range(rows)
        ],
        0,
    )
    many = dm1_ref.shape[2]
    down_turn[...] = flipped(down_ref)
    weight = down_turn[pl.ds(pl.multiple_of(dp_at * many, many), many), :]
    first_new, second_new, direction = lamb(
        weight, grad, flipped(dm1_ref), flipped(dm2_ref), fix_ref[0], fix_ref[1]
    )
    new = weight - rate(2, 3) * direction
    for ref, value in ((dm1_out, first_new), (dm2_out, second_new), (dw_out, new)):
        ref[...] = value.T.reshape(ref.shape)


def per_device(
    slot_token_ids,
    lengths,
    labels,
    optimizer_step_count,
    token_embedding_table,
    positions,
    query_key_value_weight,
    attention_output_weight,
    feedforward_input_weight,
    feedforward_output_weight,
    layer_norm_gains,
    layer_norm_biases,
    classifier,
    adapter_down_maps,
    adapter_up_maps,
    down_first_moment,
    down_second_moment,
    up_first_moment,
    up_second_moment,
    down_privacy_noise,
    up_privacy_noise,
):
    shards = lax.axis_size("head")
    groups = lax.axis_size("dp")
    devices = shards * groups
    dp_at = lax.axis_index("dp")
    head_at = lax.axis_index("head")
    slots, width = positions.shape
    rank = adapter_down_maps.shape[2]
    rank2 = 2 * rank
    units = feedforward_output_weight.shape[0]
    local_w = attention_output_weight.shape[0]
    owned = token_embedding_table.shape[0]
    shape = jax.ShapeDtypeStruct

    def turned(x):
        return jnp.swapaxes(x, 1, 2)

    down_maps = turned(adapter_down_maps)

    def ask(which, slot_token_ids):
        return call(
            functools.partial(request_kernel, groups, shards, owned),
            (shape((devices, 1, LANES), i32), shape((slots, LANES), i32)),
            [SM, SM, VM],
            (VM, VM),
            flops=10**11,
        )(jnp.stack([head_at, which]).astype(i32), lengths, slot_token_ids)

    def look(wanted):
        return call(
            lookup_kernel,
            shape((devices, CAP, LANES), bf16),
            [SM, VM],
            VM,
            [pltpu.VMEM((owned, LANES), f32), pltpu.VMEM((CAP, LANES), f32)],
            flops=10**11,
        )(wanted, token_embedding_table)

    def place(found, slot):
        got = exchange(found)
        emb = call(
            functools.partial(assemble_kernel, groups, shards),
            shape((slots, width), bf16),
            [VM, VM],
            VM,
            [pltpu.VMEM((groups * CAP, width), bf16)],
        )(got, slot)
        return emb

    def exchange(x):
        return lax.all_to_all(x, ALL, 0, 0, tiled=True)

    side = QUARTERS
    y_at, x_at = dp_at // side, dp_at % side
    turn = ((x_at + 2 * y_at) % QUARTERS).reshape(1).astype(i32)

    def along_z(x, steps):
        return [
            lax.ppermute(x, "head", [((i + 2 * step) % shards, i) for i in range(shards)]) for step in steps
        ]

    def neighbour(x, dy, dx):
        pairs = [
            (((y + dy) % side) * side + (c + dx) % side, y * side + c) for y in range(side) for c in range(side)
        ]
        return lax.ppermute(x, "dp", pairs)

    def other_core(x):
        return lax.ppermute(x, "head", [(i, i ^ 1) for i in range(shards)])

    rows = (width + 2 * units + 2 * local_w) // QUARTERS
    packed, dense = call(
        pack_kernel,
        (shape((3 * width + rank2, local_w), bf16), shape((rows, feedforward_input_weight.shape[1]), bf16)),
        [SM, ANY, VM, ANY, ANY, ANY],
        (ANY, ANY),
        [pltpu.VMEM((rank2, local_w), bf16), pltpu.SemaphoreType.DMA((7,))],
    )(
        turn,
        query_key_value_weight.reshape(3 * width, local_w),
        adapter_up_maps.reshape(rank2, local_w),
        feedforward_input_weight,
        feedforward_output_weight,
        attention_output_weight,
    )
    planes = range(1, shards // 2)
    dense_z = along_z(dense, planes)
    packed, slot_token_ids = lax.optimization_barrier((packed, slot_token_ids))
    requests, slot = ask(jnp.zeros((), i32), slot_token_ids)

    wanted, packed, dense_z = lax.optimization_barrier((exchange(requests), packed, dense_z))
    packed_z = along_z(packed, planes)
    rounds = jnp.max(wanted[:, 0, LANES - 1])
    found = look(wanted)
    dense_0 = stack([dense, *dense_z])
    dense_own = (dense_0, neighbour(dense_0, 0, 1), neighbour(dense_0, 1, 0), neighbour(dense_0, 0, -1))
    w_own = stack([packed, *packed_z])
    w_peer = other_core(w_own)
    peer_0 = other_core(dense_0)
    emb = place(found, slot)

    def again(which):
        asked, where = ask(which, slot_token_ids)
        return place(look(exchange(asked)), where)

    unused_at, emb = lax.while_loop(
        lambda state: state[0] < rounds,
        lambda state: (state[0] + 1, state[1] + again(state[0])),
        (jnp.ones((), i32), emb),
    )

    own_len = lax.dynamic_slice_in_dim(lengths, head_at, 1)
    own_label = lax.dynamic_slice_in_dim(labels, head_at, 1)
    x0, x0b, xa, q, k, v = call(
        functools.partial(project_kernel, shards),
        (
            shape((slots, width), f32),
            shape((slots, width), bf16),
            shape((slots, rank2), bf16),
            shape((shards, slots, LANES), bf16),
            shape((shards, slots, LANES), bf16),
            shape((shards, slots, LANES), bf16),
        ),
        [VM, VM, VM, VM, VM, ANY, ANY],
        (VM,) * 6,
        [
            pltpu.VMEM((shards // 2, width, 6 * LANES), bf16),
            pltpu.VMEM((shards // 2, rank2, 2 * LANES), bf16),
            pltpu.SemaphoreType.DMA((shards // 2, 8)),
        ],
        vmem=50,
    )(emb, positions, layer_norm_gains, layer_norm_biases, down_maps, w_own, w_peer)
    q, dense_own = lax.optimization_barrier((q, dense_own))
    dense_peer = [peer_0] + [other_core(x) for x in dense_own[1:]]
    lse, ctx = call(
        functools.partial(attend_kernel, shards),
        (shape((shards, 2, slots), f32), shape((slots, width), bf16)),
        [SM, VM, VM, VM],
        (VM, VM),
        vmem=40,
    )(own_len, q, k, v)

    dctx, loss = call(
        functools.partial(middle_kernel, shards),
        (shape((slots, width), bf16), shape((1, LANES), f32)),
        [SM, SM, SM, VM, VM, VM, VM, VM] + [ANY] * 8,
        (VM, VM),
        [
            pltpu.VMEM((shards // 2, 2 * width // shards, width), bf16),
            pltpu.VMEM((shards, width, units), bf16),
            pltpu.VMEM((shards, units, width), bf16),
            pltpu.VMEM((shards, slots, units), f32),
            pltpu.VMEM((slots, width), f32),
            pltpu.VMEM((slots, width), f32),
            pltpu.VMEM((slots, width), bf16),
            pltpu.VMEM((slots, width), f32),
            pltpu.VMEM((slots, width), bf16),
            pltpu.SemaphoreType.DMA((2, QUARTERS, 5)),
        ],
        vmem=60,
    )(
        own_len, own_label, turn, x0, ctx, layer_norm_gains, layer_norm_biases,
        classifier, *dense_own, *dense_peer,
    )

    z_at, core_at = head_at // 2, head_at % 2
    order = jnp.stack(
        [
            2 * ((z_at + step) % (shards // 2)) + (core_at + column) % 2
            for step in range(shards // 2)
            for column in range(2)
        ]
    ).astype(i32)
    send, norm = call(
        functools.partial(gradient_kernel, shards, groups),
        (shape((devices, width // devices, LANES), f32), shape((1, LANES), f32)),
        [SM, SM, VM, VM, VM, VM, VM, VM, VM, ANY, ANY],
        (VM, VM),
        [
            pltpu.VMEM((shards, rank2, LANES), bf16),
            pltpu.VMEM((width, rank2), f32),
            pltpu.VMEM((rank2, slots), f32),
            pltpu.SemaphoreType.DMA((shards,)),
        ],
        vmem=50,
    )(own_len, order, x0b, xa, q, k, v, lse, dctx, w_own, w_peer)

    got = exchange(send)
    examples = float(devices)
    step_number = optimizer_step_count.astype(f32)
    fixes = jnp.stack([1.0 - jnp.power(beta_one, step_number), 1.0 - jnp.power(beta_two, step_number)])
    where = jnp.stack([dp_at, head_at]).astype(i32)
    rows = width // devices
    small = shape((rows, 2 * rank2), f32)
    moments = [turned(x) for x in (down_first_moment, down_second_moment, up_first_moment, up_second_moment)]
    lines = rows * rank2 // LANES + 2
    tile, um1, um2, direction, weight = call(
        functools.partial(direction_kernel, examples),
        (shape((devices, lines, LANES), f32), small, small, small, small),
        [SM, SM] + [VM] * 10,
        (VM,) * 5,
        [
            pltpu.VMEM((local_w, rank2), f32),
            pltpu.VMEM((width, rank2), f32),
            pltpu.VMEM((3, width // groups, rank2), f32),
        ],
    )(
        where, fixes, got, loss, down_maps, adapter_up_maps, *moments,
        turned(down_privacy_noise), turned(up_privacy_noise),
    )
    spread = exchange(tile)
    down_shape = shape(moments[0].shape, f32)
    up_shape = shape(moments[2].shape, f32)
    loss_mean, dm1, dm2, dw, bm1, bm2, bw, table = call(
        functools.partial(update_kernel, examples, shards),
        (
            shape((1, 1), f32), down_shape, down_shape, down_shape, up_shape, up_shape, up_shape,
            shape((2, 4), f32),
        ),
        [SM, SM] + [VM] * 8,
        (VM,) * 8,
        [pltpu.VMEM((width, rank2), f32)],
    )(where, fixes, spread, down_maps, moments[0], moments[1], um1, um2, direction, weight)
    return (
        loss_mean.reshape(()),
        norm[0, 0:1],
        turned(dm1),
        turned(dm2),
        turned(dw),
        turned(bm1),
        turned(bm2),
        turned(bw),
        table.T,
    )


def solution(mesh):
    placed = (
        P("dp", None),
        P("dp"),
        P("dp"),
        P(),
        P("dp", "head"),
        P(),
        P(None, None, "head"),
        P("head", None),
        P(None, "head"),
        P("head", None),
        P(),
        P(),
        P(),
        P(),
        P(None, None, "head"),
        P(None, "dp", None),
        P(None, "dp", None),
        P(None, None, ("head", "dp")),
        P(None, None, ("head", "dp")),
        P(None, "dp", None),
        P(None, None, ("head", "dp")),
    )
    return jax.shard_map(
        per_device,
        mesh=mesh,
        in_specs=placed,
        out_specs=(
            P(),
            P(("dp", "head")),
            P(None, "dp", None),
            P(None, "dp", None),
            P(None, "dp", None),
            P(None, None, ("head", "dp")),
            P(None, None, ("head", "dp")),
            P(None, None, ("head", "dp")),
            P(),
        ),
        check_vma=False,
    )
```

```python
import functools

import jax
import jax.numpy as jnp
from jax import lax
from jax.experimental import pallas as pl
from jax.experimental.pallas import tpu as pltpu
from jax.sharding import PartitionSpec as P

HDIM = 64
CAP = 48
GROUPS = 16
LANES = 128
MIB = 1 << 20

adapter_scale = 2.0
clip_bound = 1.0
noise_mult = 0.6
smooth_rate = 0.1
beta_one = 0.9
beta_two = 0.999
adam_eps = 1e-06
decay_rate = 0.01
learn_rate = 0.25
norm_eps = 1e-05

f32 = jnp.float32
bf16 = jnp.bfloat16
i32 = jnp.int32
LAST = (((1,), (1,)), ((), ()))
ALL = ("dp", "head")
VM = pl.BlockSpec(memory_space=pltpu.VMEM)
SM = pl.BlockSpec(memory_space=pltpu.SMEM)
ANY = pl.BlockSpec(memory_space=pl.ANY)


def iota(shape, axis):
    return lax.broadcasted_iota(i32, shape, axis)


def mm(a, b):
    return jnp.dot(a, b, preferred_element_type=f32)


def mm_last(a, b):
    return lax.dot_general(a, b, LAST, preferred_element_type=f32)


def call(kernel, outs, in_specs, out_specs, scratch=(), vmem=32):
    return pl.pallas_call(
        kernel,
        out_shape=outs,
        in_specs=in_specs,
        out_specs=out_specs,
        scratch_shapes=list(scratch),
        compiler_params=pltpu.CompilerParams(vmem_limit_bytes=vmem * MIB),
        cost_estimate=pl.CostEstimate(flops=1, bytes_accessed=1, transcendentals=0),
    )


def request_kernel(owners, peers, owned, sc_ref, len_ref, ids_ref, req_ref, slot_ref):
    me = sc_ref[0]
    base = (sc_ref[1] * CAP).astype(f32)
    count = len_ref[me]
    ids = ids_ref[...].astype(f32)
    examples, slots = ids.shape
    row = jnp.sum(jnp.where(iota(ids.shape, 0) == me, ids, 0.0), 0, keepdims=True)
    flipped = ids.T
    col = jnp.sum(jnp.where(iota(flipped.shape, 1) == me, flipped, 0.0), 1, keepdims=True)
    t_col = iota((slots, slots), 0)
    t_row = iota((slots, slots), 1)
    valid_col = (iota((slots, 1), 0) < count).astype(f32)
    valid_row = (iota((1, slots), 1) < count).astype(f32)
    own_col = sum((col >= k * owned).astype(f32) for k in range(1, owners))
    own_row = sum((row >= k * owned).astype(f32) for k in range(1, owners))
    same = (col == row) & (t_row < count) & (t_col < count)
    before = t_row < t_col
    after = t_col < t_row
    seen_col = jnp.sum(jnp.where(same & before, 1.0, 0.0), 1, keepdims=True)
    seen_row = jnp.sum(jnp.where(same & after, 1.0, 0.0), 0, keepdims=True)
    first_col = jnp.where(seen_col == 0.0, valid_col, 0.0)
    first_row = jnp.where(seen_row == 0.0, valid_row, 0.0)
    shared = own_col == own_row
    place_col = jnp.sum(jnp.where(shared & before, first_row, 0.0), 1, keepdims=True)
    place_row = jnp.sum(jnp.where(shared & after, first_col, 0.0), 0, keepdims=True)
    rank = jnp.sum(jnp.where(same, first_row * place_row, 0.0), 1, keepdims=True)
    local = rank - base
    here = (local >= 0.0) & (local < CAP) & (valid_col > 0.0)
    slot = jnp.where(here, own_col * CAP + local, -1.0)
    slot_ref[...] = jnp.broadcast_to(slot, slot_ref.shape).astype(i32)
    rounds = jnp.floor(jnp.max(rank, 0, keepdims=True) * (1.0 / CAP) + 0.5 / CAP) + 1.0
    lane = iota((slots, LANES), 1)
    lane_f = lane.astype(f32)
    wanted = jnp.where(first_col > 0.0, place_col - base, -1.0)
    hit = (wanted == lane_f) & (lane < CAP)
    lane_row = iota((1, LANES), 1)
    for owner in range(owners):
        chosen = jnp.where(hit & (own_col == float(owner)), col - float(owner * owned), 0.0)
        line = jnp.sum(chosen, 0, keepdims=True)
        line = jnp.where(lane_row == LANES - 1, rounds, line).astype(i32)
        for peer in range(peers):
            req_ref[owner * peers + peer] = line


def lookup_kernel(want_ref, table_ref, out_ref, wide_ref, stage_ref):
    wide_ref[...] = table_ref[...].astype(f32)

    def one(src, carry):
        for p in range(CAP):
            stage_ref[p : p + 1, :] = wide_ref[pl.ds(want_ref[src, 0, p], 1), :]
        out_ref[src] = stage_ref[...].astype(bf16)
        return carry

    lax.fori_loop(0, want_ref.shape[0], one, 0)


def assemble_kernel(owners, peers, got_ref, slot_ref, emb_ref, rows_ref):
    for owner in range(owners):
        for peer in range(peers):
            rows_ref[owner * CAP : (owner + 1) * CAP, peer * LANES : (peer + 1) * LANES] = got_ref[
                owner * peers + peer
            ]
    slot = slot_ref[...]
    lane = iota(slot.shape, 1)
    picks = [
        (slot == lane + first).astype(f32).astype(bf16)
        for first in range(0, owners * CAP, LANES)
    ]
    emb_ref[...] = mm(jnp.concatenate(picks, 1), rows_ref[...]).astype(bf16)


def pack_kernel(at_ref, qkv_ref, up_ref, in_ref, out_ref, att_ref, pack_ref, sems):
    at = at_ref[0]
    wide = in_ref.shape[1]
    in_rows, out_rows = in_ref.shape[0] // GROUPS, out_ref.shape[0] // GROUPS
    att_rows = 2 * att_ref.shape[0] // GROUPS
    here = lambda rows: pl.ds(pl.multiple_of(at * rows, rows), rows)
    moves = [(in_ref.at[here(in_rows), :], pack_ref.at[pl.ds(0, in_rows), :])]
    row = in_rows
    for first in range(0, 2 * wide, wide):
        moves.append((out_ref.at[here(out_rows), pl.ds(first, wide)], pack_ref.at[pl.ds(row, out_rows), :]))
        row += out_rows
    half = att_ref.at[
        pl.ds(pl.multiple_of(at // 2 * att_rows, att_rows), att_rows),
        pl.ds(pl.multiple_of(at % 2 * wide, wide), wide),
    ]
    moves.append((half, pack_ref.at[pl.ds(row, att_rows), :]))
    row += att_rows
    for part in range(qkv_ref.shape[0]):
        moves.append(
            (qkv_ref.at[part, here(in_rows), :], pack_ref.at[pl.ds(row, in_rows), pl.ds(part * LANES, LANES)])
        )
    copies = [pltpu.make_async_copy(source, target, sems.at[n]) for n, (source, target) in enumerate(moves)]
    for one in copies:
        one.start()
    rank2 = up_ref.shape[0]
    pack_ref[row : row + rank2, 3 * LANES :] = up_ref[...].astype(bf16)
    pack_ref[row + rank2 :, 3 * LANES :] = jnp.zeros((in_rows - rank2, wide - 3 * LANES), bf16)
    for one in copies:
        one.wait()


def normalize(inputs):
    centre = inputs - jnp.mean(inputs, -1, keepdims=True)
    inv_std = lax.rsqrt(jnp.mean(centre * centre, -1, keepdims=True) + norm_eps)
    return centre * inv_std, inv_std


def norm_back(scaled, x_hat, inv_std):
    return inv_std * (
        scaled
        - jnp.mean(scaled, -1, keepdims=True)
        - x_hat * jnp.mean(scaled * x_hat, -1, keepdims=True)
    )


def halves(pair):
    low = iota(pair.shape, 1) < HDIM
    zero = jnp.zeros_like(pair)
    return jnp.where(low, pair, zero), jnp.where(low, zero, pair)


def flip(x):
    return x.astype(f32).T


def rows_of(shards, width):
    in_rows = width // GROUPS
    return in_rows, in_rows // 2, 2 * width // shards // GROUPS


def project_kernel(
    shards, emb_ref, pos_ref, gain_ref, bias_ref, down_ref, w_ref,
    x_ref, xb_ref, xa_ref, q_ref, k_ref, v_ref,
    w_buf, up_buf, sems,
):
    slots, width = emb_ref.shape
    rank = down_ref.shape[1]
    rank2 = 2 * rank
    in_rows, out_rows, att_rows = rows_of(shards, width)
    start = in_rows + 2 * out_rows + att_rows
    three = 3 * LANES
    copies = []
    for shard in range(shards):
        pair, side = shard // 2, shard % 2
        mine = [
            pltpu.make_async_copy(
                w_ref.at[shard, :, pl.ds(start, in_rows), pl.ds(0, three)],
                w_buf.at[pair, :, :, pl.ds(side * three, three)],
                sems.at[shard, 0],
            )
        ]
        for part in range(2):
            mine.append(
                pltpu.make_async_copy(
                    w_ref.at[shard, 0, pl.ds(start + part * rank, rank), pl.ds(three, LANES)],
                    up_buf.at[pair, pl.ds(part * rank, rank), pl.ds(side * three + 2 * part * LANES, LANES)],
                    sems.at[shard, 1 + part],
                )
            )
        copies.append(mine)
    up_buf[...] = jnp.zeros_like(up_buf)
    for mine in copies:
        for one in mine:
            one.start()
    x_hat, unused_std = normalize(emb_ref[...].astype(f32) + pos_ref[...].astype(f32))
    x0 = x_hat * gain_ref[0:1, :] + bias_ref[0:1, :]
    x_ref[...] = x0
    xb_ref[...] = x0.astype(bf16)
    xa = mm_last(xb_ref[...], down_ref[...].reshape(rank2, width).astype(bf16)).astype(bf16)
    xa_ref[...] = xa
    twice = xa * jnp.asarray(adapter_scale, bf16)
    for pair in range(shards // 2):
        for one in copies[2 * pair] + copies[2 * pair + 1]:
            one.wait()
        total = mm(xb_ref[...], w_buf[pair].reshape(width, 2 * three)) + mm(twice, up_buf[pair])
        for side in range(2):
            first = side * three
            q_ref[2 * pair + side] = (total[:, first : first + LANES] * (HDIM**-0.5)).astype(bf16)
            k_ref[2 * pair + side] = total[:, first + LANES : first + 2 * LANES].astype(bf16)
            v_ref[2 * pair + side] = total[:, first + 2 * LANES : first + three].astype(bf16)


def attend_kernel(shards, len_ref, q_ref, k_ref, v_ref, lse_ref, ctx_ref):
    slots = q_ref.shape[1]
    count = len_ref[0]
    block = slots // 2
    keep = iota((slots, block), 0) < count

    def one_pair(j, carry):
        k_sides = halves(k_ref[j])
        v_flip = flip(v_ref[j]).astype(bf16)
        for first in range(0, slots, block):
            q = q_ref[j, first : first + block, :]
            parts = []
            for side in range(2):
                s = jnp.where(keep, mm_last(k_sides[side], q), -1e30)
                top = jnp.max(s, 0, keepdims=True)
                e = jnp.exp(s - top)
                total = jnp.sum(e, 0, keepdims=True)
                prob = (e * (1.0 / total)).astype(bf16)
                lse_ref[j, side : side + 1, first : first + block] = top + jnp.log(total)
                parts.append(mm(v_flip[side * HDIM : (side + 1) * HDIM, :], prob))
            both = jnp.concatenate(parts, 0).T
            ctx_ref[first : first + block, pl.ds(pl.multiple_of(j * LANES, LANES), LANES)] = (
                both.astype(bf16)
            )
        return carry

    lax.fori_loop(0, shards, one_pair, 0)


def gelu_parts(x):
    z = jnp.abs(x) * (0.5**0.5)
    t = 1.0 / (1.0 + 0.3275911 * z)
    poly = t * (
        0.254829592
        + t * (-0.284496736 + t * (1.421413741 + t * (-1.453152027 + t * 1.061405429)))
    )
    bell = jnp.exp(-0.5 * x * x)
    tail = 0.5 * poly * bell
    cdf = jnp.where(x < 0.0, tail, 1.0 - tail)
    return x * cdf, cdf + x * bell * 0.3989422804014327


def middle_kernel(
    shards, len_ref, label_ref, x_ref, ctx_ref, gain_ref, bias_ref, class_ref, w_ref,
    dctx_ref, loss_ref,
    wo_buf, wi_buf, wf_buf, slope_buf, acc_ref, h_ref, hb_ref, hat_ref, df_ref, sems,
):
    slots, width = x_ref.shape
    classes = class_ref.shape[0]
    units = wi_buf.shape[-1]
    in_rows, out_rows, att_rows = rows_of(shards, width)
    start = in_rows + 2 * out_rows
    copies = []
    for shard in range(shards):
        mine = [
            pltpu.make_async_copy(w_ref.at[shard, :, pl.ds(0, in_rows), :], wi_buf.at[shard], sems.at[shard, 0])
        ]
        for side in range(2):
            cols = pl.ds(side * units, units)
            mine.append(
                pltpu.make_async_copy(
                    w_ref.at[shard, :, pl.ds(in_rows + side * out_rows, out_rows), :],
                    wf_buf.at[shard, :, :, cols],
                    sems.at[shard, 1 + side],
                )
            )
        copies.append(mine)
    wo_copies = []
    for place in range(GROUPS):
        wo_copies.append(
            pltpu.make_async_copy(
                w_ref.at[:, place, pl.ds(start, att_rows), :],
                wo_buf.at[:, place // 2, :, pl.ds(place % 2 * units, units)],
                sems.at[place % shards, 3 + place // shards],
            )
        )
    for one in wo_copies:
        one.start()
    for mine in copies:
        for one in mine:
            one.start()
    count = len_ref[0]
    count_f = count.astype(f32)
    label = label_ref[0]
    for one in wo_copies:
        one.wait()
    hat1, std1 = normalize(x_ref[...] + mm(ctx_ref[...], wo_buf[...].reshape(width, width)))
    hat_ref[...] = hat1
    h1 = hat1 * gain_ref[1:2, :] + bias_ref[1:2, :]
    h_ref[...] = h1
    hb_ref[...] = h1.astype(bf16)
    for f in range(shards):
        for one in copies[f]:
            one.wait()
        g, slope = gelu_parts(mm(hb_ref[...], wi_buf[f].reshape(width, units)))
        slope_buf[f] = slope
        part = mm(g.astype(bf16), wf_buf[f].reshape(units, width))
        if f == 0:
            acc_ref[...] = part
        else:
            acc_ref[...] += part
    hat2, std2 = normalize(h_ref[...] + acc_ref[...])
    gain2 = gain_ref[2:3, :]
    valid = (iota((slots, 1), 0) < count).astype(f32)
    pooled = jnp.sum((hat2 * gain2 + bias_ref[2:3, :]) * valid, 0, keepdims=True) / count_f
    weights = class_ref[...].astype(f32)
    logits = jnp.sum(pooled.astype(bf16).astype(f32) * weights, 1, keepdims=True)
    shifted = logits - jnp.max(logits, 0, keepdims=True)
    log_prob = shifted - jnp.log(jnp.sum(jnp.exp(shifted), 0, keepdims=True))
    target = (1.0 - smooth_rate) * (iota((classes, 1), 0) == label).astype(f32) + smooth_rate / classes
    loss_ref[...] = jnp.broadcast_to(-jnp.sum(target * log_prob, 0, keepdims=True), loss_ref.shape)
    d_pooled = jnp.sum((jnp.exp(log_prob) - target) * weights, 0, keepdims=True) / count_f
    d_two = norm_back((d_pooled * gain2) * valid, hat2, std2)
    acc_ref[...] = d_two
    df_ref[...] = d_two.astype(bf16)
    for f in range(shards):
        d_pre = (mm_last(df_ref[...], wf_buf[f].reshape(units, width)) * slope_buf[f]).astype(bf16)
        acc_ref[...] += mm_last(d_pre, wi_buf[f].reshape(width, units))
    d_attn = norm_back(acc_ref[...] * gain_ref[1:2, :], hat_ref[...], std1).astype(bf16)
    dctx_ref[...] = mm_last(d_attn, wo_buf[...].reshape(width, width)).astype(bf16)


def gradient_kernel(
    shards, groups, len_ref, xb_ref, xa_ref, q_ref, k_ref, v_ref, lse_ref, dctx_ref, w_ref,
    send_ref, norm_ref,
    up_buf, up_grad, inner_ref, sems,
):
    slots, width = xb_ref.shape
    rank2 = xa_ref.shape[1]
    rank = rank2 // 2
    in_rows, out_rows, att_rows = rows_of(shards, width)
    copies = [
        pltpu.make_async_copy(
            w_ref.at[j, 0, pl.ds(in_rows + 2 * out_rows + att_rows, rank2), pl.ds(3 * LANES, LANES)],
            up_buf.at[j],
            sems.at[j],
        )
        for j in range(shards)
    ]
    for one in copies:
        one.start()
    for one in copies:
        one.wait()
    count = len_ref[0]
    block = slots // 2
    keep = iota((slots, block), 0) < count
    xa = xa_ref[...]
    low = iota((LANES, rank2), 1) < rank
    inner_ref[...] = jnp.zeros_like(inner_ref)

    def one_pair(j, carry):
        k = k_ref[j]
        k_sides = halves(k)
        v_sides = halves(v_ref[j])
        k_flip = flip(k).astype(bf16)
        dv = jnp.zeros((slots, LANES), f32)
        flips = []
        for first in range(0, slots, block):
            q = q_ref[j, first : first + block, :]
            dctx = dctx_ref[first : first + block, pl.ds(pl.multiple_of(j * LANES, LANES), LANES)]
            dctx_sides = halves(dctx)
            parts = []
            for side in range(2):
                s = jnp.where(keep, mm_last(k_sides[side], q), -1e30)
                prob = jnp.exp(s - lse_ref[j, side : side + 1, first : first + block])
                d_prob = mm_last(v_sides[side], dctx)
                weighted = jnp.sum(prob * d_prob, 0, keepdims=True)
                d_s = (prob * (d_prob - weighted)).astype(bf16)
                dv = dv + mm(prob.astype(bf16), dctx_sides[side])
                parts.append(mm(k_flip[side * HDIM : (side + 1) * HDIM, :], d_s))
            flips.append(jnp.concatenate(parts, 0))
        dq_flip = (jnp.concatenate(flips, 1) * (HDIM**-0.5)).astype(bf16)
        dv_flip = flip(dv.astype(bf16)).astype(bf16)
        up_grad[pl.ds(pl.multiple_of(j * LANES, LANES), LANES), :] = adapter_scale * jnp.where(
            low, mm(dq_flip, xa), mm(dv_flip, xa)
        )
        inner_ref[0:rank, :] += adapter_scale * mm(up_buf[j, 0:rank, :], dq_flip)
        inner_ref[rank:rank2, :] += adapter_scale * mm(up_buf[j, rank:rank2, :], dv_flip)
        return carry

    lax.fori_loop(0, shards, one_pair, 0)
    down_grad = mm(inner_ref[...].astype(bf16), xb_ref[...]).T
    both = jnp.concatenate([up_grad[...], down_grad], 1)
    squares = jnp.sum(jnp.sum(both * both, 1, keepdims=True), 0, keepdims=True)
    norm = jnp.sqrt(squares)
    norm_ref[...] = jnp.broadcast_to(norm, norm_ref.shape)
    both = both * (clip_bound / jnp.maximum(norm, clip_bound))
    rows = width // (groups * shards)
    send_ref[...] = jnp.zeros_like(send_ref)
    for i in range(groups):
        for j in range(shards):
            to = i * shards + j
            at_up = (j * groups + i) * rows
            at_down = to * rows
            send_ref[to, :, 0:rank2] = both[at_up : at_up + rows, 0:rank2]
            send_ref[to, :, rank2 : 2 * rank2] = both[at_down : at_down + rows, rank2:]


def lamb(weight, grad, first, second, fix_one, fix_two):
    first_new = beta_one * first + (1.0 - beta_one) * grad
    second_new = beta_two * second + (1.0 - beta_two) * grad * grad
    direction = first_new / fix_one / (jnp.sqrt(second_new / fix_two) + adam_eps) + decay_rate * weight
    return first_new, second_new, direction


def side_by_side(ref):
    return jnp.concatenate([ref[0], ref[1]], 1)


def flipped(ref):
    maps, rank, cols = ref.shape
    return ref[...].reshape(maps * rank, cols).T


def direction_kernel(
    examples, sc_ref, fix_ref, got_ref, loss_ref, down_ref, up_ref, dm1_ref, dm2_ref, um1_ref, um2_ref,
    dn_ref, un_ref,
    tile_ref, um1_out, um2_out, dir_ref, w_out, up_turn, down_turn, part_turn,
):
    dp_at, head_at = sc_ref[0], sc_ref[1]
    rows = got_ref.shape[1]
    rank2 = up_turn.shape[1]
    up_at = pl.multiple_of(dp_at * rows, rows)
    at = pl.multiple_of(head_at * rows, rows)
    down_at = pl.multiple_of(dp_at * dm1_ref.shape[2] + head_at * rows, rows)
    up_turn[...] = flipped(up_ref)
    down_turn[...] = flipped(down_ref)
    for n, ref in enumerate((dn_ref, dm1_ref, dm2_ref)):
        part_turn[n] = flipped(ref)
    here = pl.ds(at, rows)
    weight = jnp.concatenate([up_turn[pl.ds(up_at, rows), :], down_turn[pl.ds(down_at, rows), :]], 1)
    noise = jnp.concatenate([side_by_side(un_ref), part_turn[0, here, :]], 1)
    first = jnp.concatenate([side_by_side(um1_ref), part_turn[1, here, :]], 1)
    second = jnp.concatenate([side_by_side(um2_ref), part_turn[2, here, :]], 1)
    total = jnp.sum(got_ref[...], 0)[:, : 2 * rank2]
    grad = (total + noise_mult * clip_bound * noise) / examples
    first_new, second_new, direction = lamb(weight, grad, first, second, fix_ref[0], fix_ref[1])
    um1_out[...] = first_new
    um2_out[...] = second_new
    dir_ref[...] = direction
    w_out[...] = weight
    down_grad = grad[:, rank2:]
    per_line = LANES // rank2
    lines = [
        jnp.concatenate([down_grad[k : k + 1] for k in range(line, line + per_line)], 1)
        for line in range(0, rows, per_line)
    ]
    lines.append(
        jnp.concatenate(
            [jnp.sum(direction * direction, 0, keepdims=True), jnp.sum(weight * weight, 0, keepdims=True)], 1
        )
    )
    lines.append(loss_ref[...])
    tile = jnp.concatenate(lines, 0)
    for to in range(tile_ref.shape[0]):
        tile_ref[to] = tile


def update_kernel(
    examples, shards, sc_ref, fix_ref, got_ref, down_ref, dm1_ref, dm2_ref, um1_ref, um2_ref, dir_ref, w_ref,
    loss_ref, dm1_out, dm2_out, dw_out, um1_out, um2_out, uw_out, table_ref, down_turn,
):
    dp_at = sc_ref[0]
    rows = w_ref.shape[0]
    rank2 = w_ref.shape[1] // 2
    rank = rank2 // 2
    per_line = LANES // rank2
    lines = rows // per_line
    total = jnp.sum(got_ref[...], 0)
    loss_ref[...] = total[lines + 1 : lines + 2, 0:1] / examples
    stats = total[lines : lines + 1, :]
    lane = iota(stats.shape, 1)

    def part(group):
        inside = (lane >= group * rank) & (lane < (group + 1) * rank)
        return jnp.sqrt(jnp.sum(jnp.where(inside, stats, 0.0), 1, keepdims=True))

    norms = [(part(group + 4), part(group)) for group in range(4)]
    for out_col, group in enumerate((2, 3, 0, 1)):
        table_ref[:, out_col : out_col + 1] = jnp.concatenate(norms[group], 0)

    def rate(a, b):
        wide = iota((1, rank2), 1) < rank
        return learn_rate * jnp.where(wide, norms[a][0] / norms[a][1], norms[b][0] / norms[b][1])

    up_new = w_ref[:, :rank2] - rate(0, 1) * dir_ref[:, :rank2]
    for ref, value in ((uw_out, up_new), (um1_out, um1_ref[...]), (um2_out, um2_ref[...])):
        ref[0] = value[:, :rank]
        ref[1] = value[:, rank:rank2]
    grad = jnp.concatenate(
        [
            got_ref[dp_at * shards + j, k // per_line, (k % per_line) * rank2 : (k % per_line + 1) * rank2]
            .reshape(1, rank2)
            for j in range(shards)
            for k in range(rows)
        ],
        0,
    )
    many = dm1_ref.shape[2]
    down_turn[...] = flipped(down_ref)
    weight = down_turn[pl.ds(pl.multiple_of(dp_at * many, many), many), :]
    first_new, second_new, direction = lamb(
        weight, grad, flipped(dm1_ref), flipped(dm2_ref), fix_ref[0], fix_ref[1]
    )
    new = weight - rate(2, 3) * direction
    for ref, value in ((dm1_out, first_new), (dm2_out, second_new), (dw_out, new)):
        ref[...] = value.T.reshape(ref.shape)


def per_device(
    slot_token_ids,
    lengths,
    labels,
    optimizer_step_count,
    token_embedding_table,
    positions,
    query_key_value_weight,
    attention_output_weight,
    feedforward_input_weight,
    feedforward_output_weight,
    layer_norm_gains,
    layer_norm_biases,
    classifier,
    adapter_down_maps,
    adapter_up_maps,
    down_first_moment,
    down_second_moment,
    up_first_moment,
    up_second_moment,
    down_privacy_noise,
    up_privacy_noise,
):
    shards = lax.axis_size("head")
    groups = lax.axis_size("dp")
    devices = shards * groups
    dp_at = lax.axis_index("dp")
    head_at = lax.axis_index("head")
    slots, width = positions.shape
    rank = adapter_down_maps.shape[2]
    rank2 = 2 * rank
    units = feedforward_output_weight.shape[0]
    local_w = attention_output_weight.shape[0]
    owned = token_embedding_table.shape[0]
    shape = jax.ShapeDtypeStruct

    def turned(x):
        return jnp.swapaxes(x, 1, 2)

    down_maps = turned(adapter_down_maps)

    def ask(which, slot_token_ids):
        return call(
            functools.partial(request_kernel, groups, shards, owned),
            (shape((devices, 1, LANES), i32), shape((slots, LANES), i32)),
            [SM, SM, VM],
            (VM, VM),
        )(jnp.stack([head_at, which]).astype(i32), lengths, slot_token_ids)

    def look(wanted):
        return call(
            lookup_kernel,
            shape((devices, CAP, LANES), bf16),
            [SM, VM],
            VM,
            [pltpu.VMEM((owned, LANES), f32), pltpu.VMEM((CAP, LANES), f32)],
        )(wanted, token_embedding_table)

    def place(found, slot):
        got = exchange(found)
        emb = call(
            functools.partial(assemble_kernel, groups, shards),
            shape((slots, width), bf16),
            [VM, VM],
            VM,
            [pltpu.VMEM((groups * CAP, width), bf16)],
        )(got, slot)
        return emb

    def exchange(x):
        return lax.all_to_all(x, ALL, 0, 0, tiled=True)

    pack = call(
        pack_kernel,
        shape((width // GROUPS * 3 + 2 * width // shards // GROUPS, units), bf16),
        [SM, ANY, VM, ANY, ANY, ANY],
        VM,
        [pltpu.SemaphoreType.DMA((7,))],
        vmem=60,
    )(
        dp_at.reshape(1).astype(i32),
        query_key_value_weight,
        adapter_up_maps.reshape(rank2, local_w),
        feedforward_input_weight,
        feedforward_output_weight,
        attention_output_weight,
    )
    pack, slot_token_ids = lax.optimization_barrier((pack, slot_token_ids))
    weights = lax.all_gather(pack, ("head", "dp"), axis=0, tiled=True).reshape(shards, groups, *pack.shape)

    requests, slot = ask(jnp.zeros((), i32), slot_token_ids)

    wanted = exchange(requests)
    rounds = jnp.max(wanted[:, 0, LANES - 1])
    found = look(wanted)
    emb = place(found, slot)

    def again(which):
        asked, where = ask(which, slot_token_ids)
        return place(look(exchange(asked)), where)

    unused_at, emb = lax.while_loop(
        lambda state: state[0] < rounds,
        lambda state: (state[0] + 1, state[1] + again(state[0])),
        (jnp.ones((), i32), emb),
    )

    own_len = lax.dynamic_slice_in_dim(lengths, head_at, 1)
    own_label = lax.dynamic_slice_in_dim(labels, head_at, 1)
    x0, x0b, xa, q, k, v = call(
        functools.partial(project_kernel, shards),
        (
            shape((slots, width), f32),
            shape((slots, width), bf16),
            shape((slots, rank2), bf16),
            shape((shards, slots, LANES), bf16),
            shape((shards, slots, LANES), bf16),
            shape((shards, slots, LANES), bf16),
        ),
        [VM, VM, VM, VM, VM, ANY],
        (VM,) * 6,
        [
            pltpu.VMEM((shards // 2, groups, width // groups, 6 * LANES), bf16),
            pltpu.VMEM((shards // 2, rank2, 6 * LANES), bf16),
            pltpu.SemaphoreType.DMA((shards, 3)),
        ],
        vmem=50,
    )(emb, positions, layer_norm_gains, layer_norm_biases, down_maps, weights)
    lse, ctx = call(
        functools.partial(attend_kernel, shards),
        (shape((shards, 2, slots), f32), shape((slots, width), bf16)),
        [SM, VM, VM, VM],
        (VM, VM),
        vmem=40,
    )(own_len, q, k, v)

    dctx, loss = call(
        functools.partial(middle_kernel, shards),
        (shape((slots, width), bf16), shape((1, LANES), f32)),
        [SM, SM, VM, VM, VM, VM, VM, ANY],
        (VM, VM),
        [
            pltpu.VMEM((shards, groups // 2, 2 * local_w // groups, width), bf16),
            pltpu.VMEM((shards, groups, width // groups, units), bf16),
            pltpu.VMEM((shards, groups, units // groups, width), bf16),
            pltpu.VMEM((shards, slots, units), f32),
            pltpu.VMEM((slots, width), f32),
            pltpu.VMEM((slots, width), f32),
            pltpu.VMEM((slots, width), bf16),
            pltpu.VMEM((slots, width), f32),
            pltpu.VMEM((slots, width), bf16),
            pltpu.SemaphoreType.DMA((shards, 5)),
        ],
        vmem=60,
    )(
        own_len, own_label, x0, ctx, layer_norm_gains, layer_norm_biases, classifier, weights
    )

    send, norm = call(
        functools.partial(gradient_kernel, shards, groups),
        (shape((devices, width // devices, LANES), f32), shape((1, LANES), f32)),
        [SM, VM, VM, VM, VM, VM, VM, VM, ANY],
        (VM, VM),
        [
            pltpu.VMEM((shards, rank2, LANES), bf16),
            pltpu.VMEM((width, rank2), f32),
            pltpu.VMEM((rank2, slots), f32),
            pltpu.SemaphoreType.DMA((shards,)),
        ],
        vmem=50,
    )(own_len, x0b, xa, q, k, v, lse, dctx, weights)

    got = exchange(send)
    examples = float(devices)
    step_number = optimizer_step_count.astype(f32)
    fixes = jnp.stack([1.0 - jnp.power(beta_one, step_number), 1.0 - jnp.power(beta_two, step_number)])
    where = jnp.stack([dp_at, head_at]).astype(i32)
    rows = width // devices
    small = shape((rows, 2 * rank2), f32)
    moments = [turned(x) for x in (down_first_moment, down_second_moment, up_first_moment, up_second_moment)]
    lines = rows * rank2 // LANES + 2
    tile, um1, um2, direction, weight = call(
        functools.partial(direction_kernel, examples),
        (shape((devices, lines, LANES), f32), small, small, small, small),
        [SM, SM] + [VM] * 10,
        (VM,) * 5,
        [
            pltpu.VMEM((local_w, rank2), f32),
            pltpu.VMEM((width, rank2), f32),
            pltpu.VMEM((3, width // groups, rank2), f32),
        ],
    )(
        where, fixes, got, loss, down_maps, adapter_up_maps, *moments,
        turned(down_privacy_noise), turned(up_privacy_noise),
    )
    spread = exchange(tile)
    down_shape = shape(moments[0].shape, f32)
    up_shape = shape(moments[2].shape, f32)
    loss_mean, dm1, dm2, dw, bm1, bm2, bw, table = call(
        functools.partial(update_kernel, examples, shards),
        (
            shape((1, 1), f32), down_shape, down_shape, down_shape, up_shape, up_shape, up_shape,
            shape((2, 4), f32),
        ),
        [SM, SM] + [VM] * 8,
        (VM,) * 8,
        [pltpu.VMEM((width, rank2), f32)],
    )(where, fixes, spread, down_maps, moments[0], moments[1], um1, um2, direction, weight)
    return (
        loss_mean.reshape(()),
        norm[0, 0:1],
        turned(dm1),
        turned(dm2),
        turned(dw),
        turned(bm1),
        turned(bm2),
        turned(bw),
        table.T,
    )


def solution(mesh):
    placed = (
        P("dp", None),
        P("dp"),
        P("dp"),
        P(),
        P("dp", "head"),
        P(),
        P(None, None, "head"),
        P("head", None),
        P(None, "head"),
        P("head", None),
        P(),
        P(),
        P(),
        P(),
        P(None, None, "head"),
        P(None, "dp", None),
        P(None, "dp", None),
        P(None, None, ("head", "dp")),
        P(None, None, ("head", "dp")),
        P(None, "dp", None),
        P(None, None, ("head", "dp")),
    )
    return jax.shard_map(
        per_device,
        mesh=mesh,
        in_specs=placed,
        out_specs=(
            P(),
            P(("dp", "head")),
            P(None, "dp", None),
            P(None, "dp", None),
            P(None, "dp", None),
            P(None, None, ("head", "dp")),
            P(None, None, ("head", "dp")),
            P(None, None, ("head", "dp")),
            P(),
        ),
        check_vma=False,
    )
```

```python
import functools

import jax
import jax.numpy as jnp
from jax import lax
from jax.experimental import pallas as pl
from jax.experimental.pallas import tpu as pltpu
from jax.sharding import PartitionSpec as P

HDIM = 64
CAP = 48
GROUPS = 16
LANES = 128
MIB = 1 << 20

adapter_scale = 2.0
clip_bound = 1.0
noise_mult = 0.6
smooth_rate = 0.1
beta_one = 0.9
beta_two = 0.999
adam_eps = 1e-06
decay_rate = 0.01
learn_rate = 0.25
norm_eps = 1e-05

f32 = jnp.float32
bf16 = jnp.bfloat16
i32 = jnp.int32
LAST = (((1,), (1,)), ((), ()))
ALL = ("dp", "head")
VM = pl.BlockSpec(memory_space=pltpu.VMEM)
SM = pl.BlockSpec(memory_space=pltpu.SMEM)
ANY = pl.BlockSpec(memory_space=pl.ANY)


def iota(shape, axis):
    return lax.broadcasted_iota(i32, shape, axis)


def mm(a, b):
    return jnp.dot(a, b, preferred_element_type=f32)


def mm_last(a, b):
    return lax.dot_general(a, b, LAST, preferred_element_type=f32)


def call(kernel, outs, in_specs, out_specs, scratch=(), vmem=32, flops=1):
    return pl.pallas_call(
        kernel,
        out_shape=outs,
        in_specs=in_specs,
        out_specs=out_specs,
        scratch_shapes=list(scratch),
        compiler_params=pltpu.CompilerParams(vmem_limit_bytes=vmem * MIB),
        cost_estimate=pl.CostEstimate(flops=flops, bytes_accessed=1, transcendentals=0),
    )


def request_kernel(owners, peers, owned, sc_ref, len_ref, ids_ref, req_ref, slot_ref):
    me = sc_ref[0]
    base = (sc_ref[1] * CAP).astype(f32)
    count = len_ref[me]
    ids = ids_ref[...].astype(f32)
    examples, slots = ids.shape
    row = jnp.sum(jnp.where(iota(ids.shape, 0) == me, ids, 0.0), 0, keepdims=True)
    flipped = ids.T
    col = jnp.sum(jnp.where(iota(flipped.shape, 1) == me, flipped, 0.0), 1, keepdims=True)
    t_col = iota((slots, slots), 0)
    t_row = iota((slots, slots), 1)
    valid_col = (iota((slots, 1), 0) < count).astype(f32)
    valid_row = (iota((1, slots), 1) < count).astype(f32)
    own_col = sum((col >= k * owned).astype(f32) for k in range(1, owners))
    own_row = sum((row >= k * owned).astype(f32) for k in range(1, owners))
    same = (col == row) & (t_row < count) & (t_col < count)
    before = t_row < t_col
    after = t_col < t_row
    seen_col = jnp.sum(jnp.where(same & before, 1.0, 0.0), 1, keepdims=True)
    seen_row = jnp.sum(jnp.where(same & after, 1.0, 0.0), 0, keepdims=True)
    first_col = jnp.where(seen_col == 0.0, valid_col, 0.0)
    first_row = jnp.where(seen_row == 0.0, valid_row, 0.0)
    shared = own_col == own_row
    place_col = jnp.sum(jnp.where(shared & before, first_row, 0.0), 1, keepdims=True)
    place_row = jnp.sum(jnp.where(shared & after, first_col, 0.0), 0, keepdims=True)
    rank = jnp.sum(jnp.where(same, first_row * place_row, 0.0), 1, keepdims=True)
    local = rank - base
    here = (local >= 0.0) & (local < CAP) & (valid_col > 0.0)
    slot = jnp.where(here, own_col * CAP + local, -1.0)
    slot_ref[...] = jnp.broadcast_to(slot, slot_ref.shape).astype(i32)
    rounds = jnp.floor(jnp.max(rank, 0, keepdims=True) * (1.0 / CAP) + 0.5 / CAP) + 1.0
    lane = iota((slots, LANES), 1)
    lane_f = lane.astype(f32)
    wanted = jnp.where(first_col > 0.0, place_col - base, -1.0)
    hit = (wanted == lane_f) & (lane < CAP)
    lane_row = iota((1, LANES), 1)
    for owner in range(owners):
        chosen = jnp.where(hit & (own_col == float(owner)), col - float(owner * owned), 0.0)
        line = jnp.sum(chosen, 0, keepdims=True)
        line = jnp.where(lane_row == LANES - 1, rounds, line).astype(i32)
        for peer in range(peers):
            req_ref[owner * peers + peer] = line


def lookup_kernel(want_ref, table_ref, out_ref, wide_ref, stage_ref):
    wide_ref[...] = table_ref[...].astype(f32)

    def one(src, carry):
        for p in range(CAP):
            stage_ref[p : p + 1, :] = wide_ref[pl.ds(want_ref[src, 0, p], 1), :]
        out_ref[src] = stage_ref[...].astype(bf16)
        return carry

    lax.fori_loop(0, want_ref.shape[0], one, 0)


def assemble_kernel(owners, peers, got_ref, slot_ref, emb_ref, rows_ref):
    for owner in range(owners):
        for peer in range(peers):
            rows_ref[owner * CAP : (owner + 1) * CAP, peer * LANES : (peer + 1) * LANES] = got_ref[
                owner * peers + peer
            ]
    slot = slot_ref[...]
    lane = iota(slot.shape, 1)
    picks = [
        (slot == lane + first).astype(f32).astype(bf16)
        for first in range(0, owners * CAP, LANES)
    ]
    emb_ref[...] = mm(jnp.concatenate(picks, 1), rows_ref[...]).astype(bf16)


def pack_kernel(at_ref, in_ref, out_ref, att_ref, pack_ref, sems):
    at = at_ref[0]
    wide = in_ref.shape[1]
    in_rows, out_rows = in_ref.shape[0] // GROUPS, out_ref.shape[0] // GROUPS
    att_rows = 2 * att_ref.shape[0] // GROUPS
    here = lambda rows: pl.ds(pl.multiple_of(at * rows, rows), rows)
    moves = [(in_ref.at[here(in_rows), :], pack_ref.at[pl.ds(0, in_rows), :])]
    row = in_rows
    for first in range(0, 2 * wide, wide):
        moves.append((out_ref.at[here(out_rows), pl.ds(first, wide)], pack_ref.at[pl.ds(row, out_rows), :]))
        row += out_rows
    half = att_ref.at[
        pl.ds(pl.multiple_of(at // 2 * att_rows, att_rows), att_rows),
        pl.ds(pl.multiple_of(at % 2 * wide, wide), wide),
    ]
    moves.append((half, pack_ref.at[pl.ds(row, att_rows), :]))
    copies = [pltpu.make_async_copy(source, target, sems.at[n]) for n, (source, target) in enumerate(moves)]
    for one in copies:
        one.start()
    for one in copies:
        one.wait()


def normalize(inputs):
    centre = inputs - jnp.mean(inputs, -1, keepdims=True)
    inv_std = lax.rsqrt(jnp.mean(centre * centre, -1, keepdims=True) + norm_eps)
    return centre * inv_std, inv_std


def norm_back(scaled, x_hat, inv_std):
    return inv_std * (
        scaled
        - jnp.mean(scaled, -1, keepdims=True)
        - x_hat * jnp.mean(scaled * x_hat, -1, keepdims=True)
    )


def halves(pair):
    low = iota(pair.shape, 1) < HDIM
    zero = jnp.zeros_like(pair)
    return jnp.where(low, pair, zero), jnp.where(low, zero, pair)


def flip(x):
    return x.astype(f32).T


def rows_of(shards, width):
    in_rows = width // GROUPS
    return in_rows, in_rows // 2, 2 * width // shards // GROUPS


def project_kernel(
    shards, emb_ref, pos_ref, gain_ref, bias_ref, down_ref, w_own, w_peer,
    x_ref, xb_ref, xa_ref, q_ref, k_ref, v_ref,
    w_buf, up_buf, sems,
):
    slots, width = emb_ref.shape
    rank = down_ref.shape[1]
    rank2 = 2 * rank
    three = 3 * LANES
    copies = []
    up_buf[...] = jnp.zeros_like(up_buf)
    for pair in range(shards // 2):
        mine = []
        for side, w_ref in enumerate((w_own, w_peer)):
            for part in range(3):
                mine.append(
                    pltpu.make_async_copy(
                        w_ref.at[pair, pl.ds(part * width, width), :],
                        w_buf.at[pair, :, pl.ds(side * three + part * LANES, LANES)],
                        sems.at[pair, side * 5 + part],
                    )
                )
            for part in range(2):
                mine.append(
                    pltpu.make_async_copy(
                        w_ref.at[pair, pl.ds(3 * width + part * rank, rank), :],
                        up_buf.at[pair, pl.ds(part * rank, rank), pl.ds(side * three + 2 * part * LANES, LANES)],
                        sems.at[pair, side * 5 + 3 + part],
                    )
                )
        copies.append(mine)
    for mine in copies:
        for one in mine:
            one.start()
    x_hat, unused_std = normalize(emb_ref[...].astype(f32) + pos_ref[...].astype(f32))
    x0 = x_hat * gain_ref[0:1, :] + bias_ref[0:1, :]
    x_ref[...] = x0
    xb_ref[...] = x0.astype(bf16)
    xa = mm_last(xb_ref[...], down_ref[...].reshape(rank2, width).astype(bf16)).astype(bf16)
    xa_ref[...] = xa
    twice = xa * jnp.asarray(adapter_scale, bf16)
    for pair in range(shards // 2):
        for one in copies[pair]:
            one.wait()
        total = mm(xb_ref[...], w_buf[pair]) + mm(twice, up_buf[pair])
        for side in range(2):
            first = side * three
            q_ref[2 * pair + side] = (total[:, first : first + LANES] * (HDIM**-0.5)).astype(bf16)
            k_ref[2 * pair + side] = total[:, first + LANES : first + 2 * LANES].astype(bf16)
            v_ref[2 * pair + side] = total[:, first + 2 * LANES : first + three].astype(bf16)


def attend_kernel(shards, len_ref, order_ref, q_ref, k_ref, v_ref, lse_ref, ctx_ref):
    slots = q_ref.shape[1]
    count = len_ref[0]
    block = slots // 2
    keep = iota((slots, block), 0) < count

    def one_pair(j, carry):
        k_sides = halves(k_ref[j])
        v_flip = flip(v_ref[j]).astype(bf16)
        for first in range(0, slots, block):
            q = q_ref[j, first : first + block, :]
            parts = []
            for side in range(2):
                s = jnp.where(keep, mm_last(k_sides[side], q), -1e30)
                top = jnp.max(s, 0, keepdims=True)
                e = jnp.exp(s - top)
                total = jnp.sum(e, 0, keepdims=True)
                prob = (e * (1.0 / total)).astype(bf16)
                lse_ref[j, side : side + 1, first : first + block] = top + jnp.log(total)
                parts.append(mm(v_flip[side * HDIM : (side + 1) * HDIM, :], prob))
            both = jnp.concatenate(parts, 0).T
            ctx_ref[first : first + block, pl.ds(pl.multiple_of(order_ref[j] * LANES, LANES), LANES)] = (
                both.astype(bf16)
            )
        return carry

    lax.fori_loop(0, shards, one_pair, 0)


def gelu_parts(x):
    z = jnp.abs(x) * (0.5**0.5)
    t = 1.0 / (1.0 + 0.3275911 * z)
    poly = t * (
        0.254829592
        + t * (-0.284496736 + t * (1.421413741 + t * (-1.453152027 + t * 1.061405429)))
    )
    bell = jnp.exp(-0.5 * x * x)
    tail = 0.5 * poly * bell
    cdf = jnp.where(x < 0.0, tail, 1.0 - tail)
    return x * cdf, cdf + x * bell * 0.3989422804014327


def middle_kernel(
    shards, len_ref, label_ref, x_ref, ctx_ref, gain_ref, bias_ref, class_ref, w_ref,
    dctx_ref, loss_ref,
    wo_buf, wi_buf, wf_buf, slope_buf, acc_ref, h_ref, hb_ref, hat_ref, df_ref, sems,
):
    slots, width = x_ref.shape
    classes = class_ref.shape[0]
    units = wi_buf.shape[-1]
    in_rows, out_rows, att_rows = rows_of(shards, width)
    start = in_rows + 2 * out_rows
    copies = []
    for shard in range(shards):
        mine = [
            pltpu.make_async_copy(w_ref.at[shard, :, pl.ds(0, in_rows), :], wi_buf.at[shard], sems.at[shard, 0])
        ]
        for side in range(2):
            cols = pl.ds(side * units, units)
            mine.append(
                pltpu.make_async_copy(
                    w_ref.at[shard, :, pl.ds(in_rows + side * out_rows, out_rows), :],
                    wf_buf.at[shard, :, :, cols],
                    sems.at[shard, 1 + side],
                )
            )
        copies.append(mine)
    wo_copies = []
    for place in range(GROUPS):
        wo_copies.append(
            pltpu.make_async_copy(
                w_ref.at[:, place, pl.ds(start, att_rows), :],
                wo_buf.at[:, place // 2, :, pl.ds(place % 2 * units, units)],
                sems.at[place % shards, 3 + place // shards],
            )
        )
    for one in wo_copies:
        one.start()
    for mine in copies:
        for one in mine:
            one.start()
    count = len_ref[0]
    count_f = count.astype(f32)
    label = label_ref[0]
    for one in wo_copies:
        one.wait()
    hat1, std1 = normalize(x_ref[...] + mm(ctx_ref[...], wo_buf[...].reshape(width, width)))
    hat_ref[...] = hat1
    h1 = hat1 * gain_ref[1:2, :] + bias_ref[1:2, :]
    h_ref[...] = h1
    hb_ref[...] = h1.astype(bf16)
    for f in range(shards):
        for one in copies[f]:
            one.wait()
        g, slope = gelu_parts(mm(hb_ref[...], wi_buf[f].reshape(width, units)))
        slope_buf[f] = slope
        part = mm(g.astype(bf16), wf_buf[f].reshape(units, width))
        if f == 0:
            acc_ref[...] = part
        else:
            acc_ref[...] += part
    hat2, std2 = normalize(h_ref[...] + acc_ref[...])
    gain2 = gain_ref[2:3, :]
    valid = (iota((slots, 1), 0) < count).astype(f32)
    pooled = jnp.sum((hat2 * gain2 + bias_ref[2:3, :]) * valid, 0, keepdims=True) / count_f
    weights = class_ref[...].astype(f32)
    logits = jnp.sum(pooled.astype(bf16).astype(f32) * weights, 1, keepdims=True)
    shifted = logits - jnp.max(logits, 0, keepdims=True)
    log_prob = shifted - jnp.log(jnp.sum(jnp.exp(shifted), 0, keepdims=True))
    target = (1.0 - smooth_rate) * (iota((classes, 1), 0) == label).astype(f32) + smooth_rate / classes
    loss_ref[...] = jnp.broadcast_to(-jnp.sum(target * log_prob, 0, keepdims=True), loss_ref.shape)
    d_pooled = jnp.sum((jnp.exp(log_prob) - target) * weights, 0, keepdims=True) / count_f
    d_two = norm_back((d_pooled * gain2) * valid, hat2, std2)
    acc_ref[...] = d_two
    df_ref[...] = d_two.astype(bf16)
    for f in range(shards):
        d_pre = (mm_last(df_ref[...], wf_buf[f].reshape(units, width)) * slope_buf[f]).astype(bf16)
        acc_ref[...] += mm_last(d_pre, wi_buf[f].reshape(width, units))
    d_attn = norm_back(acc_ref[...] * gain_ref[1:2, :], hat_ref[...], std1).astype(bf16)
    dctx_ref[...] = mm_last(d_attn, wo_buf[...].reshape(width, width)).astype(bf16)


def gradient_kernel(
    shards, groups, len_ref, order_ref, xb_ref, xa_ref, q_ref, k_ref, v_ref, lse_ref, dctx_ref, w_own, w_peer,
    send_ref, norm_ref,
    up_buf, up_grad, inner_ref, sems,
):
    slots, width = xb_ref.shape
    rank2 = xa_ref.shape[1]
    rank = rank2 // 2
    copies = [
        pltpu.make_async_copy(
            (w_own, w_peer)[j % 2].at[j // 2, pl.ds(3 * width, rank2), :], up_buf.at[j], sems.at[j]
        )
        for j in range(shards)
    ]
    for one in copies:
        one.start()
    for one in copies:
        one.wait()
    count = len_ref[0]
    block = slots // 2
    keep = iota((slots, block), 0) < count
    xa = xa_ref[...]
    low = iota((LANES, rank2), 1) < rank
    inner_ref[...] = jnp.zeros_like(inner_ref)

    def one_pair(j, carry):
        k = k_ref[j]
        k_sides = halves(k)
        v_sides = halves(v_ref[j])
        k_flip = flip(k).astype(bf16)
        columns = pl.ds(pl.multiple_of(order_ref[j] * LANES, LANES), LANES)
        dv = jnp.zeros((slots, LANES), f32)
        flips = []
        for first in range(0, slots, block):
            q = q_ref[j, first : first + block, :]
            dctx = dctx_ref[first : first + block, columns]
            dctx_sides = halves(dctx)
            parts = []
            for side in range(2):
                s = jnp.where(keep, mm_last(k_sides[side], q), -1e30)
                prob = jnp.exp(s - lse_ref[j, side : side + 1, first : first + block])
                d_prob = mm_last(v_sides[side], dctx)
                weighted = jnp.sum(prob * d_prob, 0, keepdims=True)
                d_s = (prob * (d_prob - weighted)).astype(bf16)
                dv = dv + mm(prob.astype(bf16), dctx_sides[side])
                parts.append(mm(k_flip[side * HDIM : (side + 1) * HDIM, :], d_s))
            flips.append(jnp.concatenate(parts, 0))
        dq_flip = (jnp.concatenate(flips, 1) * (HDIM**-0.5)).astype(bf16)
        dv_flip = flip(dv.astype(bf16)).astype(bf16)
        up_grad[columns, :] = adapter_scale * jnp.where(
            low, mm(dq_flip, xa), mm(dv_flip, xa)
        )
        inner_ref[0:rank, :] += adapter_scale * mm(up_buf[j, 0:rank, :], dq_flip)
        inner_ref[rank:rank2, :] += adapter_scale * mm(up_buf[j, rank:rank2, :], dv_flip)
        return carry

    lax.fori_loop(0, shards, one_pair, 0)
    down_grad = mm(inner_ref[...].astype(bf16), xb_ref[...]).T
    both = jnp.concatenate([up_grad[...], down_grad], 1)
    squares = jnp.sum(jnp.sum(both * both, 1, keepdims=True), 0, keepdims=True)
    norm = jnp.sqrt(squares)
    norm_ref[...] = jnp.broadcast_to(norm, norm_ref.shape)
    both = both * (clip_bound / jnp.maximum(norm, clip_bound))
    rows = width // (groups * shards)
    part = rows // 2
    for i in range(groups):
        for j in range(shards):
            to = i * shards + j
            at_up = (j * groups + i) * rows
            at_down = to * rows
            for n in range(2):
                lane = 2 * rank2 * n
                send_ref[to, :, lane : lane + rank2] = both[at_up + n * part : at_up + (n + 1) * part, 0:rank2]
                send_ref[to, :, lane + rank2 : lane + 2 * rank2] = both[
                    at_down + n * part : at_down + (n + 1) * part, rank2:
                ]


def lamb(weight, grad, first, second, fix_one, fix_two):
    first_new = beta_one * first + (1.0 - beta_one) * grad
    second_new = beta_two * second + (1.0 - beta_two) * grad * grad
    direction = first_new / fix_one / (jnp.sqrt(second_new / fix_two) + adam_eps) + decay_rate * weight
    return first_new, second_new, direction


def side_by_side(ref):
    return jnp.concatenate([ref[0], ref[1]], 1)


def flipped(ref):
    maps, rank, cols = ref.shape
    return ref[...].reshape(maps * rank, cols).T


def direction_kernel(
    examples, sc_ref, fix_ref, got_ref, loss_ref, down_ref, up_ref, dm1_ref, dm2_ref, um1_ref, um2_ref,
    dn_ref, un_ref,
    tile_ref, um1_out, um2_out, dir_ref, w_out, up_turn, down_turn, part_turn,
):
    dp_at, head_at = sc_ref[0], sc_ref[1]
    rank2 = up_turn.shape[1]
    rows = got_ref.shape[1] * LANES // (2 * rank2)
    up_at = pl.multiple_of(dp_at * rows, rows)
    at = pl.multiple_of(head_at * rows, rows)
    down_at = pl.multiple_of(dp_at * dm1_ref.shape[2] + head_at * rows, rows)
    up_turn[...] = flipped(up_ref)
    down_turn[...] = flipped(down_ref)
    for n, ref in enumerate((dn_ref, dm1_ref, dm2_ref)):
        part_turn[n] = flipped(ref)
    here = pl.ds(at, rows)
    weight = jnp.concatenate([up_turn[pl.ds(up_at, rows), :], down_turn[pl.ds(down_at, rows), :]], 1)
    noise = jnp.concatenate([side_by_side(un_ref), part_turn[0, here, :]], 1)
    first = jnp.concatenate([side_by_side(um1_ref), part_turn[1, here, :]], 1)
    second = jnp.concatenate([side_by_side(um2_ref), part_turn[2, here, :]], 1)
    total = jnp.sum(got_ref[...], 0)
    total = jnp.concatenate([total[:, : 2 * rank2], total[:, 2 * rank2 :]], 0)
    grad = (total + noise_mult * clip_bound * noise) / examples
    first_new, second_new, direction = lamb(weight, grad, first, second, fix_ref[0], fix_ref[1])
    um1_out[...] = first_new
    um2_out[...] = second_new
    dir_ref[...] = direction
    w_out[...] = weight
    down_grad = grad[:, rank2:]
    per_line = LANES // rank2
    lines = [
        jnp.concatenate([down_grad[k : k + 1] for k in range(line, line + per_line)], 1)
        for line in range(0, rows, per_line)
    ]
    lines.append(
        jnp.concatenate(
            [jnp.sum(direction * direction, 0, keepdims=True), jnp.sum(weight * weight, 0, keepdims=True)], 1
        )
    )
    lines.append(loss_ref[...])
    tile = jnp.concatenate(lines, 0)
    for to in range(tile_ref.shape[0]):
        tile_ref[to] = tile


def update_kernel(
    examples, shards, sc_ref, fix_ref, got_ref, down_ref, dm1_ref, dm2_ref, um1_ref, um2_ref, dir_ref, w_ref,
    loss_ref, dm1_out, dm2_out, dw_out, um1_out, um2_out, uw_out, table_ref, down_turn,
):
    dp_at = sc_ref[0]
    rows = w_ref.shape[0]
    rank2 = w_ref.shape[1] // 2
    rank = rank2 // 2
    per_line = LANES // rank2
    lines = rows // per_line
    total = jnp.sum(got_ref[...], 0)
    loss_ref[...] = total[lines + 1 : lines + 2, 0:1] / examples
    stats = total[lines : lines + 1, :]
    lane = iota(stats.shape, 1)

    def part(group):
        inside = (lane >= group * rank) & (lane < (group + 1) * rank)
        return jnp.sqrt(jnp.sum(jnp.where(inside, stats, 0.0), 1, keepdims=True))

    norms = [(part(group + 4), part(group)) for group in range(4)]
    for out_col, group in enumerate((2, 3, 0, 1)):
        table_ref[:, out_col : out_col + 1] = jnp.concatenate(norms[group], 0)

    def rate(a, b):
        wide = iota((1, rank2), 1) < rank
        return learn_rate * jnp.where(wide, norms[a][0] / norms[a][1], norms[b][0] / norms[b][1])

    up_new = w_ref[:, :rank2] - rate(0, 1) * dir_ref[:, :rank2]
    for ref, value in ((uw_out, up_new), (um1_out, um1_ref[...]), (um2_out, um2_ref[...])):
        ref[0] = value[:, :rank]
        ref[1] = value[:, rank:rank2]
    grad = jnp.concatenate(
        [
            got_ref[dp_at * shards + j, k // per_line, (k % per_line) * rank2 : (k % per_line + 1) * rank2]
            .reshape(1, rank2)
            for j in range(shards)
            for k in range(rows)
        ],
        0,
    )
    many = dm1_ref.shape[2]
    down_turn[...] = flipped(down_ref)
    weight = down_turn[pl.ds(pl.multiple_of(dp_at * many, many), many), :]
    first_new, second_new, direction = lamb(
        weight, grad, flipped(dm1_ref), flipped(dm2_ref), fix_ref[0], fix_ref[1]
    )
    new = weight - rate(2, 3) * direction
    for ref, value in ((dm1_out, first_new), (dm2_out, second_new), (dw_out, new)):
        ref[...] = value.T.reshape(ref.shape)


def per_device(
    slot_token_ids,
    lengths,
    labels,
    optimizer_step_count,
    token_embedding_table,
    positions,
    query_key_value_weight,
    attention_output_weight,
    feedforward_input_weight,
    feedforward_output_weight,
    layer_norm_gains,
    layer_norm_biases,
    classifier,
    adapter_down_maps,
    adapter_up_maps,
    down_first_moment,
    down_second_moment,
    up_first_moment,
    up_second_moment,
    down_privacy_noise,
    up_privacy_noise,
):
    shards = lax.axis_size("head")
    groups = lax.axis_size("dp")
    devices = shards * groups
    dp_at = lax.axis_index("dp")
    head_at = lax.axis_index("head")
    slots, width = positions.shape
    rank = adapter_down_maps.shape[2]
    rank2 = 2 * rank
    units = feedforward_output_weight.shape[0]
    local_w = attention_output_weight.shape[0]
    owned = token_embedding_table.shape[0]
    shape = jax.ShapeDtypeStruct

    def turned(x):
        return jnp.swapaxes(x, 1, 2)

    down_maps = turned(adapter_down_maps)

    def ask(which, slot_token_ids):
        return call(
            functools.partial(request_kernel, groups, shards, owned),
            (shape((devices, 1, LANES), i32), shape((slots, LANES), i32)),
            [SM, SM, VM],
            (VM, VM),
        )(jnp.stack([head_at, which]).astype(i32), lengths, slot_token_ids)

    def look(wanted):
        return call(
            lookup_kernel,
            shape((devices, CAP, LANES), bf16),
            [SM, VM],
            VM,
            [pltpu.VMEM((owned, LANES), f32), pltpu.VMEM((CAP, LANES), f32)],
            flops=10**10,
        )(wanted, token_embedding_table)

    def place(found, slot):
        got = exchange(found)
        emb = call(
            functools.partial(assemble_kernel, groups, shards),
            shape((slots, width), bf16),
            [VM, VM],
            VM,
            [pltpu.VMEM((groups * CAP, width), bf16)],
            flops=2 * 10**10,
        )(got, slot)
        return emb

    def exchange(x):
        return lax.all_to_all(x, ALL, 0, 0, tiled=True)

    pack = call(
        pack_kernel,
        shape((width // GROUPS * 2 + 2 * width // shards // GROUPS, units), bf16),
        [SM, ANY, ANY, ANY],
        VM,
        [pltpu.SemaphoreType.DMA((4,))],
        vmem=60,
    )(
        dp_at.reshape(1).astype(i32), feedforward_input_weight, feedforward_output_weight,
        attention_output_weight,
    )
    pack, slot_token_ids = lax.optimization_barrier((pack, slot_token_ids))
    weights = lax.all_gather(pack, ("head", "dp"), axis=0, tiled=True).reshape(shards, groups, *pack.shape)

    steps = shards // 2
    packed = jnp.concatenate(
        [
            query_key_value_weight.reshape(3 * width, local_w),
            adapter_up_maps.reshape(rank2, local_w).astype(bf16),
        ],
        0,
    )
    order = jnp.stack(
        [
            2 * ((head_at // 2 + step) % steps) + (head_at + column) % 2
            for step in range(steps)
            for column in range(2)
        ]
    ).astype(i32)

    def permuted(x, source):
        return lax.ppermute(x, "head", [(source(i), i) for i in range(shards)])

    packed_z = [permuted(packed, lambda i, step=step: (i + 2 * step) % shards) for step in range(1, steps)]
    requests, slot = ask(jnp.zeros((), i32), slot_token_ids)

    wanted = exchange(requests)
    rounds = jnp.max(wanted[:, 0, LANES - 1])
    found, packed_z = lax.optimization_barrier((look(wanted), packed_z))
    w_own = jnp.stack([packed, *packed_z])
    w_peer = permuted(w_own, lambda i: i ^ 1)
    emb = place(found, slot)

    def again(which):
        asked, where = ask(which, slot_token_ids)
        return place(look(exchange(asked)), where)

    unused_at, emb = lax.while_loop(
        lambda state: state[0] < rounds,
        lambda state: (state[0] + 1, state[1] + again(state[0])),
        (jnp.ones((), i32), emb),
    )

    own_len = lax.dynamic_slice_in_dim(lengths, head_at, 1)
    own_label = lax.dynamic_slice_in_dim(labels, head_at, 1)
    x0, x0b, xa, q, k, v = call(
        functools.partial(project_kernel, shards),
        (
            shape((slots, width), f32),
            shape((slots, width), bf16),
            shape((slots, rank2), bf16),
            shape((shards, slots, LANES), bf16),
            shape((shards, slots, LANES), bf16),
            shape((shards, slots, LANES), bf16),
        ),
        [VM, VM, VM, VM, VM, ANY, ANY],
        (VM,) * 6,
        [
            pltpu.VMEM((shards // 2, width, 6 * LANES), bf16),
            pltpu.VMEM((shards // 2, rank2, 6 * LANES), bf16),
            pltpu.SemaphoreType.DMA((shards // 2, 10)),
        ],
        vmem=50,
    )(emb, positions, layer_norm_gains, layer_norm_biases, down_maps, w_own, w_peer)
    lse, ctx = call(
        functools.partial(attend_kernel, shards),
        (shape((shards, 2, slots), f32), shape((slots, width), bf16)),
        [SM, SM, VM, VM, VM],
        (VM, VM),
        vmem=40,
    )(own_len, order, q, k, v)

    dctx, loss = call(
        functools.partial(middle_kernel, shards),
        (shape((slots, width), bf16), shape((1, LANES), f32)),
        [SM, SM, VM, VM, VM, VM, VM, ANY],
        (VM, VM),
        [
            pltpu.VMEM((shards, groups // 2, 2 * local_w // groups, width), bf16),
            pltpu.VMEM((shards, groups, width // groups, units), bf16),
            pltpu.VMEM((shards, groups, units // groups, width), bf16),
            pltpu.VMEM((shards, slots, units), f32),
            pltpu.VMEM((slots, width), f32),
            pltpu.VMEM((slots, width), f32),
            pltpu.VMEM((slots, width), bf16),
            pltpu.VMEM((slots, width), f32),
            pltpu.VMEM((slots, width), bf16),
            pltpu.SemaphoreType.DMA((shards, 5)),
        ],
        vmem=60,
    )(
        own_len, own_label, x0, ctx, layer_norm_gains, layer_norm_biases, classifier, weights
    )

    send, norm = call(
        functools.partial(gradient_kernel, shards, groups),
        (shape((devices, 2 * rank2 * width // devices // LANES, LANES), f32), shape((1, LANES), f32)),
        [SM, SM, VM, VM, VM, VM, VM, VM, VM, ANY, ANY],
        (VM, VM),
        [
            pltpu.VMEM((shards, rank2, LANES), bf16),
            pltpu.VMEM((width, rank2), f32),
            pltpu.VMEM((rank2, slots), f32),
            pltpu.SemaphoreType.DMA((shards,)),
        ],
        vmem=50,
    )(own_len, order, x0b, xa, q, k, v, lse, dctx, w_own, w_peer)

    got = exchange(send)
    examples = float(devices)
    step_number = optimizer_step_count.astype(f32)
    fixes = jnp.stack([1.0 - jnp.power(beta_one, step_number), 1.0 - jnp.power(beta_two, step_number)])
    where = jnp.stack([dp_at, head_at]).astype(i32)
    rows = width // devices
    small = shape((rows, 2 * rank2), f32)
    moments = [turned(x) for x in (down_first_moment, down_second_moment, up_first_moment, up_second_moment)]
    lines = rows * rank2 // LANES + 2
    tile, um1, um2, direction, weight = call(
        functools.partial(direction_kernel, examples),
        (shape((devices, lines, LANES), f32), small, small, small, small),
        [SM, SM] + [VM] * 10,
        (VM,) * 5,
        [
            pltpu.VMEM((local_w, rank2), f32),
            pltpu.VMEM((width, rank2), f32),
            pltpu.VMEM((3, width // groups, rank2), f32),
        ],
    )(
        where, fixes, got, loss, down_maps, adapter_up_maps, *moments,
        turned(down_privacy_noise), turned(up_privacy_noise),
    )
    spread = exchange(tile)
    down_shape = shape(moments[0].shape, f32)
    up_shape = shape(moments[2].shape, f32)
    loss_mean, dm1, dm2, dw, bm1, bm2, bw, table = call(
        functools.partial(update_kernel, examples, shards),
        (
            shape((1, 1), f32), down_shape, down_shape, down_shape, up_shape, up_shape, up_shape,
            shape((2, 4), f32),
        ),
        [SM, SM] + [VM] * 8,
        (VM,) * 8,
        [pltpu.VMEM((width, rank2), f32)],
    )(where, fixes, spread, down_maps, moments[0], moments[1], um1, um2, direction, weight)
    return (
        loss_mean.reshape(()),
        norm[0, 0:1],
        turned(dm1),
        turned(dm2),
        turned(dw),
        turned(bm1),
        turned(bm2),
        turned(bw),
        table.T,
    )


def solution(mesh):
    placed = (
        P("dp", None),
        P("dp"),
        P("dp"),
        P(),
        P("dp", "head"),
        P(),
        P(None, None, "head"),
        P("head", None),
        P(None, "head"),
        P("head", None),
        P(),
        P(),
        P(),
        P(),
        P(None, None, "head"),
        P(None, "dp", None),
        P(None, "dp", None),
        P(None, None, ("head", "dp")),
        P(None, None, ("head", "dp")),
        P(None, "dp", None),
        P(None, None, ("head", "dp")),
    )
    return jax.shard_map(
        per_device,
        mesh=mesh,
        in_specs=placed,
        out_specs=(
            P(),
            P(("dp", "head")),
            P(None, "dp", None),
            P(None, "dp", None),
            P(None, "dp", None),
            P(None, None, ("head", "dp")),
            P(None, None, ("head", "dp")),
            P(None, None, ("head", "dp")),
            P(),
        ),
        check_vma=False,
    )
```

```python
import functools

import jax
import jax.numpy as jnp
from jax import lax
from jax.experimental import pallas as pl
from jax.experimental.pallas import tpu as pltpu
from jax.sharding import PartitionSpec as P

HDIM = 64
CAP = 48
GROUPS = 16
LANES = 128
MIB = 1 << 20

adapter_scale = 2.0
clip_bound = 1.0
noise_mult = 0.6
smooth_rate = 0.1
beta_one = 0.9
beta_two = 0.999
adam_eps = 1e-06
decay_rate = 0.01
learn_rate = 0.25
norm_eps = 1e-05

f32 = jnp.float32
bf16 = jnp.bfloat16
i32 = jnp.int32
LAST = (((1,), (1,)), ((), ()))
ALL = ("dp", "head")
VM = pl.BlockSpec(memory_space=pltpu.VMEM)
SM = pl.BlockSpec(memory_space=pltpu.SMEM)
ANY = pl.BlockSpec(memory_space=pl.ANY)


def iota(shape, axis):
    return lax.broadcasted_iota(i32, shape, axis)


def mm(a, b):
    return jnp.dot(a, b, preferred_element_type=f32)


def mm_last(a, b):
    return lax.dot_general(a, b, LAST, preferred_element_type=f32)


def call(kernel, outs, in_specs, out_specs, scratch=(), vmem=32, flops=1):
    return pl.pallas_call(
        kernel,
        out_shape=outs,
        in_specs=in_specs,
        out_specs=out_specs,
        scratch_shapes=list(scratch),
        compiler_params=pltpu.CompilerParams(vmem_limit_bytes=vmem * MIB),
        cost_estimate=pl.CostEstimate(flops=flops, bytes_accessed=1, transcendentals=0),
    )


def request_kernel(owners, peers, owned, sc_ref, len_ref, ids_ref, req_ref, slot_ref):
    me = sc_ref[0]
    base = (sc_ref[1] * CAP).astype(f32)
    count = len_ref[me]
    ids = ids_ref[...].astype(f32)
    examples, slots = ids.shape
    row = jnp.sum(jnp.where(iota(ids.shape, 0) == me, ids, 0.0), 0, keepdims=True)
    flipped = ids.T
    col = jnp.sum(jnp.where(iota(flipped.shape, 1) == me, flipped, 0.0), 1, keepdims=True)
    t_col = iota((slots, slots), 0)
    t_row = iota((slots, slots), 1)
    valid_col = (iota((slots, 1), 0) < count).astype(f32)
    valid_row = (iota((1, slots), 1) < count).astype(f32)
    own_col = sum((col >= k * owned).astype(f32) for k in range(1, owners))
    own_row = sum((row >= k * owned).astype(f32) for k in range(1, owners))
    same = (col == row) & (t_row < count) & (t_col < count)
    before = t_row < t_col
    after = t_col < t_row
    seen_col = jnp.sum(jnp.where(same & before, 1.0, 0.0), 1, keepdims=True)
    seen_row = jnp.sum(jnp.where(same & after, 1.0, 0.0), 0, keepdims=True)
    first_col = jnp.where(seen_col == 0.0, valid_col, 0.0)
    first_row = jnp.where(seen_row == 0.0, valid_row, 0.0)
    shared = own_col == own_row
    place_col = jnp.sum(jnp.where(shared & before, first_row, 0.0), 1, keepdims=True)
    place_row = jnp.sum(jnp.where(shared & after, first_col, 0.0), 0, keepdims=True)
    rank = jnp.sum(jnp.where(same, first_row * place_row, 0.0), 1, keepdims=True)
    local = rank - base
    here = (local >= 0.0) & (local < CAP) & (valid_col > 0.0)
    slot = jnp.where(here, own_col * CAP + local, -1.0)
    slot_ref[...] = jnp.broadcast_to(slot, slot_ref.shape).astype(i32)
    rounds = jnp.floor(jnp.max(rank, 0, keepdims=True) * (1.0 / CAP) + 0.5 / CAP) + 1.0
    lane = iota((slots, LANES), 1)
    lane_f = lane.astype(f32)
    wanted = jnp.where(first_col > 0.0, place_col - base, -1.0)
    hit = (wanted == lane_f) & (lane < CAP)
    lane_row = iota((1, LANES), 1)
    for owner in range(owners):
        chosen = jnp.where(hit & (own_col == float(owner)), col - float(owner * owned), 0.0)
        line = jnp.sum(chosen, 0, keepdims=True)
        line = jnp.where(lane_row == LANES - 1, rounds, line).astype(i32)
        for peer in range(peers):
            req_ref[owner * peers + peer] = line


def lookup_kernel(want_ref, table_ref, out_ref, wide_ref, stage_ref):
    wide_ref[...] = table_ref[...].astype(f32)

    def one(src, carry):
        for p in range(CAP):
            stage_ref[p : p + 1, :] = wide_ref[pl.ds(want_ref[src, 0, p], 1), :]
        out_ref[src] = stage_ref[...].astype(bf16)
        return carry

    lax.fori_loop(0, want_ref.shape[0], one, 0)


def assemble_kernel(owners, peers, got_ref, slot_ref, emb_ref, rows_ref):
    for owner in range(owners):
        for peer in range(peers):
            rows_ref[owner * CAP : (owner + 1) * CAP, peer * LANES : (peer + 1) * LANES] = got_ref[
                owner * peers + peer
            ]
    slot = slot_ref[...]
    lane = iota(slot.shape, 1)
    picks = [
        (slot == lane + first).astype(f32).astype(bf16)
        for first in range(0, owners * CAP, LANES)
    ]
    emb_ref[...] = mm(jnp.concatenate(picks, 1), rows_ref[...]).astype(bf16)


def pack_kernel(at_ref, in_ref, out_ref, att_ref, pack_ref, sems):
    at = at_ref[0]
    wide = in_ref.shape[1]
    in_rows, out_rows = in_ref.shape[0] // GROUPS, out_ref.shape[0] // GROUPS
    att_rows = 2 * att_ref.shape[0] // GROUPS
    here = lambda rows: pl.ds(pl.multiple_of(at * rows, rows), rows)
    moves = [(in_ref.at[here(in_rows), :], pack_ref.at[pl.ds(0, in_rows), :])]
    row = in_rows
    for first in range(0, 2 * wide, wide):
        moves.append((out_ref.at[here(out_rows), pl.ds(first, wide)], pack_ref.at[pl.ds(row, out_rows), :]))
        row += out_rows
    half = att_ref.at[
        pl.ds(pl.multiple_of(at // 2 * att_rows, att_rows), att_rows),
        pl.ds(pl.multiple_of(at % 2 * wide, wide), wide),
    ]
    moves.append((half, pack_ref.at[pl.ds(row, att_rows), :]))
    copies = [pltpu.make_async_copy(source, target, sems.at[n]) for n, (source, target) in enumerate(moves)]
    for one in copies:
        one.start()
    for one in copies:
        one.wait()


def normalize(inputs):
    centre = inputs - jnp.mean(inputs, -1, keepdims=True)
    inv_std = lax.rsqrt(jnp.mean(centre * centre, -1, keepdims=True) + norm_eps)
    return centre * inv_std, inv_std


def norm_back(scaled, x_hat, inv_std):
    return inv_std * (
        scaled
        - jnp.mean(scaled, -1, keepdims=True)
        - x_hat * jnp.mean(scaled * x_hat, -1, keepdims=True)
    )


def halves(pair):
    low = iota(pair.shape, 1) < HDIM
    zero = jnp.zeros_like(pair)
    return jnp.where(low, pair, zero), jnp.where(low, zero, pair)


def flip(x):
    return x.astype(f32).T


def rows_of(shards, width):
    in_rows = width // GROUPS
    return in_rows, in_rows // 2, 2 * width // shards // GROUPS


def project_kernel(
    shards, emb_ref, pos_ref, gain_ref, bias_ref, down_ref, w_own, w_peer,
    x_ref, xb_ref, xa_ref, q_ref, k_ref, v_ref,
    w_buf, up_buf, sems,
):
    slots, width = emb_ref.shape
    rank = down_ref.shape[1]
    rank2 = 2 * rank
    three = 3 * LANES
    copies = []
    up_buf[...] = jnp.zeros_like(up_buf)
    for pair in range(shards // 2):
        mine = []
        for side, w_ref in enumerate((w_own, w_peer)):
            for part in range(3):
                mine.append(
                    pltpu.make_async_copy(
                        w_ref.at[pair, pl.ds(part * width, width), :],
                        w_buf.at[pair, :, pl.ds(side * three + part * LANES, LANES)],
                        sems.at[pair, side * 5 + part],
                    )
                )
            for part in range(2):
                mine.append(
                    pltpu.make_async_copy(
                        w_ref.at[pair, pl.ds(3 * width + part * rank, rank), :],
                        up_buf.at[pair, pl.ds(part * rank, rank), pl.ds(side * three + 2 * part * LANES, LANES)],
                        sems.at[pair, side * 5 + 3 + part],
                    )
                )
        copies.append(mine)
    for mine in copies:
        for one in mine:
            one.start()
    x_hat, unused_std = normalize(emb_ref[...].astype(f32) + pos_ref[...].astype(f32))
    x0 = x_hat * gain_ref[0:1, :] + bias_ref[0:1, :]
    x_ref[...] = x0
    xb_ref[...] = x0.astype(bf16)
    xa = mm_last(xb_ref[...], down_ref[...].reshape(rank2, width).astype(bf16)).astype(bf16)
    xa_ref[...] = xa
    twice = xa * jnp.asarray(adapter_scale, bf16)
    for pair in range(shards // 2):
        for one in copies[pair]:
            one.wait()
        total = mm(xb_ref[...], w_buf[pair]) + mm(twice, up_buf[pair])
        for side in range(2):
            first = side * three
            q_ref[2 * pair + side] = (total[:, first : first + LANES] * (HDIM**-0.5)).astype(bf16)
            k_ref[2 * pair + side] = total[:, first + LANES : first + 2 * LANES].astype(bf16)
            v_ref[2 * pair + side] = total[:, first + 2 * LANES : first + three].astype(bf16)


def attend_kernel(shards, len_ref, order_ref, q_ref, k_ref, v_ref, lse_ref, ctx_ref):
    slots = q_ref.shape[1]
    count = len_ref[0]
    block = slots // 2
    keep = iota((slots, block), 0) < count

    def one_pair(j, carry):
        k_sides = halves(k_ref[j])
        v_flip = flip(v_ref[j]).astype(bf16)
        for first in range(0, slots, block):
            q = q_ref[j, first : first + block, :]
            parts = []
            for side in range(2):
                s = jnp.where(keep, mm_last(k_sides[side], q), -1e30)
                top = jnp.max(s, 0, keepdims=True)
                e = jnp.exp(s - top)
                total = jnp.sum(e, 0, keepdims=True)
                prob = (e * (1.0 / total)).astype(bf16)
                lse_ref[j, side : side + 1, first : first + block] = top + jnp.log(total)
                parts.append(mm(v_flip[side * HDIM : (side + 1) * HDIM, :], prob))
            both = jnp.concatenate(parts, 0).T
            ctx_ref[first : first + block, pl.ds(pl.multiple_of(order_ref[j] * LANES, LANES), LANES)] = (
                both.astype(bf16)
            )
        return carry

    lax.fori_loop(0, shards, one_pair, 0)


def gelu_parts(x):
    z = jnp.abs(x) * (0.5**0.5)
    t = 1.0 / (1.0 + 0.3275911 * z)
    poly = t * (
        0.254829592
        + t * (-0.284496736 + t * (1.421413741 + t * (-1.453152027 + t * 1.061405429)))
    )
    bell = jnp.exp(-0.5 * x * x)
    tail = 0.5 * poly * bell
    cdf = jnp.where(x < 0.0, tail, 1.0 - tail)
    return x * cdf, cdf + x * bell * 0.3989422804014327


def middle_kernel(
    shards, len_ref, label_ref, x_ref, ctx_ref, gain_ref, bias_ref, class_ref, w_ref,
    dctx_ref, loss_ref,
    wo_buf, wi_buf, wf_buf, slope_buf, acc_ref, h_ref, hb_ref, hat_ref, df_ref, sems,
):
    slots, width = x_ref.shape
    classes = class_ref.shape[0]
    units = wi_buf.shape[-1]
    in_rows, out_rows, att_rows = rows_of(shards, width)
    start = in_rows + 2 * out_rows
    copies = []
    for shard in range(shards):
        mine = [
            pltpu.make_async_copy(w_ref.at[shard, :, pl.ds(0, in_rows), :], wi_buf.at[shard], sems.at[shard, 0])
        ]
        for side in range(2):
            cols = pl.ds(side * units, units)
            mine.append(
                pltpu.make_async_copy(
                    w_ref.at[shard, :, pl.ds(in_rows + side * out_rows, out_rows), :],
                    wf_buf.at[shard, :, :, cols],
                    sems.at[shard, 1 + side],
                )
            )
        copies.append(mine)
    wo_copies = []
    for place in range(GROUPS):
        wo_copies.append(
            pltpu.make_async_copy(
                w_ref.at[:, place, pl.ds(start, att_rows), :],
                wo_buf.at[:, place // 2, :, pl.ds(place % 2 * units, units)],
                sems.at[place % shards, 3 + place // shards],
            )
        )
    for one in wo_copies:
        one.start()
    for mine in copies:
        for one in mine:
            one.start()
    count = len_ref[0]
    count_f = count.astype(f32)
    label = label_ref[0]
    for one in wo_copies:
        one.wait()
    hat1, std1 = normalize(x_ref[...] + mm(ctx_ref[...], wo_buf[...].reshape(width, width)))
    hat_ref[...] = hat1
    h1 = hat1 * gain_ref[1:2, :] + bias_ref[1:2, :]
    h_ref[...] = h1
    hb_ref[...] = h1.astype(bf16)
    for f in range(shards):
        for one in copies[f]:
            one.wait()
        g, slope = gelu_parts(mm(hb_ref[...], wi_buf[f].reshape(width, units)))
        slope_buf[f] = slope
        part = mm(g.astype(bf16), wf_buf[f].reshape(units, width))
        if f == 0:
            acc_ref[...] = part
        else:
            acc_ref[...] += part
    hat2, std2 = normalize(h_ref[...] + acc_ref[...])
    gain2 = gain_ref[2:3, :]
    valid = (iota((slots, 1), 0) < count).astype(f32)
    pooled = jnp.sum((hat2 * gain2 + bias_ref[2:3, :]) * valid, 0, keepdims=True) / count_f
    weights = class_ref[...].astype(f32)
    logits = jnp.sum(pooled.astype(bf16).astype(f32) * weights, 1, keepdims=True)
    shifted = logits - jnp.max(logits, 0, keepdims=True)
    log_prob = shifted - jnp.log(jnp.sum(jnp.exp(shifted), 0, keepdims=True))
    target = (1.0 - smooth_rate) * (iota((classes, 1), 0) == label).astype(f32) + smooth_rate / classes
    loss_ref[...] = jnp.broadcast_to(-jnp.sum(target * log_prob, 0, keepdims=True), loss_ref.shape)
    d_pooled = jnp.sum((jnp.exp(log_prob) - target) * weights, 0, keepdims=True) / count_f
    d_two = norm_back((d_pooled * gain2) * valid, hat2, std2)
    acc_ref[...] = d_two
    df_ref[...] = d_two.astype(bf16)
    for f in range(shards):
        d_pre = (mm_last(df_ref[...], wf_buf[f].reshape(units, width)) * slope_buf[f]).astype(bf16)
        acc_ref[...] += mm_last(d_pre, wi_buf[f].reshape(width, units))
    d_attn = norm_back(acc_ref[...] * gain_ref[1:2, :], hat_ref[...], std1).astype(bf16)
    dctx_ref[...] = mm_last(d_attn, wo_buf[...].reshape(width, width)).astype(bf16)


def gradient_kernel(
    shards, groups, len_ref, order_ref, xb_ref, xa_ref, q_ref, k_ref, v_ref, lse_ref, dctx_ref, w_own, w_peer,
    send_ref, norm_ref,
    up_buf, up_grad, inner_ref, sems,
):
    slots, width = xb_ref.shape
    rank2 = xa_ref.shape[1]
    rank = rank2 // 2
    copies = [
        pltpu.make_async_copy(
            (w_own, w_peer)[j % 2].at[j // 2, pl.ds(3 * width, rank2), :], up_buf.at[j], sems.at[j]
        )
        for j in range(shards)
    ]
    for one in copies:
        one.start()
    for one in copies:
        one.wait()
    count = len_ref[0]
    block = slots // 2
    keep = iota((slots, block), 0) < count
    xa = xa_ref[...]
    low = iota((LANES, rank2), 1) < rank
    inner_ref[...] = jnp.zeros_like(inner_ref)

    def one_pair(j, carry):
        k = k_ref[j]
        k_sides = halves(k)
        v_sides = halves(v_ref[j])
        k_flip = flip(k).astype(bf16)
        columns = pl.ds(pl.multiple_of(order_ref[j] * LANES, LANES), LANES)
        dv = jnp.zeros((slots, LANES), f32)
        flips = []
        for first in range(0, slots, block):
            q = q_ref[j, first : first + block, :]
            dctx = dctx_ref[first : first + block, columns]
            dctx_sides = halves(dctx)
            parts = []
            for side in range(2):
                s = jnp.where(keep, mm_last(k_sides[side], q), -1e30)
                prob = jnp.exp(s - lse_ref[j, side : side + 1, first : first + block])
                d_prob = mm_last(v_sides[side], dctx)
                weighted = jnp.sum(prob * d_prob, 0, keepdims=True)
                d_s = (prob * (d_prob - weighted)).astype(bf16)
                dv = dv + mm(prob.astype(bf16), dctx_sides[side])
                parts.append(mm(k_flip[side * HDIM : (side + 1) * HDIM, :], d_s))
            flips.append(jnp.concatenate(parts, 0))
        dq_flip = (jnp.concatenate(flips, 1) * (HDIM**-0.5)).astype(bf16)
        dv_flip = flip(dv.astype(bf16)).astype(bf16)
        up_grad[columns, :] = adapter_scale * jnp.where(
            low, mm(dq_flip, xa), mm(dv_flip, xa)
        )
        inner_ref[0:rank, :] += adapter_scale * mm(up_buf[j, 0:rank, :], dq_flip)
        inner_ref[rank:rank2, :] += adapter_scale * mm(up_buf[j, rank:rank2, :], dv_flip)
        return carry

    lax.fori_loop(0, shards, one_pair, 0)
    down_grad = mm(inner_ref[...].astype(bf16), xb_ref[...]).T
    both = jnp.concatenate([up_grad[...], down_grad], 1)
    squares = jnp.sum(jnp.sum(both * both, 1, keepdims=True), 0, keepdims=True)
    norm = jnp.sqrt(squares)
    norm_ref[...] = jnp.broadcast_to(norm, norm_ref.shape)
    both = both * (clip_bound / jnp.maximum(norm, clip_bound))
    rows = width // (groups * shards)
    part = rows // 2
    for i in range(groups):
        for j in range(shards):
            to = i * shards + j
            at_up = (j * groups + i) * rows
            at_down = to * rows
            for n in range(2):
                lane = 2 * rank2 * n
                send_ref[to, :, lane : lane + rank2] = both[at_up + n * part : at_up + (n + 1) * part, 0:rank2]
                send_ref[to, :, lane + rank2 : lane + 2 * rank2] = both[
                    at_down + n * part : at_down + (n + 1) * part, rank2:
                ]


def lamb(weight, grad, first, second, fix_one, fix_two):
    first_new = beta_one * first + (1.0 - beta_one) * grad
    second_new = beta_two * second + (1.0 - beta_two) * grad * grad
    direction = first_new / fix_one / (jnp.sqrt(second_new / fix_two) + adam_eps) + decay_rate * weight
    return first_new, second_new, direction


def side_by_side(ref):
    return jnp.concatenate([ref[0], ref[1]], 1)


def flipped(ref):
    maps, rank, cols = ref.shape
    return ref[...].reshape(maps * rank, cols).T


def direction_kernel(
    examples, sc_ref, fix_ref, got_ref, loss_ref, down_ref, up_ref, dm1_ref, dm2_ref, um1_ref, um2_ref,
    dn_ref, un_ref,
    tile_ref, um1_out, um2_out, dir_ref, w_out, up_turn, down_turn, part_turn,
):
    dp_at, head_at = sc_ref[0], sc_ref[1]
    rank2 = up_turn.shape[1]
    rows = got_ref.shape[1] * LANES // (2 * rank2)
    up_at = pl.multiple_of(dp_at * rows, rows)
    at = pl.multiple_of(head_at * rows, rows)
    down_at = pl.multiple_of(dp_at * dm1_ref.shape[2] + head_at * rows, rows)
    up_turn[...] = flipped(up_ref)
    down_turn[...] = flipped(down_ref)
    for n, ref in enumerate((dn_ref, dm1_ref, dm2_ref)):
        part_turn[n] = flipped(ref)
    here = pl.ds(at, rows)
    weight = jnp.concatenate([up_turn[pl.ds(up_at, rows), :], down_turn[pl.ds(down_at, rows), :]], 1)
    noise = jnp.concatenate([side_by_side(un_ref), part_turn[0, here, :]], 1)
    first = jnp.concatenate([side_by_side(um1_ref), part_turn[1, here, :]], 1)
    second = jnp.concatenate([side_by_side(um2_ref), part_turn[2, here, :]], 1)
    total = jnp.sum(got_ref[...], 0)
    total = jnp.concatenate([total[:, : 2 * rank2], total[:, 2 * rank2 :]], 0)
    grad = (total + noise_mult * clip_bound * noise) / examples
    first_new, second_new, direction = lamb(weight, grad, first, second, fix_ref[0], fix_ref[1])
    um1_out[...] = first_new
    um2_out[...] = second_new
    dir_ref[...] = direction
    w_out[...] = weight
    down_grad = grad[:, rank2:]
    per_line = LANES // rank2
    lines = [
        jnp.concatenate([down_grad[k : k + 1] for k in range(line, line + per_line)], 1)
        for line in range(0, rows, per_line)
    ]
    lines.append(
        jnp.concatenate(
            [jnp.sum(direction * direction, 0, keepdims=True), jnp.sum(weight * weight, 0, keepdims=True)], 1
        )
    )
    lines.append(loss_ref[...])
    tile = jnp.concatenate(lines, 0)
    for to in range(tile_ref.shape[0]):
        tile_ref[to] = tile


def update_kernel(
    examples, shards, sc_ref, fix_ref, got_ref, down_ref, dm1_ref, dm2_ref, um1_ref, um2_ref, dir_ref, w_ref,
    loss_ref, dm1_out, dm2_out, dw_out, um1_out, um2_out, uw_out, table_ref, down_turn,
):
    dp_at = sc_ref[0]
    rows = w_ref.shape[0]
    rank2 = w_ref.shape[1] // 2
    rank = rank2 // 2
    per_line = LANES // rank2
    lines = rows // per_line
    total = jnp.sum(got_ref[...], 0)
    loss_ref[...] = total[lines + 1 : lines + 2, 0:1] / examples
    stats = total[lines : lines + 1, :]
    lane = iota(stats.shape, 1)

    def part(group):
        inside = (lane >= group * rank) & (lane < (group + 1) * rank)
        return jnp.sqrt(jnp.sum(jnp.where(inside, stats, 0.0), 1, keepdims=True))

    norms = [(part(group + 4), part(group)) for group in range(4)]
    for out_col, group in enumerate((2, 3, 0, 1)):
        table_ref[:, out_col : out_col + 1] = jnp.concatenate(norms[group], 0)

    def rate(a, b):
        wide = iota((1, rank2), 1) < rank
        return learn_rate * jnp.where(wide, norms[a][0] / norms[a][1], norms[b][0] / norms[b][1])

    up_new = w_ref[:, :rank2] - rate(0, 1) * dir_ref[:, :rank2]
    for ref, value in ((uw_out, up_new), (um1_out, um1_ref[...]), (um2_out, um2_ref[...])):
        ref[0] = value[:, :rank]
        ref[1] = value[:, rank:rank2]
    grad = jnp.concatenate(
        [
            got_ref[dp_at * shards + j, k // per_line, (k % per_line) * rank2 : (k % per_line + 1) * rank2]
            .reshape(1, rank2)
            for j in range(shards)
            for k in range(rows)
        ],
        0,
    )
    many = dm1_ref.shape[2]
    down_turn[...] = flipped(down_ref)
    weight = down_turn[pl.ds(pl.multiple_of(dp_at * many, many), many), :]
    first_new, second_new, direction = lamb(
        weight, grad, flipped(dm1_ref), flipped(dm2_ref), fix_ref[0], fix_ref[1]
    )
    new = weight - rate(2, 3) * direction
    for ref, value in ((dm1_out, first_new), (dm2_out, second_new), (dw_out, new)):
        ref[...] = value.T.reshape(ref.shape)


def per_device(
    slot_token_ids,
    lengths,
    labels,
    optimizer_step_count,
    token_embedding_table,
    positions,
    query_key_value_weight,
    attention_output_weight,
    feedforward_input_weight,
    feedforward_output_weight,
    layer_norm_gains,
    layer_norm_biases,
    classifier,
    adapter_down_maps,
    adapter_up_maps,
    down_first_moment,
    down_second_moment,
    up_first_moment,
    up_second_moment,
    down_privacy_noise,
    up_privacy_noise,
):
    shards = lax.axis_size("head")
    groups = lax.axis_size("dp")
    devices = shards * groups
    dp_at = lax.axis_index("dp")
    head_at = lax.axis_index("head")
    slots, width = positions.shape
    rank = adapter_down_maps.shape[2]
    rank2 = 2 * rank
    units = feedforward_output_weight.shape[0]
    local_w = attention_output_weight.shape[0]
    owned = token_embedding_table.shape[0]
    shape = jax.ShapeDtypeStruct

    def turned(x):
        return jnp.swapaxes(x, 1, 2)

    down_maps = turned(adapter_down_maps)

    def ask(which, slot_token_ids):
        return call(
            functools.partial(request_kernel, groups, shards, owned),
            (shape((devices, 1, LANES), i32), shape((slots, LANES), i32)),
            [SM, SM, VM],
            (VM, VM),
        )(jnp.stack([head_at, which]).astype(i32), lengths, slot_token_ids)

    def look(wanted):
        return call(
            lookup_kernel,
            shape((devices, CAP, LANES), bf16),
            [SM, VM],
            VM,
            [pltpu.VMEM((owned, LANES), f32), pltpu.VMEM((CAP, LANES), f32)],
            flops=10**10,
        )(wanted, token_embedding_table)

    def place(found, slot):
        got = exchange(found)
        emb = call(
            functools.partial(assemble_kernel, groups, shards),
            shape((slots, width), bf16),
            [VM, VM],
            VM,
            [pltpu.VMEM((groups * CAP, width), bf16)],
            flops=2 * 10**10,
        )(got, slot)
        return emb

    def exchange(x):
        return lax.all_to_all(x, ALL, 0, 0, tiled=True)

    pack = call(
        pack_kernel,
        shape((width // GROUPS * 2 + 2 * width // shards // GROUPS, units), bf16),
        [SM, ANY, ANY, ANY],
        VM,
        [pltpu.SemaphoreType.DMA((4,))],
        vmem=60,
    )(
        dp_at.reshape(1).astype(i32), feedforward_input_weight, feedforward_output_weight,
        attention_output_weight,
    )
    pack, slot_token_ids = lax.optimization_barrier((pack, slot_token_ids))
    weights = lax.all_gather(pack, ("head", "dp"), axis=0, tiled=True).reshape(shards, groups, *pack.shape)

    steps = shards // 2
    packed = jnp.concatenate(
        [
            query_key_value_weight.reshape(3 * width, local_w),
            adapter_up_maps.reshape(rank2, local_w).astype(bf16),
        ],
        0,
    )
    order = jnp.stack(
        [
            2 * ((head_at // 2 + step) % steps) + (head_at + column) % 2
            for step in range(steps)
            for column in range(2)
        ]
    ).astype(i32)

    def permuted(x, source):
        return lax.ppermute(x, "head", [(source(i), i) for i in range(shards)])

    packed_z = [permuted(packed, lambda i, step=step: (i + 2 * step) % shards) for step in range(1, steps)]
    requests, slot = ask(jnp.zeros((), i32), slot_token_ids)

    wanted = exchange(requests)
    rounds = jnp.max(wanted[:, 0, LANES - 1])
    wanted, packed_z = lax.optimization_barrier((wanted, packed_z))
    found = look(wanted)
    w_own = jnp.stack([packed, *packed_z])
    w_peer = permuted(w_own, lambda i: i ^ 1)
    emb = place(found, slot)

    def again(which):
        asked, where = ask(which, slot_token_ids)
        return place(look(exchange(asked)), where)

    unused_at, emb = lax.while_loop(
        lambda state: state[0] < rounds,
        lambda state: (state[0] + 1, state[1] + again(state[0])),
        (jnp.ones((), i32), emb),
    )

    own_len = lax.dynamic_slice_in_dim(lengths, head_at, 1)
    own_label = lax.dynamic_slice_in_dim(labels, head_at, 1)
    x0, x0b, xa, q, k, v = call(
        functools.partial(project_kernel, shards),
        (
            shape((slots, width), f32),
            shape((slots, width), bf16),
            shape((slots, rank2), bf16),
            shape((shards, slots, LANES), bf16),
            shape((shards, slots, LANES), bf16),
            shape((shards, slots, LANES), bf16),
        ),
        [VM, VM, VM, VM, VM, ANY, ANY],
        (VM,) * 6,
        [
            pltpu.VMEM((shards // 2, width, 6 * LANES), bf16),
            pltpu.VMEM((shards // 2, rank2, 6 * LANES), bf16),
            pltpu.SemaphoreType.DMA((shards // 2, 10)),
        ],
        vmem=50,
    )(emb, positions, layer_norm_gains, layer_norm_biases, down_maps, w_own, w_peer)
    lse, ctx = call(
        functools.partial(attend_kernel, shards),
        (shape((shards, 2, slots), f32), shape((slots, width), bf16)),
        [SM, SM, VM, VM, VM],
        (VM, VM),
        vmem=40,
    )(own_len, order, q, k, v)

    dctx, loss = call(
        functools.partial(middle_kernel, shards),
        (shape((slots, width), bf16), shape((1, LANES), f32)),
        [SM, SM, VM, VM, VM, VM, VM, ANY],
        (VM, VM),
        [
            pltpu.VMEM((shards, groups // 2, 2 * local_w // groups, width), bf16),
            pltpu.VMEM((shards, groups, width // groups, units), bf16),
            pltpu.VMEM((shards, groups, units // groups, width), bf16),
            pltpu.VMEM((shards, slots, units), f32),
            pltpu.VMEM((slots, width), f32),
            pltpu.VMEM((slots, width), f32),
            pltpu.VMEM((slots, width), bf16),
            pltpu.VMEM((slots, width), f32),
            pltpu.VMEM((slots, width), bf16),
            pltpu.SemaphoreType.DMA((shards, 5)),
        ],
        vmem=60,
    )(
        own_len, own_label, x0, ctx, layer_norm_gains, layer_norm_biases, classifier, weights
    )

    send, norm = call(
        functools.partial(gradient_kernel, shards, groups),
        (shape((devices, 2 * rank2 * width // devices // LANES, LANES), f32), shape((1, LANES), f32)),
        [SM, SM, VM, VM, VM, VM, VM, VM, VM, ANY, ANY],
        (VM, VM),
        [
            pltpu.VMEM((shards, rank2, LANES), bf16),
            pltpu.VMEM((width, rank2), f32),
            pltpu.VMEM((rank2, slots), f32),
            pltpu.SemaphoreType.DMA((shards,)),
        ],
        vmem=50,
    )(own_len, order, x0b, xa, q, k, v, lse, dctx, w_own, w_peer)

    got = exchange(send)
    examples = float(devices)
    step_number = optimizer_step_count.astype(f32)
    fixes = jnp.stack([1.0 - jnp.power(beta_one, step_number), 1.0 - jnp.power(beta_two, step_number)])
    where = jnp.stack([dp_at, head_at]).astype(i32)
    rows = width // devices
    small = shape((rows, 2 * rank2), f32)
    moments = [turned(x) for x in (down_first_moment, down_second_moment, up_first_moment, up_second_moment)]
    lines = rows * rank2 // LANES + 2
    tile, um1, um2, direction, weight = call(
        functools.partial(direction_kernel, examples),
        (shape((devices, lines, LANES), f32), small, small, small, small),
        [SM, SM] + [VM] * 10,
        (VM,) * 5,
        [
            pltpu.VMEM((local_w, rank2), f32),
            pltpu.VMEM((width, rank2), f32),
            pltpu.VMEM((3, width // groups, rank2), f32),
        ],
    )(
        where, fixes, got, loss, down_maps, adapter_up_maps, *moments,
        turned(down_privacy_noise), turned(up_privacy_noise),
    )
    spread = exchange(tile)
    down_shape = shape(moments[0].shape, f32)
    up_shape = shape(moments[2].shape, f32)
    loss_mean, dm1, dm2, dw, bm1, bm2, bw, table = call(
        functools.partial(update_kernel, examples, shards),
        (
            shape((1, 1), f32), down_shape, down_shape, down_shape, up_shape, up_shape, up_shape,
            shape((2, 4), f32),
        ),
        [SM, SM] + [VM] * 8,
        (VM,) * 8,
        [pltpu.VMEM((width, rank2), f32)],
    )(where, fixes, spread, down_maps, moments[0], moments[1], um1, um2, direction, weight)
    return (
        loss_mean.reshape(()),
        norm[0, 0:1],
        turned(dm1),
        turned(dm2),
        turned(dw),
        turned(bm1),
        turned(bm2),
        turned(bw),
        table.T,
    )


def solution(mesh):
    placed = (
        P("dp", None),
        P("dp"),
        P("dp"),
        P(),
        P("dp", "head"),
        P(),
        P(None, None, "head"),
        P("head", None),
        P(None, "head"),
        P("head", None),
        P(),
        P(),
        P(),
        P(),
        P(None, None, "head"),
        P(None, "dp", None),
        P(None, "dp", None),
        P(None, None, ("head", "dp")),
        P(None, None, ("head", "dp")),
        P(None, "dp", None),
        P(None, None, ("head", "dp")),
    )
    return jax.shard_map(
        per_device,
        mesh=mesh,
        in_specs=placed,
        out_specs=(
            P(),
            P(("dp", "head")),
            P(None, "dp", None),
            P(None, "dp", None),
            P(None, "dp", None),
            P(None, None, ("head", "dp")),
            P(None, None, ("head", "dp")),
            P(None, None, ("head", "dp")),
            P(),
        ),
        check_vma=False,
    )
```

```python
import functools

import jax
import jax.numpy as jnp
from jax import lax
from jax.experimental import pallas as pl
from jax.experimental.pallas import tpu as pltpu
from jax.sharding import PartitionSpec as P

HDIM = 64
CAP = 48
GROUPS = 16
BAND = 128
LANES = 128
MIB = 1 << 20

adapter_scale = 2.0
clip_bound = 1.0
noise_mult = 0.6
smooth_rate = 0.1
beta_one = 0.9
beta_two = 0.999
adam_eps = 1e-06
decay_rate = 0.01
learn_rate = 0.25
norm_eps = 1e-05

f32 = jnp.float32
bf16 = jnp.bfloat16
i32 = jnp.int32
LAST = (((1,), (1,)), ((), ()))
FIRST = (((0,), (0,)), ((), ()))
ALL = ("dp", "head")
VM = pl.BlockSpec(memory_space=pltpu.VMEM)
SM = pl.BlockSpec(memory_space=pltpu.SMEM)
ANY = pl.BlockSpec(memory_space=pl.ANY)


def iota(shape, axis):
    return lax.broadcasted_iota(i32, shape, axis)


def mm(a, b):
    return jnp.dot(a, b, preferred_element_type=f32)


def mm_last(a, b):
    return lax.dot_general(a, b, LAST, preferred_element_type=f32)


def call(kernel, outs, in_specs, out_specs, scratch=(), vmem=32, flops=1):
    return pl.pallas_call(
        kernel,
        out_shape=outs,
        in_specs=in_specs,
        out_specs=out_specs,
        scratch_shapes=list(scratch),
        compiler_params=pltpu.CompilerParams(vmem_limit_bytes=vmem * MIB),
        cost_estimate=pl.CostEstimate(flops=flops, bytes_accessed=1, transcendentals=0),
    )


def request_kernel(owners, peers, owned, sc_ref, len_ref, ids_ref, req_ref, slot_ref):
    me = sc_ref[0]
    base = (sc_ref[1] * CAP).astype(f32)
    count = len_ref[me]
    ids = ids_ref[...].astype(f32)
    examples, slots = ids.shape
    row = jnp.sum(jnp.where(iota(ids.shape, 0) == me, ids, 0.0), 0, keepdims=True)
    flipped = ids.T
    col = jnp.sum(jnp.where(iota(flipped.shape, 1) == me, flipped, 0.0), 1, keepdims=True)
    t_col = iota((slots, slots), 0)
    t_row = iota((slots, slots), 1)
    valid_col = (iota((slots, 1), 0) < count).astype(f32)
    valid_row = (iota((1, slots), 1) < count).astype(f32)
    own_col = sum((col >= k * owned).astype(f32) for k in range(1, owners))
    own_row = sum((row >= k * owned).astype(f32) for k in range(1, owners))
    same = (col == row) & (t_row < count) & (t_col < count)
    before = t_row < t_col
    after = t_col < t_row
    seen_col = jnp.sum(jnp.where(same & before, 1.0, 0.0), 1, keepdims=True)
    seen_row = jnp.sum(jnp.where(same & after, 1.0, 0.0), 0, keepdims=True)
    first_col = jnp.where(seen_col == 0.0, valid_col, 0.0)
    first_row = jnp.where(seen_row == 0.0, valid_row, 0.0)
    shared = own_col == own_row
    place_col = jnp.sum(jnp.where(shared & before, first_row, 0.0), 1, keepdims=True)
    place_row = jnp.sum(jnp.where(shared & after, first_col, 0.0), 0, keepdims=True)
    rank = jnp.sum(jnp.where(same, first_row * place_row, 0.0), 1, keepdims=True)
    local = rank - base
    here = (local >= 0.0) & (local < CAP) & (valid_col > 0.0)
    slot = jnp.where(here, own_col * CAP + local, -1.0)
    slot_ref[...] = jnp.broadcast_to(slot, slot_ref.shape).astype(i32)
    rounds = jnp.floor(jnp.max(rank, 0, keepdims=True) * (1.0 / CAP) + 0.5 / CAP) + 1.0
    lane = iota((slots, LANES), 1)
    lane_f = lane.astype(f32)
    wanted = jnp.where(first_col > 0.0, place_col - base, -1.0)
    hit = (wanted == lane_f) & (lane < CAP)
    lane_row = iota((1, LANES), 1)
    for owner in range(owners):
        chosen = jnp.where(hit & (own_col == float(owner)), col - float(owner * owned), 0.0)
        line = jnp.sum(chosen, 0, keepdims=True)
        line = jnp.where(lane_row == LANES - 1, rounds, line).astype(i32)
        for peer in range(peers):
            req_ref[owner * peers + peer] = line


def lookup_kernel(want_ref, table_ref, out_ref, wide_ref, stage_ref):
    wide_ref[...] = table_ref[...].astype(f32)

    def one(src, carry):
        for p in range(CAP):
            stage_ref[p : p + 1, :] = wide_ref[pl.ds(want_ref[src, 0, p], 1), :]
        out_ref[src] = stage_ref[...].astype(bf16)
        return carry

    lax.fori_loop(0, want_ref.shape[0], one, 0)


def assemble_kernel(owners, peers, got_ref, slot_ref, emb_ref, rows_ref):
    for owner in range(owners):
        for peer in range(peers):
            rows_ref[owner * CAP : (owner + 1) * CAP, peer * LANES : (peer + 1) * LANES] = got_ref[
                owner * peers + peer
            ]
    slot = slot_ref[...]
    lane = iota(slot.shape, 1)
    picks = [
        (slot == lane + first).astype(f32).astype(bf16)
        for first in range(0, owners * CAP, LANES)
    ]
    emb_ref[...] = mm(jnp.concatenate(picks, 1), rows_ref[...]).astype(bf16)


def pack_kernel(at_ref, in_ref, out_ref, att_ref, pack_ref, sems):
    at = at_ref[0]
    wide = in_ref.shape[1]
    in_rows, out_rows = in_ref.shape[0] // GROUPS, out_ref.shape[0] // GROUPS
    att_rows = 2 * att_ref.shape[0] // GROUPS
    here = lambda rows: pl.ds(pl.multiple_of(at * rows, rows), rows)
    moves = [(in_ref.at[here(in_rows), :], pack_ref.at[pl.ds(0, in_rows), :])]
    row = in_rows
    for first in range(0, 2 * wide, wide):
        moves.append((out_ref.at[here(out_rows), pl.ds(first, wide)], pack_ref.at[pl.ds(row, out_rows), :]))
        row += out_rows
    half = att_ref.at[
        pl.ds(pl.multiple_of(at // 2 * att_rows, att_rows), att_rows),
        pl.ds(pl.multiple_of(at % 2 * wide, wide), wide),
    ]
    moves.append((half, pack_ref.at[pl.ds(row, att_rows), :]))
    copies = [pltpu.make_async_copy(source, target, sems.at[n]) for n, (source, target) in enumerate(moves)]
    for one in copies:
        one.start()
    for one in copies:
        one.wait()


def normalize(inputs):
    centre = inputs - jnp.mean(inputs, -1, keepdims=True)
    inv_std = lax.rsqrt(jnp.mean(centre * centre, -1, keepdims=True) + norm_eps)
    return centre * inv_std, inv_std


def norm_back(scaled, x_hat, inv_std):
    return inv_std * (
        scaled
        - jnp.mean(scaled, -1, keepdims=True)
        - x_hat * jnp.mean(scaled * x_hat, -1, keepdims=True)
    )


def halves(pair):
    low = iota(pair.shape, 1) < HDIM
    zero = jnp.zeros_like(pair)
    return jnp.where(low, pair, zero), jnp.where(low, zero, pair)


def flip(x):
    return x.astype(f32).T


def rows_of(shards, width):
    in_rows = width // GROUPS
    return in_rows, in_rows // 2, 2 * width // shards // GROUPS


def project_kernel(
    shards, emb_ref, pos_ref, gain_ref, bias_ref, down_ref, w_own, w_peer,
    x_ref, xb_ref, xa_ref, q_ref, k_ref, v_ref,
    w_buf, up_buf, sems,
):
    slots, width = emb_ref.shape
    rank = down_ref.shape[1]
    rank2 = 2 * rank
    three = 3 * LANES
    copies = []
    up_buf[...] = jnp.zeros_like(up_buf)
    for pair in range(shards // 2):
        mine = []
        for side, w_ref in enumerate((w_own, w_peer)):
            for part in range(3):
                mine.append(
                    pltpu.make_async_copy(
                        w_ref.at[pair, pl.ds(part * width, width), :],
                        w_buf.at[pair, :, pl.ds(side * three + part * LANES, LANES)],
                        sems.at[pair, side * 5 + part],
                    )
                )
            for part in range(2):
                mine.append(
                    pltpu.make_async_copy(
                        w_ref.at[pair, pl.ds(3 * width + part * rank, rank), :],
                        up_buf.at[pair, pl.ds(part * rank, rank), pl.ds(side * three + 2 * part * LANES, LANES)],
                        sems.at[pair, side * 5 + 3 + part],
                    )
                )
        copies.append(mine)
    for mine in copies:
        for one in mine:
            one.start()
    x_hat, unused_std = normalize(emb_ref[...].astype(f32) + pos_ref[...].astype(f32))
    x0 = x_hat * gain_ref[0:1, :] + bias_ref[0:1, :]
    x_ref[...] = x0
    xb_ref[...] = x0.astype(bf16)
    xa = mm_last(xb_ref[...], down_ref[...].reshape(rank2, width).astype(bf16)).astype(bf16)
    xa_ref[...] = xa
    twice = xa * jnp.asarray(adapter_scale, bf16)
    for pair in range(shards // 2):
        for one in copies[pair]:
            one.wait()
        total = mm(xb_ref[...], w_buf[pair]) + mm(twice, up_buf[pair])
        for side in range(2):
            first = side * three
            q_ref[2 * pair + side] = (total[:, first : first + LANES] * (HDIM**-0.5)).astype(bf16)
            k_ref[2 * pair + side] = total[:, first + LANES : first + 2 * LANES].astype(bf16)
            v_ref[2 * pair + side] = total[:, first + 2 * LANES : first + three].astype(bf16)


def attend_kernel(shards, len_ref, order_ref, q_ref, k_ref, v_ref, lse_ref, ctx_ref, lse_cols):
    slots = q_ref.shape[1]
    count = len_ref[0]
    block = slots
    keep = iota((block, slots), 1) < count
    lane = iota((block, LANES), 1)

    def one_pair(j, carry):
        k = k_ref[j]
        v_sides = halves(v_ref[j])
        columns = pl.ds(pl.multiple_of(order_ref[j] * LANES, LANES), LANES)
        for first in range(0, slots, block):
            band = slice(first, first + block)
            q_sides = halves(q_ref[j, band, :])
            both = jnp.zeros((block, LANES), f32)
            for side in range(2):
                s = jnp.where(keep, mm_last(q_sides[side], k), -1e30)
                top = jnp.max(s, 1, keepdims=True)
                e = jnp.exp(s - top)
                total = jnp.sum(e, 1, keepdims=True)
                both = both + mm((e * (1.0 / total)).astype(bf16), v_sides[side])
                lse_cols[band, :] = jnp.where(lane == 2 * j + side, top + jnp.log(total), lse_cols[band, :])
            ctx_ref[band, columns] = both.astype(bf16)
        return carry

    lax.fori_loop(0, shards, one_pair, 0, unroll=2)
    lse_ref[...] = lse_cols[...].T[: 2 * shards].reshape(lse_ref.shape)


def gelu_parts(x):
    size = jnp.abs(x)
    t = 1.0 / (1.0 + (0.3275911 * 0.5**0.5) * size)
    bell = jnp.exp2((-0.5 * 1.4426950408889634) * (x * x))
    tail = bell * t * (
        0.127414796
        + t * (-0.142248368 + t * (0.7107068705 + t * (-0.7265760135 + t * 0.5307027145)))
    )
    cdf = jnp.where(x < 0.0, tail, 1.0 - tail)
    return x * cdf, cdf + x * (bell * 0.3989422804014327)


def middle_kernel(
    shards, len_ref, label_ref, x_ref, ctx_ref, gain_ref, bias_ref, class_ref, w_ref,
    dctx_ref, loss_ref,
    wo_buf, wi_buf, wf_buf, slope_buf, acc_ref, h_ref, hb_ref, hat_ref, df_ref, g_two, sems,
):
    slots, width = x_ref.shape
    classes = class_ref.shape[0]
    units = wi_buf.shape[-1]
    in_rows, out_rows, att_rows = rows_of(shards, width)
    start = in_rows + 2 * out_rows
    copies = []
    for shard in range(shards):
        mine = [
            pltpu.make_async_copy(w_ref.at[shard, :, pl.ds(0, in_rows), :], wi_buf.at[shard], sems.at[shard, 0])
        ]
        for side in range(2):
            cols = pl.ds(side * units, units)
            mine.append(
                pltpu.make_async_copy(
                    w_ref.at[shard, :, pl.ds(in_rows + side * out_rows, out_rows), :],
                    wf_buf.at[shard, :, :, cols],
                    sems.at[shard, 1 + side],
                )
            )
        copies.append(mine)
    wo_copies = []
    for place in range(GROUPS):
        wo_copies.append(
            pltpu.make_async_copy(
                w_ref.at[:, place, pl.ds(start, att_rows), :],
                wo_buf.at[:, place // 2, :, pl.ds(place % 2 * units, units)],
                sems.at[place % shards, 3 + place // shards],
            )
        )
    for one in wo_copies:
        one.start()
    for mine in copies:
        for one in mine:
            one.start()
    count = len_ref[0]
    count_f = count.astype(f32)
    label = label_ref[0]
    for one in wo_copies:
        one.wait()
    hat1, std1 = normalize(x_ref[...] + mm(ctx_ref[...], wo_buf[...].reshape(width, width)))
    hat_ref[...] = hat1
    h1 = hat1 * gain_ref[1:2, :] + bias_ref[1:2, :]
    h_ref[...] = h1
    hb_ref[...] = h1.astype(bf16)
    for f in range(shards):
        for one in copies[f]:
            one.wait()
        for top in range(0, slots, BAND):
            band = slice(top, top + BAND)
            g, slope = gelu_parts(mm(hb_ref[band, :], wi_buf[f].reshape(width, units)))
            slope_buf[f, band, :] = slope
            g_two[band, (f % 2) * units : (f % 2 + 1) * units] = g.astype(bf16)
        if f % 2:
            part = mm(g_two[...], wf_buf[f - 1 : f + 1].reshape(2 * units, width))
            if f == 1:
                acc_ref[...] = h_ref[...] + part
            else:
                acc_ref[...] += part
    hat2, std2 = normalize(acc_ref[...])
    gain2 = gain_ref[2:3, :]
    valid = (iota((slots, 1), 0) < count).astype(f32)
    pooled = jnp.sum((hat2 * gain2 + bias_ref[2:3, :]) * valid, 0, keepdims=True) / count_f
    weights = class_ref[...].astype(f32)
    logits = jnp.sum(pooled.astype(bf16).astype(f32) * weights, 1, keepdims=True)
    shifted = logits - jnp.max(logits, 0, keepdims=True)
    log_prob = shifted - jnp.log(jnp.sum(jnp.exp(shifted), 0, keepdims=True))
    target = (1.0 - smooth_rate) * (iota((classes, 1), 0) == label).astype(f32) + smooth_rate / classes
    loss_ref[...] = jnp.broadcast_to(-jnp.sum(target * log_prob, 0, keepdims=True), loss_ref.shape)
    d_pooled = jnp.sum((jnp.exp(log_prob) - target) * weights, 0, keepdims=True) / count_f
    d_two = norm_back((d_pooled * gain2) * valid, hat2, std2)
    acc_ref[...] = d_two
    df_ref[...] = d_two.astype(bf16)
    for f in range(shards):
        d_pre = (mm_last(df_ref[...], wf_buf[f].reshape(units, width)) * slope_buf[f]).astype(bf16)
        acc_ref[...] += mm_last(d_pre, wi_buf[f].reshape(width, units))
    d_attn = norm_back(acc_ref[...] * gain_ref[1:2, :], hat_ref[...], std1).astype(bf16)
    dctx_ref[...] = mm_last(d_attn, wo_buf[...].reshape(width, width)).astype(bf16)


def gradient_kernel(
    shards, groups, len_ref, order_ref, xb_ref, xa_ref, q_ref, k_ref, v_ref, lse_ref, dctx_ref, w_own, w_peer,
    send_ref, norm_ref,
    up_buf, up_grad, inner_ref, sems,
):
    slots, width = xb_ref.shape
    rank2 = xa_ref.shape[1]
    rank = rank2 // 2
    copies = [
        pltpu.make_async_copy(
            (w_own, w_peer)[j % 2].at[j // 2, pl.ds(3 * width, rank2), :], up_buf.at[j], sems.at[j]
        )
        for j in range(shards)
    ]
    for one in copies:
        one.start()
    count = len_ref[0]
    block = slots // 1
    keep = iota((slots, block), 0) < count
    xa = xa_ref[...]
    low = iota((LANES, rank2), 1) < rank
    upper = iota((rank2, LANES), 0) < rank
    rows = width // (groups * shards)
    part = rows // 2
    inner_ref[...] = jnp.zeros_like(inner_ref)
    for one in copies:
        one.wait()

    def one_pair(j, carry):
        k = k_ref[j]
        k_sides = halves(k)
        v_sides = halves(v_ref[j])
        shard = order_ref[j]
        columns = pl.ds(pl.multiple_of(shard * LANES, LANES), LANES)
        dv = jnp.zeros((slots, LANES), f32)
        found = []
        for first in range(0, slots, block):
            band = slice(first, first + block)
            q = q_ref[j, band, :]
            dctx = dctx_ref[band, columns]
            dctx_sides = halves(dctx)
            parts = []
            for side in range(2):
                s = jnp.where(keep, mm_last(k_sides[side], q), -1e30)
                prob = jnp.exp(s - lse_ref[j, side : side + 1, band])
                d_prob = mm_last(v_sides[side], dctx)
                weighted = jnp.sum(prob * d_prob, 0, keepdims=True)
                d_s = (prob * (d_prob - weighted)).astype(bf16)
                dv = dv + mm(prob.astype(bf16), dctx_sides[side])
                parts.append(lax.dot_general(d_s, k_sides[side], FIRST, preferred_element_type=f32))
            found.append(parts[0] + parts[1])
        dq = (jnp.concatenate(found, 0) * (HDIM**-0.5)).astype(bf16)
        dq_flip = flip(dq).astype(bf16)
        dv = dv.astype(bf16)
        grad = adapter_scale * jnp.where(low, mm(dq_flip, xa), mm(flip(dv).astype(bf16), xa))
        for i in range(groups):
            at = pl.multiple_of((i * shards + shard) * rows, rows)
            up_grad[pl.ds(at, rows), :] = grad[i * rows : (i + 1) * rows]
        up = up_buf[j]
        zero = jnp.zeros_like(up)
        up = jnp.concatenate([jnp.where(upper, up, zero), jnp.where(upper, zero, up)], 1)
        inner_ref[...] += adapter_scale * mm_last(jnp.concatenate([dq, dv], 1), up)
        return carry

    lax.fori_loop(0, shards, one_pair, 0, unroll=2)
    down_grad = mm(flip(inner_ref[...].astype(bf16)).astype(bf16), xb_ref[...]).T
    both = jnp.concatenate([up_grad[...], down_grad], 1)
    squares = jnp.sum(jnp.sum(both * both, 1, keepdims=True), 0, keepdims=True)
    norm = jnp.sqrt(squares)
    norm_ref[...] = jnp.broadcast_to(norm, norm_ref.shape)
    both = both * (clip_bound / jnp.maximum(norm, clip_bound))
    both = jnp.concatenate([both, pltpu.roll(both, width - part, 0)], 1)
    for to in range(groups * shards):
        send_ref[to] = both[to * rows : to * rows + part, :]


def lamb(weight, grad, first, second, fix_one, fix_two):
    first_new = beta_one * first + (1.0 - beta_one) * grad
    second_new = beta_two * second + (1.0 - beta_two) * grad * grad
    direction = first_new / fix_one / (jnp.sqrt(second_new / fix_two) + adam_eps) + decay_rate * weight
    return first_new, second_new, direction


def side_by_side(ref):
    return jnp.concatenate([ref[0], ref[1]], 1)


def flipped(ref):
    maps, rank, cols = ref.shape
    return ref[...].reshape(maps * rank, cols).T


def direction_kernel(
    examples, sc_ref, fix_ref, got_ref, loss_ref, down_ref, up_ref, dm1_ref, dm2_ref, um1_ref, um2_ref,
    dn_ref, un_ref,
    tile_ref, um1_out, um2_out, dir_ref, w_out, up_turn, down_turn, part_turn,
):
    dp_at, head_at = sc_ref[0], sc_ref[1]
    rank2 = up_turn.shape[1]
    rows = got_ref.shape[1] * LANES // (2 * rank2)
    up_at = pl.multiple_of(dp_at * rows, rows)
    at = pl.multiple_of(head_at * rows, rows)
    down_at = pl.multiple_of(dp_at * dm1_ref.shape[2] + head_at * rows, rows)
    up_turn[...] = flipped(up_ref)
    down_turn[...] = flipped(down_ref)
    for n, ref in enumerate((dn_ref, dm1_ref, dm2_ref)):
        part_turn[n] = flipped(ref)
    here = pl.ds(at, rows)
    weight = jnp.concatenate([up_turn[pl.ds(up_at, rows), :], down_turn[pl.ds(down_at, rows), :]], 1)
    noise = jnp.concatenate([side_by_side(un_ref), part_turn[0, here, :]], 1)
    first = jnp.concatenate([side_by_side(um1_ref), part_turn[1, here, :]], 1)
    second = jnp.concatenate([side_by_side(um2_ref), part_turn[2, here, :]], 1)
    total = jnp.sum(got_ref[...], 0)
    total = jnp.concatenate([total[:, : 2 * rank2], total[:, 2 * rank2 :]], 0)
    grad = (total + noise_mult * clip_bound * noise) / examples
    first_new, second_new, direction = lamb(weight, grad, first, second, fix_ref[0], fix_ref[1])
    um1_out[...] = first_new
    um2_out[...] = second_new
    dir_ref[...] = direction
    w_out[...] = weight
    down_grad = grad[:, rank2:]
    per_line = LANES // rank2
    lines = [
        jnp.concatenate([down_grad[k : k + 1] for k in range(line, line + per_line)], 1)
        for line in range(0, rows, per_line)
    ]
    lines.append(
        jnp.concatenate(
            [jnp.sum(direction * direction, 0, keepdims=True), jnp.sum(weight * weight, 0, keepdims=True)], 1
        )
    )
    lines.append(loss_ref[...])
    tile = jnp.concatenate(lines, 0)
    for to in range(tile_ref.shape[0]):
        tile_ref[to] = tile


def update_kernel(
    examples, shards, sc_ref, fix_ref, got_ref, down_ref, dm1_ref, dm2_ref, um1_ref, um2_ref, dir_ref, w_ref,
    loss_ref, dm1_out, dm2_out, dw_out, um1_out, um2_out, uw_out, table_ref, down_turn,
):
    dp_at = sc_ref[0]
    rows = w_ref.shape[0]
    rank2 = w_ref.shape[1] // 2
    rank = rank2 // 2
    per_line = LANES // rank2
    lines = rows // per_line
    total = jnp.sum(got_ref[...], 0)
    loss_ref[...] = total[lines + 1 : lines + 2, 0:1] / examples
    stats = total[lines : lines + 1, :]
    lane = iota(stats.shape, 1)

    def part(group):
        inside = (lane >= group * rank) & (lane < (group + 1) * rank)
        return jnp.sqrt(jnp.sum(jnp.where(inside, stats, 0.0), 1, keepdims=True))

    norms = [(part(group + 4), part(group)) for group in range(4)]
    for out_col, group in enumerate((2, 3, 0, 1)):
        table_ref[:, out_col : out_col + 1] = jnp.concatenate(norms[group], 0)

    def rate(a, b):
        wide = iota((1, rank2), 1) < rank
        return learn_rate * jnp.where(wide, norms[a][0] / norms[a][1], norms[b][0] / norms[b][1])

    up_new = w_ref[:, :rank2] - rate(0, 1) * dir_ref[:, :rank2]
    for ref, value in ((uw_out, up_new), (um1_out, um1_ref[...]), (um2_out, um2_ref[...])):
        ref[0] = value[:, :rank]
        ref[1] = value[:, rank:rank2]
    grad = jnp.concatenate(
        [
            got_ref[dp_at * shards + j, k // per_line, (k % per_line) * rank2 : (k % per_line + 1) * rank2]
            .reshape(1, rank2)
            for j in range(shards)
            for k in range(rows)
        ],
        0,
    )
    many = dm1_ref.shape[2]
    down_turn[...] = flipped(down_ref)
    weight = down_turn[pl.ds(pl.multiple_of(dp_at * many, many), many), :]
    first_new, second_new, direction = lamb(
        weight, grad, flipped(dm1_ref), flipped(dm2_ref), fix_ref[0], fix_ref[1]
    )
    new = weight - rate(2, 3) * direction
    for ref, value in ((dm1_out, first_new), (dm2_out, second_new), (dw_out, new)):
        ref[...] = value.T.reshape(ref.shape)


def per_device(
    slot_token_ids,
    lengths,
    labels,
    optimizer_step_count,
    token_embedding_table,
    positions,
    query_key_value_weight,
    attention_output_weight,
    feedforward_input_weight,
    feedforward_output_weight,
    layer_norm_gains,
    layer_norm_biases,
    classifier,
    adapter_down_maps,
    adapter_up_maps,
    down_first_moment,
    down_second_moment,
    up_first_moment,
    up_second_moment,
    down_privacy_noise,
    up_privacy_noise,
):
    shards = lax.axis_size("head")
    groups = lax.axis_size("dp")
    devices = shards * groups
    dp_at = lax.axis_index("dp")
    head_at = lax.axis_index("head")
    slots, width = positions.shape
    rank = adapter_down_maps.shape[2]
    rank2 = 2 * rank
    units = feedforward_output_weight.shape[0]
    local_w = attention_output_weight.shape[0]
    owned = token_embedding_table.shape[0]
    shape = jax.ShapeDtypeStruct

    def turned(x):
        return jnp.swapaxes(x, 1, 2)

    down_maps = turned(adapter_down_maps)

    def ask(which, slot_token_ids):
        return call(
            functools.partial(request_kernel, groups, shards, owned),
            (shape((devices, 1, LANES), i32), shape((slots, LANES), i32)),
            [SM, SM, VM],
            (VM, VM),
        )(jnp.stack([head_at, which]).astype(i32), lengths, slot_token_ids)

    def look(wanted):
        return call(
            lookup_kernel,
            shape((devices, CAP, LANES), bf16),
            [SM, VM],
            VM,
            [pltpu.VMEM((owned, LANES), f32), pltpu.VMEM((CAP, LANES), f32)],
            flops=10**10,
        )(wanted, token_embedding_table)

    def place(found, slot):
        got = exchange(found)
        emb = call(
            functools.partial(assemble_kernel, groups, shards),
            shape((slots, width), bf16),
            [VM, VM],
            VM,
            [pltpu.VMEM((groups * CAP, width), bf16)],
            flops=2 * 10**10,
        )(got, slot)
        return emb

    def exchange(x):
        return lax.all_to_all(x, ALL, 0, 0, tiled=True)

    pack = call(
        pack_kernel,
        shape((width // GROUPS * 2 + 2 * width // shards // GROUPS, units), bf16),
        [SM, ANY, ANY, ANY],
        VM,
        [pltpu.SemaphoreType.DMA((4,))],
        vmem=60,
    )(
        dp_at.reshape(1).astype(i32), feedforward_input_weight, feedforward_output_weight,
        attention_output_weight,
    )
    pack, slot_token_ids = lax.optimization_barrier((pack, slot_token_ids))
    weights = lax.all_gather(pack, ("head", "dp"), axis=0, tiled=True).reshape(shards, groups, *pack.shape)

    steps = shards // 2
    packed = jnp.concatenate(
        [
            query_key_value_weight.reshape(3 * width, local_w),
            adapter_up_maps.reshape(rank2, local_w).astype(bf16),
        ],
        0,
    )
    order = jnp.stack(
        [
            2 * ((head_at // 2 + step) % steps) + (head_at + column) % 2
            for step in range(steps)
            for column in range(2)
        ]
    ).astype(i32)

    def permuted(x, source):
        return lax.ppermute(x, "head", [(source(i), i) for i in range(shards)])

    packed_z = [permuted(packed, lambda i, step=step: (i + 2 * step) % shards) for step in range(1, steps)]
    requests, slot = ask(jnp.zeros((), i32), slot_token_ids)

    wanted = exchange(requests)
    rounds = jnp.max(wanted[:, 0, LANES - 1])
    wanted, packed_z = lax.optimization_barrier((wanted, packed_z))
    found = look(wanted)
    w_own = jnp.stack([packed, *packed_z])
    w_peer = permuted(w_own, lambda i: i ^ 1)
    emb = place(found, slot)

    def again(which):
        asked, where = ask(which, slot_token_ids)
        return place(look(exchange(asked)), where)

    unused_at, emb = lax.while_loop(
        lambda state: state[0] < rounds,
        lambda state: (state[0] + 1, state[1] + again(state[0])),
        (jnp.ones((), i32), emb),
    )

    own_len = lax.dynamic_slice_in_dim(lengths, head_at, 1)
    own_label = lax.dynamic_slice_in_dim(labels, head_at, 1)
    x0, x0b, xa, q, k, v = call(
        functools.partial(project_kernel, shards),
        (
            shape((slots, width), f32),
            shape((slots, width), bf16),
            shape((slots, rank2), bf16),
            shape((shards, slots, LANES), bf16),
            shape((shards, slots, LANES), bf16),
            shape((shards, slots, LANES), bf16),
        ),
        [VM, VM, VM, VM, VM, ANY, ANY],
        (VM,) * 6,
        [
            pltpu.VMEM((shards // 2, width, 6 * LANES), bf16),
            pltpu.VMEM((shards // 2, rank2, 6 * LANES), bf16),
            pltpu.SemaphoreType.DMA((shards // 2, 10)),
        ],
        vmem=50,
    )(emb, positions, layer_norm_gains, layer_norm_biases, down_maps, w_own, w_peer)
    lse, ctx = call(
        functools.partial(attend_kernel, shards),
        (shape((shards, 2, slots), f32), shape((slots, width), bf16)),
        [SM, SM, VM, VM, VM],
        (VM, VM),
        [pltpu.VMEM((slots, LANES), f32)],
        vmem=40,
    )(own_len, order, q, k, v)

    dctx, loss = call(
        functools.partial(middle_kernel, shards),
        (shape((slots, width), bf16), shape((1, LANES), f32)),
        [SM, SM, VM, VM, VM, VM, VM, ANY],
        (VM, VM),
        [
            pltpu.VMEM((shards, groups // 2, 2 * local_w // groups, width), bf16),
            pltpu.VMEM((shards, groups, width // groups, units), bf16),
            pltpu.VMEM((shards, groups, units // groups, width), bf16),
            pltpu.VMEM((shards, slots, units), f32),
            pltpu.VMEM((slots, width), f32),
            pltpu.VMEM((slots, width), f32),
            pltpu.VMEM((slots, width), bf16),
            pltpu.VMEM((slots, width), f32),
            pltpu.VMEM((slots, width), bf16),
            pltpu.VMEM((slots, 2 * units), bf16),
            pltpu.SemaphoreType.DMA((shards, 5)),
        ],
        vmem=60,
    )(
        own_len, own_label, x0, ctx, layer_norm_gains, layer_norm_biases, classifier, weights
    )

    send, norm = call(
        functools.partial(gradient_kernel, shards, groups),
        (shape((devices, 2 * rank2 * width // devices // LANES, LANES), f32), shape((1, LANES), f32)),
        [SM, SM, VM, VM, VM, VM, VM, VM, VM, ANY, ANY],
        (VM, VM),
        [
            pltpu.VMEM((shards, rank2, LANES), bf16),
            pltpu.VMEM((width, rank2), f32),
            pltpu.VMEM((slots, rank2), f32),
            pltpu.SemaphoreType.DMA((shards,)),
        ],
        vmem=50,
    )(own_len, order, x0b, xa, q, k, v, lse, dctx, w_own, w_peer)

    got = exchange(send)
    examples = float(devices)
    step_number = optimizer_step_count.astype(f32)
    fixes = jnp.stack([1.0 - jnp.power(beta_one, step_number), 1.0 - jnp.power(beta_two, step_number)])
    where = jnp.stack([dp_at, head_at]).astype(i32)
    rows = width // devices
    small = shape((rows, 2 * rank2), f32)
    moments = [turned(x) for x in (down_first_moment, down_second_moment, up_first_moment, up_second_moment)]
    lines = rows * rank2 // LANES + 2
    tile, um1, um2, direction, weight = call(
        functools.partial(direction_kernel, examples),
        (shape((devices, lines, LANES), f32), small, small, small, small),
        [SM, SM] + [VM] * 10,
        (VM,) * 5,
        [
            pltpu.VMEM((local_w, rank2), f32),
            pltpu.VMEM((width, rank2), f32),
            pltpu.VMEM((3, width // groups, rank2), f32),
        ],
    )(
        where, fixes, got, loss, down_maps, adapter_up_maps, *moments,
        turned(down_privacy_noise), turned(up_privacy_noise),
    )
    spread = exchange(tile)
    down_shape = shape(moments[0].shape, f32)
    up_shape = shape(moments[2].shape, f32)
    loss_mean, dm1, dm2, dw, bm1, bm2, bw, table = call(
        functools.partial(update_kernel, examples, shards),
        (
            shape((1, 1), f32), down_shape, down_shape, down_shape, up_shape, up_shape, up_shape,
            shape((2, 4), f32),
        ),
        [SM, SM] + [VM] * 8,
        (VM,) * 8,
        [pltpu.VMEM((width, rank2), f32)],
    )(where, fixes, spread, down_maps, moments[0], moments[1], um1, um2, direction, weight)
    return (
        loss_mean.reshape(()),
        norm[0, 0:1],
        turned(dm1),
        turned(dm2),
        turned(dw),
        turned(bm1),
        turned(bm2),
        turned(bw),
        table.T,
    )


def solution(mesh):
    placed = (
        P("dp", None),
        P("dp"),
        P("dp"),
        P(),
        P("dp", "head"),
        P(),
        P(None, None, "head"),
        P("head", None),
        P(None, "head"),
        P("head", None),
        P(),
        P(),
        P(),
        P(),
        P(None, None, "head"),
        P(None, "dp", None),
        P(None, "dp", None),
        P(None, None, ("head", "dp")),
        P(None, None, ("head", "dp")),
        P(None, "dp", None),
        P(None, None, ("head", "dp")),
    )
    return jax.shard_map(
        per_device,
        mesh=mesh,
        in_specs=placed,
        out_specs=(
            P(),
            P(("dp", "head")),
            P(None, "dp", None),
            P(None, "dp", None),
            P(None, "dp", None),
            P(None, None, ("head", "dp")),
            P(None, None, ("head", "dp")),
            P(None, None, ("head", "dp")),
            P(),
        ),
        check_vma=False,
    )
```

```python
import functools

import jax
import jax.numpy as jnp
from jax import lax
from jax.experimental import pallas as pl
from jax.experimental.pallas import tpu as pltpu
from jax.sharding import PartitionSpec as P

HDIM = 64
CAP = 48
GROUPS = 16
BAND = 128
LANES = 128
MIB = 1 << 20

adapter_scale = 2.0
clip_bound = 1.0
noise_mult = 0.6
smooth_rate = 0.1
beta_one = 0.9
beta_two = 0.999
adam_eps = 1e-06
decay_rate = 0.01
learn_rate = 0.25
norm_eps = 1e-05

f32 = jnp.float32
bf16 = jnp.bfloat16
i32 = jnp.int32
LAST = (((1,), (1,)), ((), ()))
FIRST = (((0,), (0,)), ((), ()))
ALL = ("dp", "head")
VM = pl.BlockSpec(memory_space=pltpu.VMEM)
SM = pl.BlockSpec(memory_space=pltpu.SMEM)
ANY = pl.BlockSpec(memory_space=pl.ANY)


def iota(shape, axis):
    return lax.broadcasted_iota(i32, shape, axis)


def mm(a, b):
    return jnp.dot(a, b, preferred_element_type=f32)


def mm_last(a, b):
    return lax.dot_general(a, b, LAST, preferred_element_type=f32)


def call(kernel, outs, in_specs, out_specs, scratch=(), vmem=32, flops=1):
    return pl.pallas_call(
        kernel,
        out_shape=outs,
        in_specs=in_specs,
        out_specs=out_specs,
        scratch_shapes=list(scratch),
        compiler_params=pltpu.CompilerParams(vmem_limit_bytes=vmem * MIB),
        cost_estimate=pl.CostEstimate(flops=flops, bytes_accessed=1, transcendentals=0),
    )


def request_kernel(owners, peers, owned, sc_ref, len_ref, ids_ref, req_ref, slot_ref):
    me = sc_ref[0]
    base = (sc_ref[1] * CAP).astype(f32)
    count = len_ref[me]
    ids = ids_ref[...].astype(f32)
    examples, slots = ids.shape
    row = jnp.sum(jnp.where(iota(ids.shape, 0) == me, ids, 0.0), 0, keepdims=True)
    flipped = ids.T
    col = jnp.sum(jnp.where(iota(flipped.shape, 1) == me, flipped, 0.0), 1, keepdims=True)
    t_col = iota((slots, slots), 0)
    t_row = iota((slots, slots), 1)
    valid_col = (iota((slots, 1), 0) < count).astype(f32)
    valid_row = (iota((1, slots), 1) < count).astype(f32)
    own_col = sum((col >= k * owned).astype(f32) for k in range(1, owners))
    own_row = sum((row >= k * owned).astype(f32) for k in range(1, owners))
    same = (col == row) & (t_row < count) & (t_col < count)
    before = t_row < t_col
    after = t_col < t_row
    seen_col = jnp.sum(jnp.where(same & before, 1.0, 0.0), 1, keepdims=True)
    seen_row = jnp.sum(jnp.where(same & after, 1.0, 0.0), 0, keepdims=True)
    first_col = jnp.where(seen_col == 0.0, valid_col, 0.0)
    first_row = jnp.where(seen_row == 0.0, valid_row, 0.0)
    shared = own_col == own_row
    place_col = jnp.sum(jnp.where(shared & before, first_row, 0.0), 1, keepdims=True)
    place_row = jnp.sum(jnp.where(shared & after, first_col, 0.0), 0, keepdims=True)
    rank = jnp.sum(jnp.where(same, first_row * place_row, 0.0), 1, keepdims=True)
    local = rank - base
    here = (local >= 0.0) & (local < CAP) & (valid_col > 0.0)
    slot = jnp.where(here, own_col * CAP + local, -1.0)
    slot_ref[...] = jnp.broadcast_to(slot, slot_ref.shape).astype(i32)
    rounds = jnp.floor(jnp.max(rank, 0, keepdims=True) * (1.0 / CAP) + 0.5 / CAP) + 1.0
    lane = iota((slots, LANES), 1)
    lane_f = lane.astype(f32)
    wanted = jnp.where(first_col > 0.0, place_col - base, -1.0)
    hit = (wanted == lane_f) & (lane < CAP)
    lane_row = iota((1, LANES), 1)
    for owner in range(owners):
        chosen = jnp.where(hit & (own_col == float(owner)), col - float(owner * owned), 0.0)
        line = jnp.sum(chosen, 0, keepdims=True)
        line = jnp.where(lane_row == LANES - 1, rounds, line).astype(i32)
        for peer in range(peers):
            req_ref[owner * peers + peer] = line


def lookup_kernel(want_ref, table_ref, out_ref, wide_ref, stage_ref):
    wide_ref[...] = table_ref[...].astype(f32)

    def one(src, carry):
        for p in range(CAP):
            stage_ref[p : p + 1, :] = wide_ref[pl.ds(want_ref[src, 0, p], 1), :]
        out_ref[src] = stage_ref[...].astype(bf16)
        return carry

    lax.fori_loop(0, want_ref.shape[0], one, 0)


def assemble_kernel(owners, peers, got_ref, slot_ref, emb_ref, rows_ref):
    for owner in range(owners):
        for peer in range(peers):
            rows_ref[owner * CAP : (owner + 1) * CAP, peer * LANES : (peer + 1) * LANES] = got_ref[
                owner * peers + peer
            ]
    slot = slot_ref[...]
    lane = iota(slot.shape, 1)
    picks = [
        (slot == lane + first).astype(f32).astype(bf16)
        for first in range(0, owners * CAP, LANES)
    ]
    emb_ref[...] = mm(jnp.concatenate(picks, 1), rows_ref[...]).astype(bf16)


def pack_kernel(at_ref, in_ref, out_ref, att_ref, pack_ref, sems):
    at = at_ref[0]
    wide = in_ref.shape[1]
    in_rows, out_rows = in_ref.shape[0] // GROUPS, out_ref.shape[0] // GROUPS
    att_rows = 2 * att_ref.shape[0] // GROUPS
    here = lambda rows: pl.ds(pl.multiple_of(at * rows, rows), rows)
    moves = [(in_ref.at[here(in_rows), :], pack_ref.at[pl.ds(0, in_rows), :])]
    row = in_rows
    for first in range(0, 2 * wide, wide):
        moves.append((out_ref.at[here(out_rows), pl.ds(first, wide)], pack_ref.at[pl.ds(row, out_rows), :]))
        row += out_rows
    half = att_ref.at[
        pl.ds(pl.multiple_of(at // 2 * att_rows, att_rows), att_rows),
        pl.ds(pl.multiple_of(at % 2 * wide, wide), wide),
    ]
    moves.append((half, pack_ref.at[pl.ds(row, att_rows), :]))
    copies = [pltpu.make_async_copy(source, target, sems.at[n]) for n, (source, target) in enumerate(moves)]
    for one in copies:
        one.start()
    for one in copies:
        one.wait()


def normalize(inputs):
    centre = inputs - jnp.mean(inputs, -1, keepdims=True)
    inv_std = lax.rsqrt(jnp.mean(centre * centre, -1, keepdims=True) + norm_eps)
    return centre * inv_std, inv_std


def norm_back(scaled, x_hat, inv_std):
    return inv_std * (
        scaled
        - jnp.mean(scaled, -1, keepdims=True)
        - x_hat * jnp.mean(scaled * x_hat, -1, keepdims=True)
    )


def halves(pair):
    low = iota(pair.shape, 1) < HDIM
    zero = jnp.zeros_like(pair)
    return jnp.where(low, pair, zero), jnp.where(low, zero, pair)


def flip(x):
    return x.astype(f32).T


def rows_of(shards, width):
    in_rows = width // GROUPS
    return in_rows, in_rows // 2, 2 * width // shards // GROUPS


def project_kernel(
    shards, emb_ref, pos_ref, gain_ref, bias_ref, down_ref, w_own, w_peer,
    x_ref, xb_ref, xa_ref, q_ref, k_ref, v_ref, up_ref,
    w_buf, up_buf, sems,
):
    slots, width = emb_ref.shape
    rank = down_ref.shape[1]
    rank2 = 2 * rank
    three = 3 * LANES
    copies = []
    up_buf[...] = jnp.zeros_like(up_buf)
    for pair in range(shards // 2):
        mine = []
        for side, w_ref in enumerate((w_own, w_peer)):
            for part in range(3):
                mine.append(
                    pltpu.make_async_copy(
                        w_ref.at[pair, pl.ds(part * width, width), :],
                        w_buf.at[pair, :, pl.ds(side * three + part * LANES, LANES)],
                        sems.at[pair, side * 5 + part],
                    )
                )
            for part in range(2):
                mine.append(
                    pltpu.make_async_copy(
                        w_ref.at[pair, pl.ds(3 * width + part * rank, rank), :],
                        up_buf.at[pair, pl.ds(part * rank, rank), pl.ds(side * three + 2 * part * LANES, LANES)],
                        sems.at[pair, side * 5 + 3 + part],
                    )
                )
        copies.append(mine)
    for mine in copies:
        for one in mine:
            one.start()
    x_hat, unused_std = normalize(emb_ref[...].astype(f32) + pos_ref[...].astype(f32))
    x0 = x_hat * gain_ref[0:1, :] + bias_ref[0:1, :]
    x_ref[...] = x0
    xb_ref[...] = x0.astype(bf16)
    xa = mm_last(xb_ref[...], down_ref[...].reshape(rank2, width).astype(bf16)).astype(bf16)
    xa_ref[...] = xa
    twice = xa * jnp.asarray(adapter_scale, bf16)
    for pair in range(shards // 2):
        for one in copies[pair]:
            one.wait()
        total = mm(xb_ref[...], w_buf[pair]) + mm(twice, up_buf[pair])
        for side in range(2):
            first = side * three
            q_ref[2 * pair + side] = (total[:, first : first + LANES] * (HDIM**-0.5)).astype(bf16)
            k_ref[2 * pair + side] = total[:, first + LANES : first + 2 * LANES].astype(bf16)
            v_ref[2 * pair + side] = total[:, first + 2 * LANES : first + three].astype(bf16)
            up_ref[2 * pair + side, :, :LANES] = up_buf[pair, :, first : first + LANES]
            up_ref[2 * pair + side, :, LANES:] = up_buf[pair, :, first + 2 * LANES : first + three]


def attend_kernel(shards, len_ref, order_ref, q_ref, k_ref, v_ref, lse_ref, ctx_ref, lse_cols):
    slots = q_ref.shape[1]
    count = len_ref[0]
    block = slots
    keep = iota((block, slots), 1) < count
    lane = iota((block, LANES), 1)

    def one_pair(j, carry):
        k = k_ref[j]
        v_sides = halves(v_ref[j])
        columns = pl.ds(pl.multiple_of(order_ref[j] * LANES, LANES), LANES)
        for first in range(0, slots, block):
            band = slice(first, first + block)
            q_sides = halves(q_ref[j, band, :])
            both = jnp.zeros((block, LANES), f32)
            for side in range(2):
                s = jnp.where(keep, mm_last(q_sides[side], k), -1e30)
                top = jnp.max(s, 1, keepdims=True)
                e = jnp.exp(s - top)
                total = jnp.sum(e, 1, keepdims=True)
                both = both + mm((e * (1.0 / total)).astype(bf16), v_sides[side])
                lse_cols[band, :] = jnp.where(lane == 2 * j + side, top + jnp.log(total), lse_cols[band, :])
            ctx_ref[band, columns] = both.astype(bf16)
        return carry

    lax.fori_loop(0, shards, one_pair, 0, unroll=2)
    lse_ref[...] = lse_cols[...].T[: 2 * shards].reshape(lse_ref.shape)


def gelu_parts(x):
    size = jnp.abs(x)
    t = 1.0 / (1.0 + (0.3275911 * 0.5**0.5) * size)
    bell = jnp.exp2((-0.5 * 1.4426950408889634) * (x * x))
    tail = bell * t * (
        0.127414796
        + t * (-0.142248368 + t * (0.7107068705 + t * (-0.7265760135 + t * 0.5307027145)))
    )
    cdf = jnp.where(x < 0.0, tail, 1.0 - tail)
    return x * cdf, cdf + x * (bell * 0.3989422804014327)


def middle_kernel(
    shards, len_ref, label_ref, x_ref, ctx_ref, gain_ref, bias_ref, class_ref, w_ref,
    dctx_ref, loss_ref,
    wo_buf, wi_buf, wf_buf, slope_buf, acc_ref, h_ref, hb_ref, hat_ref, df_ref, g_two, sems,
):
    slots, width = x_ref.shape
    classes = class_ref.shape[0]
    units = wi_buf.shape[-1]
    in_rows, out_rows, att_rows = rows_of(shards, width)
    start = in_rows + 2 * out_rows
    copies = []
    for shard in range(shards):
        mine = [
            pltpu.make_async_copy(w_ref.at[shard, :, pl.ds(0, in_rows), :], wi_buf.at[shard], sems.at[shard, 0])
        ]
        for side in range(2):
            cols = pl.ds(side * units, units)
            mine.append(
                pltpu.make_async_copy(
                    w_ref.at[shard, :, pl.ds(in_rows + side * out_rows, out_rows), :],
                    wf_buf.at[shard, :, :, cols],
                    sems.at[shard, 1 + side],
                )
            )
        copies.append(mine)
    wo_copies = []
    for place in range(GROUPS):
        wo_copies.append(
            pltpu.make_async_copy(
                w_ref.at[:, place, pl.ds(start, att_rows), :],
                wo_buf.at[:, place // 2, :, pl.ds(place % 2 * units, units)],
                sems.at[place % shards, 3 + place // shards],
            )
        )
    for one in wo_copies:
        one.start()
    for mine in copies:
        for one in mine:
            one.start()
    count = len_ref[0]
    count_f = count.astype(f32)
    label = label_ref[0]
    for one in wo_copies:
        one.wait()
    hat1, std1 = normalize(x_ref[...] + mm(ctx_ref[...], wo_buf[...].reshape(width, width)))
    hat_ref[...] = hat1
    h1 = hat1 * gain_ref[1:2, :] + bias_ref[1:2, :]
    h_ref[...] = h1
    hb_ref[...] = h1.astype(bf16)
    for f in range(shards):
        for one in copies[f]:
            one.wait()
        for top in range(0, slots, BAND):
            band = slice(top, top + BAND)
            g, slope = gelu_parts(mm(hb_ref[band, :], wi_buf[f].reshape(width, units)))
            slope_buf[f, band, :] = slope
            g_two[band, (f % 2) * units : (f % 2 + 1) * units] = g.astype(bf16)
        if f % 2:
            part = mm(g_two[...], wf_buf[f - 1 : f + 1].reshape(2 * units, width))
            if f == 1:
                acc_ref[...] = h_ref[...] + part
            else:
                acc_ref[...] += part
    hat2, std2 = normalize(acc_ref[...])
    gain2 = gain_ref[2:3, :]
    valid = (iota((slots, 1), 0) < count).astype(f32)
    pooled = jnp.sum((hat2 * gain2 + bias_ref[2:3, :]) * valid, 0, keepdims=True) / count_f
    weights = class_ref[...].astype(f32)
    logits = jnp.sum(pooled.astype(bf16).astype(f32) * weights, 1, keepdims=True)
    shifted = logits - jnp.max(logits, 0, keepdims=True)
    log_prob = shifted - jnp.log(jnp.sum(jnp.exp(shifted), 0, keepdims=True))
    target = (1.0 - smooth_rate) * (iota((classes, 1), 0) == label).astype(f32) + smooth_rate / classes
    loss_ref[...] = jnp.broadcast_to(-jnp.sum(target * log_prob, 0, keepdims=True), loss_ref.shape)
    d_pooled = jnp.sum((jnp.exp(log_prob) - target) * weights, 0, keepdims=True) / count_f
    d_two = norm_back((d_pooled * gain2) * valid, hat2, std2)
    acc_ref[...] = d_two
    df_ref[...] = d_two.astype(bf16)
    for f in range(shards):
        d_pre = (mm_last(df_ref[...], wf_buf[f].reshape(units, width)) * slope_buf[f]).astype(bf16)
        acc_ref[...] += mm_last(d_pre, wi_buf[f].reshape(width, units))
    d_attn = norm_back(acc_ref[...] * gain_ref[1:2, :], hat_ref[...], std1).astype(bf16)
    dctx_ref[...] = mm_last(d_attn, wo_buf[...].reshape(width, width)).astype(bf16)


def gradient_kernel(
    shards, groups, len_ref, order_ref, xb_ref, xa_ref, q_ref, k_ref, v_ref, lse_ref, dctx_ref, up_ref,
    send_ref, norm_ref,
    up_grad, inner_ref,
):
    slots, width = xb_ref.shape
    rank2 = xa_ref.shape[1]
    rank = rank2 // 2
    count = len_ref[0]
    block = slots
    keep = iota((slots, block), 0) < count
    xa = xa_ref[...]
    low = iota((LANES, rank2), 1) < rank
    rows = width // (groups * shards)
    part = rows // 2
    inner_ref[...] = jnp.zeros_like(inner_ref)

    def one_pair(j, carry):
        k = k_ref[j]
        k_sides = halves(k)
        v_sides = halves(v_ref[j])
        shard = order_ref[j]
        columns = pl.ds(pl.multiple_of(shard * LANES, LANES), LANES)
        dv = jnp.zeros((slots, LANES), f32)
        found = []
        for first in range(0, slots, block):
            band = slice(first, first + block)
            q = q_ref[j, band, :]
            dctx = dctx_ref[band, columns]
            dctx_sides = halves(dctx)
            parts = []
            for side in range(2):
                s = jnp.where(keep, mm_last(k_sides[side], q), -1e30)
                prob = jnp.exp(s - lse_ref[j, side : side + 1, band])
                d_prob = mm_last(v_sides[side], dctx)
                weighted = jnp.sum(prob * d_prob, 0, keepdims=True)
                d_s = (prob * (d_prob - weighted)).astype(bf16)
                dv = dv + mm(prob.astype(bf16), dctx_sides[side])
                parts.append(lax.dot_general(d_s, k_sides[side], FIRST, preferred_element_type=f32))
            found.append(parts[0] + parts[1])
        dq = (jnp.concatenate(found, 0) * (HDIM**-0.5)).astype(bf16)
        dq_flip = flip(dq).astype(bf16)
        dv = dv.astype(bf16)
        grad = adapter_scale * jnp.where(low, mm(dq_flip, xa), mm(flip(dv).astype(bf16), xa))
        for i in range(groups):
            at = pl.multiple_of((i * shards + shard) * rows, rows)
            up_grad[pl.ds(at, rows), :] = grad[i * rows : (i + 1) * rows]
        inner_ref[...] += adapter_scale * mm_last(jnp.concatenate([dq, dv], 1), up_ref[j])
        return carry

    lax.fori_loop(0, shards, one_pair, 0, unroll=2)
    down_grad = mm(flip(inner_ref[...].astype(bf16)).astype(bf16), xb_ref[...]).T
    both = jnp.concatenate([up_grad[...], down_grad], 1)
    squares = jnp.sum(jnp.sum(both * both, 1, keepdims=True), 0, keepdims=True)
    norm = jnp.sqrt(squares)
    norm_ref[...] = jnp.broadcast_to(norm, norm_ref.shape)
    both = both * (clip_bound / jnp.maximum(norm, clip_bound))
    both = jnp.concatenate([both, pltpu.roll(both, width - part, 0)], 1)
    for to in range(groups * shards):
        send_ref[to] = both[to * rows : to * rows + part, :].astype(bf16)


def lamb(weight, grad, first, second, fix_one, fix_two):
    first_new = beta_one * first + (1.0 - beta_one) * grad
    second_new = beta_two * second + (1.0 - beta_two) * grad * grad
    direction = first_new / fix_one / (jnp.sqrt(second_new / fix_two) + adam_eps) + decay_rate * weight
    return first_new, second_new, direction


def side_by_side(ref):
    return jnp.concatenate([ref[0], ref[1]], 1)


def flipped(ref):
    maps, rank, cols = ref.shape
    return ref[...].reshape(maps * rank, cols).T


def early_kernel(
    sc_ref, down_ref, up_ref, dm1_ref, dm2_ref, um1_ref, um2_ref, dn_ref, un_ref,
    slice_ref, rows_ref, up_turn, down_turn, part_turn,
):
    dp_at, head_at = sc_ref[0], sc_ref[1]
    rows = slice_ref.shape[1]
    rank2 = up_turn.shape[1]
    many = dm1_ref.shape[2]
    up_turn[...] = flipped(up_ref)
    down_turn[...] = flipped(down_ref)
    rows_ref[0] = down_turn[pl.ds(pl.multiple_of(dp_at * many, many), many), :]
    for n, ref in enumerate((dm1_ref, dm2_ref, dn_ref)):
        part_turn[n] = flipped(ref)
    rows_ref[1] = part_turn[0]
    rows_ref[2] = part_turn[1]
    here = pl.ds(pl.multiple_of(head_at * rows, rows), rows)
    up_weight = up_turn[pl.ds(pl.multiple_of(dp_at * rows, rows), rows), :]
    ups = (up_weight, side_by_side(un_ref), side_by_side(um1_ref), side_by_side(um2_ref))
    downs = (rows_ref[0, here, :], part_turn[2, here, :], part_turn[0, here, :], part_turn[1, here, :])
    for n in range(4):
        slice_ref[n, :, :rank2] = ups[n]
        slice_ref[n, :, rank2:] = downs[n]


def direction_kernel(examples, fix_ref, got_ref, loss_ref, slice_ref, tile_ref, new_ref):
    rows = slice_ref.shape[1]
    rank2 = slice_ref.shape[2] // 2
    weight, noise, first, second = (slice_ref[n] for n in range(4))
    total = jnp.sum(got_ref[...].astype(f32), 0)
    total = jnp.concatenate([total[:, : 2 * rank2], total[:, 2 * rank2 :]], 0)
    grad = (total + noise_mult * clip_bound * noise) / examples
    first_new, second_new, direction = lamb(weight, grad, first, second, fix_ref[0], fix_ref[1])
    new_ref[0] = first_new
    new_ref[1] = second_new
    new_ref[2] = direction
    down_grad = grad[:, rank2:]
    per_line = LANES // rank2
    lines = [
        jnp.concatenate([down_grad[k : k + 1] for k in range(line, line + per_line)], 1)
        for line in range(0, rows, per_line)
    ]
    lines.append(
        jnp.concatenate(
            [jnp.sum(direction * direction, 0, keepdims=True), jnp.sum(weight * weight, 0, keepdims=True)], 1
        )
    )
    lines.append(loss_ref[...])
    tile = jnp.concatenate(lines, 0)
    for to in range(tile_ref.shape[0]):
        tile_ref[to] = tile


def update_kernel(
    examples, shards, sc_ref, fix_ref, got_ref, slice_ref, rows_ref, new_ref,
    loss_ref, dm1_out, dm2_out, dw_out, um1_out, um2_out, uw_out, table_ref,
):
    dp_at = sc_ref[0]
    rows = slice_ref.shape[1]
    rank2 = slice_ref.shape[2] // 2
    rank = rank2 // 2
    per_line = LANES // rank2
    lines = rows // per_line
    total = jnp.sum(got_ref[...], 0)
    loss_ref[...] = total[lines + 1 : lines + 2, 0:1] / examples
    stats = total[lines : lines + 1, :]
    lane = iota(stats.shape, 1)

    def part(group):
        inside = (lane >= group * rank) & (lane < (group + 1) * rank)
        return jnp.sqrt(jnp.sum(jnp.where(inside, stats, 0.0), 1, keepdims=True))

    norms = [(part(group + 4), part(group)) for group in range(4)]
    for out_col, group in enumerate((2, 3, 0, 1)):
        table_ref[:, out_col : out_col + 1] = jnp.concatenate(norms[group], 0)

    def rate(a, b):
        wide = iota((1, rank2), 1) < rank
        return learn_rate * jnp.where(wide, norms[a][0] / norms[a][1], norms[b][0] / norms[b][1])

    up_new = slice_ref[0, :, :rank2] - rate(0, 1) * new_ref[2, :, :rank2]
    for ref, value in ((uw_out, up_new), (um1_out, new_ref[0]), (um2_out, new_ref[1])):
        ref[0] = value[:, :rank]
        ref[1] = value[:, rank:rank2]
    grad = jnp.concatenate(
        [
            got_ref[dp_at * shards + j, k // per_line, (k % per_line) * rank2 : (k % per_line + 1) * rank2]
            .reshape(1, rank2)
            for j in range(shards)
            for k in range(rows)
        ],
        0,
    )
    first_new, second_new, direction = lamb(
        rows_ref[0], grad, rows_ref[1], rows_ref[2], fix_ref[0], fix_ref[1]
    )
    new = rows_ref[0] - rate(2, 3) * direction
    for ref, value in ((dm1_out, first_new), (dm2_out, second_new), (dw_out, new)):
        ref[...] = value.T.reshape(ref.shape)


def per_device(
    slot_token_ids,
    lengths,
    labels,
    optimizer_step_count,
    token_embedding_table,
    positions,
    query_key_value_weight,
    attention_output_weight,
    feedforward_input_weight,
    feedforward_output_weight,
    layer_norm_gains,
    layer_norm_biases,
    classifier,
    adapter_down_maps,
    adapter_up_maps,
    down_first_moment,
    down_second_moment,
    up_first_moment,
    up_second_moment,
    down_privacy_noise,
    up_privacy_noise,
):
    shards = lax.axis_size("head")
    groups = lax.axis_size("dp")
    devices = shards * groups
    dp_at = lax.axis_index("dp")
    head_at = lax.axis_index("head")
    slots, width = positions.shape
    rank = adapter_down_maps.shape[2]
    rank2 = 2 * rank
    units = feedforward_output_weight.shape[0]
    local_w = attention_output_weight.shape[0]
    owned = token_embedding_table.shape[0]
    shape = jax.ShapeDtypeStruct

    def turned(x):
        return jnp.swapaxes(x, 1, 2)

    down_maps = turned(adapter_down_maps)

    def ask(which, slot_token_ids):
        return call(
            functools.partial(request_kernel, groups, shards, owned),
            (shape((devices, 1, LANES), i32), shape((slots, LANES), i32)),
            [SM, SM, VM],
            (VM, VM),
        )(jnp.stack([head_at, which]).astype(i32), lengths, slot_token_ids)

    def look(wanted):
        return call(
            lookup_kernel,
            shape((devices, CAP, LANES), bf16),
            [SM, VM],
            VM,
            [pltpu.VMEM((owned, LANES), f32), pltpu.VMEM((CAP, LANES), f32)],
            flops=10**10,
        )(wanted, token_embedding_table)

    def place(found, slot):
        got = exchange(found)
        emb = call(
            functools.partial(assemble_kernel, groups, shards),
            shape((slots, width), bf16),
            [VM, VM],
            VM,
            [pltpu.VMEM((groups * CAP, width), bf16)],
            flops=2 * 10**10,
        )(got, slot)
        return emb

    def exchange(x):
        return lax.all_to_all(x, ALL, 0, 0, tiled=True)

    pack = call(
        pack_kernel,
        shape((width // GROUPS * 2 + 2 * width // shards // GROUPS, units), bf16),
        [SM, ANY, ANY, ANY],
        VM,
        [pltpu.SemaphoreType.DMA((4,))],
        vmem=60,
    )(
        dp_at.reshape(1).astype(i32), feedforward_input_weight, feedforward_output_weight,
        attention_output_weight,
    )
    pack, slot_token_ids = lax.optimization_barrier((pack, slot_token_ids))
    weights = lax.all_gather(pack, ("head", "dp"), axis=0, tiled=True).reshape(shards, groups, *pack.shape)

    steps = shards // 2
    packed = jnp.concatenate(
        [
            query_key_value_weight.reshape(3 * width, local_w),
            adapter_up_maps.reshape(rank2, local_w).astype(bf16),
        ],
        0,
    )
    order = jnp.stack(
        [
            2 * ((head_at // 2 + step) % steps) + (head_at + column) % 2
            for step in range(steps)
            for column in range(2)
        ]
    ).astype(i32)

    def permuted(x, source):
        return lax.ppermute(x, "head", [(source(i), i) for i in range(shards)])

    packed_z = [permuted(packed, lambda i, step=step: (i + 2 * step) % shards) for step in range(1, steps)]
    requests, slot = ask(jnp.zeros((), i32), slot_token_ids)

    wanted = exchange(requests)
    rounds = jnp.max(wanted[:, 0, LANES - 1])
    wanted, packed_z = lax.optimization_barrier((wanted, packed_z))
    found = look(wanted)
    w_own = jnp.stack([packed, *packed_z])
    w_peer = permuted(w_own, lambda i: i ^ 1)
    emb = place(found, slot)

    def again(which):
        asked, where = ask(which, slot_token_ids)
        return place(look(exchange(asked)), where)

    unused_at, emb = lax.while_loop(
        lambda state: state[0] < rounds,
        lambda state: (state[0] + 1, state[1] + again(state[0])),
        (jnp.ones((), i32), emb),
    )

    own_len = lax.dynamic_slice_in_dim(lengths, head_at, 1)
    own_label = lax.dynamic_slice_in_dim(labels, head_at, 1)
    x0, x0b, xa, q, k, v, up = call(
        functools.partial(project_kernel, shards),
        (
            shape((slots, width), f32),
            shape((slots, width), bf16),
            shape((slots, rank2), bf16),
            shape((shards, slots, LANES), bf16),
            shape((shards, slots, LANES), bf16),
            shape((shards, slots, LANES), bf16),
            shape((shards, rank2, 2 * LANES), bf16),
        ),
        [VM, VM, VM, VM, VM, ANY, ANY],
        (VM,) * 7,
        [
            pltpu.VMEM((shards // 2, width, 6 * LANES), bf16),
            pltpu.VMEM((shards // 2, rank2, 6 * LANES), bf16),
            pltpu.SemaphoreType.DMA((shards // 2, 10)),
        ],
        vmem=50,
    )(emb, positions, layer_norm_gains, layer_norm_biases, down_maps, w_own, w_peer)
    lse, ctx = call(
        functools.partial(attend_kernel, shards),
        (shape((shards, 2, slots), f32), shape((slots, width), bf16)),
        [SM, SM, VM, VM, VM],
        (VM, VM),
        [pltpu.VMEM((slots, LANES), f32)],
        vmem=40,
    )(own_len, order, q, k, v)

    dctx, loss = call(
        functools.partial(middle_kernel, shards),
        (shape((slots, width), bf16), shape((1, LANES), f32)),
        [SM, SM, VM, VM, VM, VM, VM, ANY],
        (VM, VM),
        [
            pltpu.VMEM((shards, groups // 2, 2 * local_w // groups, width), bf16),
            pltpu.VMEM((shards, groups, width // groups, units), bf16),
            pltpu.VMEM((shards, groups, units // groups, width), bf16),
            pltpu.VMEM((shards, slots, units), f32),
            pltpu.VMEM((slots, width), f32),
            pltpu.VMEM((slots, width), f32),
            pltpu.VMEM((slots, width), bf16),
            pltpu.VMEM((slots, width), f32),
            pltpu.VMEM((slots, width), bf16),
            pltpu.VMEM((slots, 2 * units), bf16),
            pltpu.SemaphoreType.DMA((shards, 5)),
        ],
        vmem=60,
    )(
        own_len, own_label, x0, ctx, layer_norm_gains, layer_norm_biases, classifier, weights
    )

    send, norm = call(
        functools.partial(gradient_kernel, shards, groups),
        (shape((devices, 2 * rank2 * width // devices // LANES, LANES), bf16), shape((1, LANES), f32)),
        [SM, SM, VM, VM, VM, VM, VM, VM, VM, VM],
        (VM, VM),
        [pltpu.VMEM((width, rank2), f32), pltpu.VMEM((slots, rank2), f32)],
        vmem=50,
    )(own_len, order, x0b, xa, q, k, v, lse, dctx, up)

    got = exchange(send)
    examples = float(devices)
    step_number = optimizer_step_count.astype(f32)
    fixes = jnp.stack([1.0 - jnp.power(beta_one, step_number), 1.0 - jnp.power(beta_two, step_number)])
    where = jnp.stack([dp_at, head_at]).astype(i32)
    rows = width // devices
    moments = [turned(x) for x in (down_first_moment, down_second_moment, up_first_moment, up_second_moment)]
    lines = rows * rank2 // LANES + 2
    many = width // groups
    slices, down_rows = call(
        early_kernel,
        (shape((4, rows, 2 * rank2), f32), shape((3, many, rank2), f32)),
        [SM] + [VM] * 8,
        (VM, VM),
        [
            pltpu.VMEM((local_w, rank2), f32),
            pltpu.VMEM((width, rank2), f32),
            pltpu.VMEM((3, many, rank2), f32),
        ],
    )(where, down_maps, adapter_up_maps, *moments, turned(down_privacy_noise), turned(up_privacy_noise))
    tile, fresh = call(
        functools.partial(direction_kernel, examples),
        (shape((devices, lines, LANES), f32), shape((3, rows, 2 * rank2), f32)),
        [SM] + [VM] * 3,
        (VM, VM),
    )(fixes, got, loss, slices)
    spread = exchange(tile)
    down_shape = shape(moments[0].shape, f32)
    up_shape = shape(moments[2].shape, f32)
    loss_mean, dm1, dm2, dw, bm1, bm2, bw, table = call(
        functools.partial(update_kernel, examples, shards),
        (
            shape((1, 1), f32), down_shape, down_shape, down_shape, up_shape, up_shape, up_shape,
            shape((2, 4), f32),
        ),
        [SM, SM] + [VM] * 4,
        (VM,) * 8,
    )(where, fixes, spread, slices, down_rows, fresh)
    return (
        loss_mean.reshape(()),
        norm[0, 0:1],
        turned(dm1),
        turned(dm2),
        turned(dw),
        turned(bm1),
        turned(bm2),
        turned(bw),
        table.T,
    )


def solution(mesh):
    placed = (
        P("dp", None),
        P("dp"),
        P("dp"),
        P(),
        P("dp", "head"),
        P(),
        P(None, None, "head"),
        P("head", None),
        P(None, "head"),
        P("head", None),
        P(),
        P(),
        P(),
        P(),
        P(None, None, "head"),
        P(None, "dp", None),
        P(None, "dp", None),
        P(None, None, ("head", "dp")),
        P(None, None, ("head", "dp")),
        P(None, "dp", None),
        P(None, None, ("head", "dp")),
    )
    return jax.shard_map(
        per_device,
        mesh=mesh,
        in_specs=placed,
        out_specs=(
            P(),
            P(("dp", "head")),
            P(None, "dp", None),
            P(None, "dp", None),
            P(None, "dp", None),
            P(None, None, ("head", "dp")),
            P(None, None, ("head", "dp")),
            P(None, None, ("head", "dp")),
            P(),
        ),
        check_vma=False,
    )
```

```python
import functools

import jax
import jax.numpy as jnp
from jax import lax
from jax.experimental import pallas as pl
from jax.experimental.pallas import tpu as pltpu
from jax.sharding import PartitionSpec as P

HDIM = 64
CAP = 48
GROUPS = 16
BAND = 128
LANES = 128
MIB = 1 << 20

adapter_scale = 2.0
clip_bound = 1.0
noise_mult = 0.6
smooth_rate = 0.1
beta_one = 0.9
beta_two = 0.999
adam_eps = 1e-06
decay_rate = 0.01
learn_rate = 0.25
norm_eps = 1e-05

f32 = jnp.float32
bf16 = jnp.bfloat16
i32 = jnp.int32
LAST = (((1,), (1,)), ((), ()))
FIRST = (((0,), (0,)), ((), ()))
ALL = ("dp", "head")
VM = pl.BlockSpec(memory_space=pltpu.VMEM)
SM = pl.BlockSpec(memory_space=pltpu.SMEM)
ANY = pl.BlockSpec(memory_space=pl.ANY)


def iota(shape, axis):
    return lax.broadcasted_iota(i32, shape, axis)


def mm(a, b):
    return jnp.dot(a, b, preferred_element_type=f32)


def mm_last(a, b):
    return lax.dot_general(a, b, LAST, preferred_element_type=f32)


def call(kernel, outs, in_specs, out_specs, scratch=(), vmem=32, flops=1):
    return pl.pallas_call(
        kernel,
        out_shape=outs,
        in_specs=in_specs,
        out_specs=out_specs,
        scratch_shapes=list(scratch),
        compiler_params=pltpu.CompilerParams(vmem_limit_bytes=vmem * MIB),
        cost_estimate=pl.CostEstimate(flops=flops, bytes_accessed=1, transcendentals=0),
    )


def request_kernel(owners, peers, owned, sc_ref, len_ref, ids_ref, req_ref, slot_ref):
    me = sc_ref[0]
    base = (sc_ref[1] * CAP).astype(f32)
    count = len_ref[me]
    ids = ids_ref[...].astype(f32)
    examples, slots = ids.shape
    row = jnp.sum(jnp.where(iota(ids.shape, 0) == me, ids, 0.0), 0, keepdims=True)
    flipped = ids.T
    col = jnp.sum(jnp.where(iota(flipped.shape, 1) == me, flipped, 0.0), 1, keepdims=True)
    t_col = iota((slots, slots), 0)
    t_row = iota((slots, slots), 1)
    valid_col = (iota((slots, 1), 0) < count).astype(f32)
    valid_row = (iota((1, slots), 1) < count).astype(f32)
    own_col = sum((col >= k * owned).astype(f32) for k in range(1, owners))
    own_row = sum((row >= k * owned).astype(f32) for k in range(1, owners))
    same = (col == row) & (t_row < count) & (t_col < count)
    before = t_row < t_col
    after = t_col < t_row
    seen_col = jnp.sum(jnp.where(same & before, 1.0, 0.0), 1, keepdims=True)
    seen_row = jnp.sum(jnp.where(same & after, 1.0, 0.0), 0, keepdims=True)
    first_col = jnp.where(seen_col == 0.0, valid_col, 0.0)
    first_row = jnp.where(seen_row == 0.0, valid_row, 0.0)
    shared = own_col == own_row
    place_col = jnp.sum(jnp.where(shared & before, first_row, 0.0), 1, keepdims=True)
    place_row = jnp.sum(jnp.where(shared & after, first_col, 0.0), 0, keepdims=True)
    rank = jnp.sum(jnp.where(same, first_row * place_row, 0.0), 1, keepdims=True)
    local = rank - base
    here = (local >= 0.0) & (local < CAP) & (valid_col > 0.0)
    slot = jnp.where(here, own_col * CAP + local, -1.0)
    slot_ref[...] = jnp.broadcast_to(slot, slot_ref.shape).astype(i32)
    rounds = jnp.floor(jnp.max(rank, 0, keepdims=True) * (1.0 / CAP) + 0.5 / CAP) + 1.0
    lane = iota((slots, LANES), 1)
    lane_f = lane.astype(f32)
    wanted = jnp.where(first_col > 0.0, place_col - base, -1.0)
    hit = (wanted == lane_f) & (lane < CAP)
    lane_row = iota((1, LANES), 1)
    for owner in range(owners):
        chosen = jnp.where(hit & (own_col == float(owner)), col - float(owner * owned), 0.0)
        line = jnp.sum(chosen, 0, keepdims=True)
        line = jnp.where(lane_row == LANES - 1, rounds, line).astype(i32)
        for peer in range(peers):
            req_ref[owner * peers + peer] = line


def lookup_kernel(want_ref, table_ref, out_ref, wide_ref, stage_ref):
    wide_ref[...] = table_ref[...].astype(f32)

    def one(pair, carry):
        for half in range(2):
            for p in range(CAP):
                stage_ref[half, p : p + 1, :] = wide_ref[pl.ds(want_ref[2 * pair + half, 0, p], 1), :]
        for half in range(2):
            out_ref[2 * pair + half] = stage_ref[half].astype(bf16)
        return carry

    lax.fori_loop(0, want_ref.shape[0] // 2, one, 0)


def assemble_kernel(owners, peers, got_ref, slot_ref, emb_ref, rows_ref):
    for owner in range(owners):
        for peer in range(peers):
            rows_ref[owner * CAP : (owner + 1) * CAP, peer * LANES : (peer + 1) * LANES] = got_ref[
                owner * peers + peer
            ]
    slot = slot_ref[...]
    lane = iota(slot.shape, 1)
    picks = [
        (slot == lane + first).astype(f32).astype(bf16)
        for first in range(0, owners * CAP, LANES)
    ]
    emb_ref[...] = mm(jnp.concatenate(picks, 1), rows_ref[...]).astype(bf16)


def pack_kernel(at_ref, in_ref, out_ref, att_ref, pack_ref, sems):
    at = at_ref[0]
    wide = in_ref.shape[1]
    in_rows, out_rows = in_ref.shape[0] // GROUPS, out_ref.shape[0] // GROUPS
    att_rows = 2 * att_ref.shape[0] // GROUPS
    here = lambda rows: pl.ds(pl.multiple_of(at * rows, rows), rows)
    moves = [(in_ref.at[here(in_rows), :], pack_ref.at[pl.ds(0, in_rows), :])]
    row = in_rows
    for first in range(0, 2 * wide, wide):
        moves.append((out_ref.at[here(out_rows), pl.ds(first, wide)], pack_ref.at[pl.ds(row, out_rows), :]))
        row += out_rows
    half = att_ref.at[
        pl.ds(pl.multiple_of(at // 2 * att_rows, att_rows), att_rows),
        pl.ds(pl.multiple_of(at % 2 * wide, wide), wide),
    ]
    moves.append((half, pack_ref.at[pl.ds(row, att_rows), :]))
    copies = [pltpu.make_async_copy(source, target, sems.at[n]) for n, (source, target) in enumerate(moves)]
    for one in copies:
        one.start()
    for one in copies:
        one.wait()


def normalize(inputs):
    centre = inputs - jnp.mean(inputs, -1, keepdims=True)
    inv_std = lax.rsqrt(jnp.mean(centre * centre, -1, keepdims=True) + norm_eps)
    return centre * inv_std, inv_std


def norm_back(scaled, x_hat, inv_std):
    return inv_std * (
        scaled
        - jnp.mean(scaled, -1, keepdims=True)
        - x_hat * jnp.mean(scaled * x_hat, -1, keepdims=True)
    )


def halves(pair):
    low = iota(pair.shape, 1) < HDIM
    zero = jnp.zeros_like(pair)
    return jnp.where(low, pair, zero), jnp.where(low, zero, pair)


def flip(x):
    return x.astype(f32).T


def rows_of(shards, width):
    in_rows = width // GROUPS
    return in_rows, in_rows // 2, 2 * width // shards // GROUPS


def project_kernel(
    shards, emb_ref, pos_ref, gain_ref, bias_ref, down_ref, w_own, w_peer,
    x_ref, xb_ref, xa_ref, q_ref, k_ref, v_ref, up_ref,
    w_buf, up_buf, sems,
):
    slots, width = emb_ref.shape
    rank = down_ref.shape[1]
    rank2 = 2 * rank
    three = 3 * LANES
    copies = []
    up_buf[...] = jnp.zeros_like(up_buf)
    for pair in range(shards // 2):
        mine = []
        for side, w_ref in enumerate((w_own, w_peer)):
            for part in range(3):
                mine.append(
                    pltpu.make_async_copy(
                        w_ref.at[pair, pl.ds(part * width, width), :],
                        w_buf.at[pair, :, pl.ds(side * three + part * LANES, LANES)],
                        sems.at[pair, side * 5 + part],
                    )
                )
            for part in range(2):
                mine.append(
                    pltpu.make_async_copy(
                        w_ref.at[pair, pl.ds(3 * width + part * rank, rank), :],
                        up_buf.at[pair, pl.ds(part * rank, rank), pl.ds(side * three + 2 * part * LANES, LANES)],
                        sems.at[pair, side * 5 + 3 + part],
                    )
                )
        copies.append(mine)
    for mine in copies:
        for one in mine:
            one.start()
    x_hat, unused_std = normalize(emb_ref[...].astype(f32) + pos_ref[...].astype(f32))
    x0 = x_hat * gain_ref[0:1, :] + bias_ref[0:1, :]
    x_ref[...] = x0
    xb_ref[...] = x0.astype(bf16)
    xa = mm_last(xb_ref[...], down_ref[...].reshape(rank2, width).astype(bf16)).astype(bf16)
    xa_ref[...] = xa
    twice = xa * jnp.asarray(adapter_scale, bf16)
    for pair in range(shards // 2):
        for one in copies[pair]:
            one.wait()
        total = mm(xb_ref[...], w_buf[pair]) + mm(twice, up_buf[pair])
        for side in range(2):
            first = side * three
            q_ref[2 * pair + side] = (total[:, first : first + LANES] * (HDIM**-0.5)).astype(bf16)
            k_ref[2 * pair + side] = total[:, first + LANES : first + 2 * LANES].astype(bf16)
            v_ref[2 * pair + side] = total[:, first + 2 * LANES : first + three].astype(bf16)
            up_ref[2 * pair + side, :, :LANES] = up_buf[pair, :, first : first + LANES]
            up_ref[2 * pair + side, :, LANES:] = up_buf[pair, :, first + 2 * LANES : first + three]


def attend_kernel(shards, len_ref, order_ref, q_ref, k_ref, v_ref, lse_ref, ctx_ref, lse_cols):
    slots = q_ref.shape[1]
    count = len_ref[0]
    block = slots
    keep = iota((block, slots), 1) < count
    lane = iota((block, LANES), 1)

    def one_pair(j, carry):
        k = k_ref[j]
        v_sides = halves(v_ref[j])
        columns = pl.ds(pl.multiple_of(order_ref[j] * LANES, LANES), LANES)
        for first in range(0, slots, block):
            band = slice(first, first + block)
            q_sides = halves(q_ref[j, band, :])
            both = jnp.zeros((block, LANES), f32)
            for side in range(2):
                s = jnp.where(keep, mm_last(q_sides[side], k), -1e30)
                top = jnp.max(s, 1, keepdims=True)
                e = jnp.exp(s - top)
                total = jnp.sum(e, 1, keepdims=True)
                both = both + mm((e * (1.0 / total)).astype(bf16), v_sides[side])
                lse_cols[band, :] = jnp.where(lane == 2 * j + side, top + jnp.log(total), lse_cols[band, :])
            ctx_ref[band, columns] = both.astype(bf16)
        return carry

    lax.fori_loop(0, shards, one_pair, 0, unroll=2)
    lse_ref[...] = lse_cols[...].T[: 2 * shards].reshape(lse_ref.shape)


def gelu_parts(x):
    size = jnp.abs(x)
    t = 1.0 / (1.0 + (0.3275911 * 0.5**0.5) * size)
    bell = jnp.exp2((-0.5 * 1.4426950408889634) * (x * x))
    tail = bell * t * (
        0.127414796
        + t * (-0.142248368 + t * (0.7107068705 + t * (-0.7265760135 + t * 0.5307027145)))
    )
    cdf = jnp.where(x < 0.0, tail, 1.0 - tail)
    return x * cdf, cdf + x * (bell * 0.3989422804014327)


def middle_kernel(
    shards, len_ref, label_ref, x_ref, ctx_ref, gain_ref, bias_ref, class_ref, w_ref,
    dctx_ref, loss_ref,
    wo_buf, wi_buf, wf_buf, slope_buf, acc_ref, h_ref, hb_ref, hat_ref, df_ref, g_two, sems,
):
    slots, width = x_ref.shape
    classes = class_ref.shape[0]
    units = wi_buf.shape[-1]
    in_rows, out_rows, att_rows = rows_of(shards, width)
    start = in_rows + 2 * out_rows
    copies = []
    for shard in range(shards):
        mine = [
            pltpu.make_async_copy(w_ref.at[shard, :, pl.ds(0, in_rows), :], wi_buf.at[shard], sems.at[shard, 0])
        ]
        for side in range(2):
            cols = pl.ds(side * units, units)
            mine.append(
                pltpu.make_async_copy(
                    w_ref.at[shard, :, pl.ds(in_rows + side * out_rows, out_rows), :],
                    wf_buf.at[shard, :, :, cols],
                    sems.at[shard, 1 + side],
                )
            )
        copies.append(mine)
    wo_copies = []
    for place in range(GROUPS):
        wo_copies.append(
            pltpu.make_async_copy(
                w_ref.at[:, place, pl.ds(start, att_rows), :],
                wo_buf.at[:, place // 2, :, pl.ds(place % 2 * units, units)],
                sems.at[place % shards, 3 + place // shards],
            )
        )
    for one in wo_copies:
        one.start()
    for mine in copies:
        for one in mine:
            one.start()
    count = len_ref[0]
    count_f = count.astype(f32)
    label = label_ref[0]
    for one in wo_copies:
        one.wait()
    hat1, std1 = normalize(x_ref[...] + mm(ctx_ref[...], wo_buf[...].reshape(width, width)))
    hat_ref[...] = hat1
    h1 = hat1 * gain_ref[1:2, :] + bias_ref[1:2, :]
    h_ref[...] = h1
    hb_ref[...] = h1.astype(bf16)
    for f in range(shards):
        for one in copies[f]:
            one.wait()
        for top in range(0, slots, BAND):
            band = slice(top, top + BAND)
            g, slope = gelu_parts(mm(hb_ref[band, :], wi_buf[f].reshape(width, units)))
            slope_buf[f, band, :] = slope
            g_two[band, (f % 2) * units : (f % 2 + 1) * units] = g.astype(bf16)
        if f % 2:
            part = mm(g_two[...], wf_buf[f - 1 : f + 1].reshape(2 * units, width))
            if f == 1:
                acc_ref[...] = h_ref[...] + part
            else:
                acc_ref[...] += part
    hat2, std2 = normalize(acc_ref[...])
    gain2 = gain_ref[2:3, :]
    valid = (iota((slots, 1), 0) < count).astype(f32)
    pooled = jnp.sum((hat2 * gain2 + bias_ref[2:3, :]) * valid, 0, keepdims=True) / count_f
    weights = class_ref[...].astype(f32)
    logits = jnp.sum(pooled.astype(bf16).astype(f32) * weights, 1, keepdims=True)
    shifted = logits - jnp.max(logits, 0, keepdims=True)
    log_prob = shifted - jnp.log(jnp.sum(jnp.exp(shifted), 0, keepdims=True))
    target = (1.0 - smooth_rate) * (iota((classes, 1), 0) == label).astype(f32) + smooth_rate / classes
    loss_ref[...] = jnp.broadcast_to(-jnp.sum(target * log_prob, 0, keepdims=True), loss_ref.shape)
    d_pooled = jnp.sum((jnp.exp(log_prob) - target) * weights, 0, keepdims=True) / count_f
    d_two = norm_back((d_pooled * gain2) * valid, hat2, std2)
    acc_ref[...] = d_two
    df_ref[...] = d_two.astype(bf16)
    for f in range(shards):
        d_pre = (mm_last(df_ref[...], wf_buf[f].reshape(units, width)) * slope_buf[f]).astype(bf16)
        if f % 2 == 0:
            held = d_pre
        else:
            acc_ref[...] += mm_last(held, wi_buf[f - 1].reshape(width, units)) + mm_last(
                d_pre, wi_buf[f].reshape(width, units)
            )
    d_attn = norm_back(acc_ref[...] * gain_ref[1:2, :], hat_ref[...], std1).astype(bf16)
    dctx_ref[...] = mm_last(d_attn, wo_buf[...].reshape(width, width)).astype(bf16)


def gradient_kernel(
    shards, groups, len_ref, order_ref, xb_ref, xa_ref, q_ref, k_ref, v_ref, lse_ref, dctx_ref, up_ref,
    send_ref, norm_ref,
    up_grad, inner_ref,
):
    slots, width = xb_ref.shape
    rank2 = xa_ref.shape[1]
    rank = rank2 // 2
    count = len_ref[0]
    block = slots
    keep = iota((slots, block), 0) < count
    xa = xa_ref[...]
    low = iota((LANES, rank2), 1) < rank
    rows = width // (groups * shards)
    part = rows // 2
    inner_ref[...] = jnp.zeros_like(inner_ref)

    def one_pair(j, carry):
        k = k_ref[j]
        k_sides = halves(k)
        v_sides = halves(v_ref[j])
        shard = order_ref[j]
        columns = pl.ds(pl.multiple_of(shard * LANES, LANES), LANES)
        dv = jnp.zeros((slots, LANES), f32)
        found = []
        for first in range(0, slots, block):
            band = slice(first, first + block)
            q = q_ref[j, band, :]
            dctx = dctx_ref[band, columns]
            dctx_sides = halves(dctx)
            parts = []
            for side in range(2):
                s = jnp.where(keep, mm_last(k_sides[side], q), -1e30)
                prob = jnp.exp(s - lse_ref[j, side : side + 1, band])
                d_prob = mm_last(v_sides[side], dctx)
                weighted = jnp.sum(prob * d_prob, 0, keepdims=True)
                d_s = (prob * (d_prob - weighted)).astype(bf16)
                dv = dv + mm(prob.astype(bf16), dctx_sides[side])
                parts.append(lax.dot_general(d_s, k_sides[side], FIRST, preferred_element_type=f32))
            found.append(parts[0] + parts[1])
        dq = (jnp.concatenate(found, 0) * (HDIM**-0.5)).astype(bf16)
        dq_flip = flip(dq).astype(bf16)
        dv = dv.astype(bf16)
        grad = adapter_scale * jnp.where(low, mm(dq_flip, xa), mm(flip(dv).astype(bf16), xa))
        for i in range(groups):
            at = pl.multiple_of((i * shards + shard) * rows, rows)
            up_grad[pl.ds(at, rows), :] = grad[i * rows : (i + 1) * rows]
        inner_ref[...] += adapter_scale * mm_last(jnp.concatenate([dq, dv], 1), up_ref[j])
        return carry

    lax.fori_loop(0, shards, one_pair, 0, unroll=2)
    down_grad = mm(flip(inner_ref[...].astype(bf16)).astype(bf16), xb_ref[...]).T
    both = jnp.concatenate([up_grad[...], down_grad], 1)
    squares = jnp.sum(jnp.sum(both * both, 1, keepdims=True), 0, keepdims=True)
    norm = jnp.sqrt(squares)
    norm_ref[...] = jnp.broadcast_to(norm, norm_ref.shape)
    both = both * (clip_bound / jnp.maximum(norm, clip_bound))
    both = jnp.concatenate([both, pltpu.roll(both, width - part, 0)], 1)
    for to in range(groups * shards):
        send_ref[to] = both[to * rows : to * rows + part, :].astype(bf16)


def lamb(weight, grad, first, second, fix_one, fix_two):
    first_new = beta_one * first + (1.0 - beta_one) * grad
    second_new = beta_two * second + (1.0 - beta_two) * grad * grad
    direction = first_new / fix_one / (jnp.sqrt(second_new / fix_two) + adam_eps) + decay_rate * weight
    return first_new, second_new, direction


def side_by_side(ref):
    return jnp.concatenate([ref[0], ref[1]], 1)


def flipped(ref):
    maps, rank, cols = ref.shape
    return ref[...].reshape(maps * rank, cols).T


def early_kernel(
    sc_ref, down_ref, up_ref, dm1_ref, dm2_ref, um1_ref, um2_ref, dn_ref, un_ref,
    slice_ref, rows_ref, up_turn, down_turn, part_turn,
):
    dp_at, head_at = sc_ref[0], sc_ref[1]
    rows = slice_ref.shape[1]
    rank2 = up_turn.shape[1]
    many = dm1_ref.shape[2]
    up_turn[...] = flipped(up_ref)
    down_turn[...] = flipped(down_ref)
    rows_ref[0] = down_turn[pl.ds(pl.multiple_of(dp_at * many, many), many), :]
    for n, ref in enumerate((dm1_ref, dm2_ref, dn_ref)):
        part_turn[n] = flipped(ref)
    rows_ref[1] = part_turn[0]
    rows_ref[2] = part_turn[1]
    here = pl.ds(pl.multiple_of(head_at * rows, rows), rows)
    up_weight = up_turn[pl.ds(pl.multiple_of(dp_at * rows, rows), rows), :]
    ups = (up_weight, side_by_side(un_ref), side_by_side(um1_ref), side_by_side(um2_ref))
    downs = (rows_ref[0, here, :], part_turn[2, here, :], part_turn[0, here, :], part_turn[1, here, :])
    for n in range(4):
        slice_ref[n, :, :rank2] = ups[n]
        slice_ref[n, :, rank2:] = downs[n]


def direction_kernel(examples, fix_ref, got_ref, loss_ref, slice_ref, tile_ref, new_ref):
    rows = slice_ref.shape[1]
    rank2 = slice_ref.shape[2] // 2
    weight, noise, first, second = (slice_ref[n] for n in range(4))
    total = jnp.sum(got_ref[...].astype(f32), 0)
    total = jnp.concatenate([total[:, : 2 * rank2], total[:, 2 * rank2 :]], 0)
    grad = (total + noise_mult * clip_bound * noise) / examples
    first_new, second_new, direction = lamb(weight, grad, first, second, fix_ref[0], fix_ref[1])
    new_ref[0] = first_new
    new_ref[1] = second_new
    new_ref[2] = direction
    down_grad = grad[:, rank2:]
    per_line = LANES // rank2
    lines = [
        jnp.concatenate([down_grad[k : k + 1] for k in range(line, line + per_line)], 1)
        for line in range(0, rows, per_line)
    ]
    lines.append(
        jnp.concatenate(
            [jnp.sum(direction * direction, 0, keepdims=True), jnp.sum(weight * weight, 0, keepdims=True)], 1
        )
    )
    lines.append(loss_ref[...])
    tile = jnp.concatenate(lines, 0)
    for to in range(tile_ref.shape[0]):
        tile_ref[to] = tile


def update_kernel(
    examples, shards, sc_ref, fix_ref, got_ref, slice_ref, rows_ref, new_ref,
    loss_ref, dm1_out, dm2_out, dw_out, um1_out, um2_out, uw_out, table_ref,
):
    dp_at = sc_ref[0]
    rows = slice_ref.shape[1]
    rank2 = slice_ref.shape[2] // 2
    rank = rank2 // 2
    per_line = LANES // rank2
    lines = rows // per_line
    total = jnp.sum(got_ref[...], 0)
    loss_ref[...] = total[lines + 1 : lines + 2, 0:1] / examples
    stats = total[lines : lines + 1, :]
    lane = iota(stats.shape, 1)

    def part(group):
        inside = (lane >= group * rank) & (lane < (group + 1) * rank)
        return jnp.sqrt(jnp.sum(jnp.where(inside, stats, 0.0), 1, keepdims=True))

    norms = [(part(group + 4), part(group)) for group in range(4)]
    for out_col, group in enumerate((2, 3, 0, 1)):
        table_ref[:, out_col : out_col + 1] = jnp.concatenate(norms[group], 0)

    def rate(a, b):
        wide = iota((1, rank2), 1) < rank
        return learn_rate * jnp.where(wide, norms[a][0] / norms[a][1], norms[b][0] / norms[b][1])

    up_new = slice_ref[0, :, :rank2] - rate(0, 1) * new_ref[2, :, :rank2]
    for ref, value in ((uw_out, up_new), (um1_out, new_ref[0]), (um2_out, new_ref[1])):
        ref[0] = value[:, :rank]
        ref[1] = value[:, rank:rank2]
    grad = jnp.concatenate(
        [
            got_ref[dp_at * shards + j, k // per_line, (k % per_line) * rank2 : (k % per_line + 1) * rank2]
            .reshape(1, rank2)
            for j in range(shards)
            for k in range(rows)
        ],
        0,
    )
    first_new, second_new, direction = lamb(
        rows_ref[0], grad, rows_ref[1], rows_ref[2], fix_ref[0], fix_ref[1]
    )
    new = rows_ref[0] - rate(2, 3) * direction
    for ref, value in ((dm1_out, first_new), (dm2_out, second_new), (dw_out, new)):
        ref[...] = value.T.reshape(ref.shape)


def per_device(
    slot_token_ids,
    lengths,
    labels,
    optimizer_step_count,
    token_embedding_table,
    positions,
    query_key_value_weight,
    attention_output_weight,
    feedforward_input_weight,
    feedforward_output_weight,
    layer_norm_gains,
    layer_norm_biases,
    classifier,
    adapter_down_maps,
    adapter_up_maps,
    down_first_moment,
    down_second_moment,
    up_first_moment,
    up_second_moment,
    down_privacy_noise,
    up_privacy_noise,
):
    shards = lax.axis_size("head")
    groups = lax.axis_size("dp")
    devices = shards * groups
    dp_at = lax.axis_index("dp")
    head_at = lax.axis_index("head")
    slots, width = positions.shape
    rank = adapter_down_maps.shape[2]
    rank2 = 2 * rank
    units = feedforward_output_weight.shape[0]
    local_w = attention_output_weight.shape[0]
    owned = token_embedding_table.shape[0]
    shape = jax.ShapeDtypeStruct

    def turned(x):
        return jnp.swapaxes(x, 1, 2)

    down_maps = turned(adapter_down_maps)

    def ask(which, slot_token_ids):
        return call(
            functools.partial(request_kernel, groups, shards, owned),
            (shape((devices, 1, LANES), i32), shape((slots, LANES), i32)),
            [SM, SM, VM],
            (VM, VM),
        )(jnp.stack([head_at, which]).astype(i32), lengths, slot_token_ids)

    def look(wanted):
        return call(
            lookup_kernel,
            shape((devices, CAP, LANES), bf16),
            [SM, VM],
            VM,
            [pltpu.VMEM((owned, LANES), f32), pltpu.VMEM((2, CAP, LANES), f32)],
            flops=10**10,
        )(wanted, token_embedding_table)

    def place(found, slot):
        got = exchange(found)
        emb = call(
            functools.partial(assemble_kernel, groups, shards),
            shape((slots, width), bf16),
            [VM, VM],
            VM,
            [pltpu.VMEM((groups * CAP, width), bf16)],
            flops=2 * 10**10,
        )(got, slot)
        return emb

    def exchange(x):
        return lax.all_to_all(x, ALL, 0, 0, tiled=True)

    pack = call(
        pack_kernel,
        shape((width // GROUPS * 2 + 2 * width // shards // GROUPS, units), bf16),
        [SM, ANY, ANY, ANY],
        VM,
        [pltpu.SemaphoreType.DMA((4,))],
        vmem=60,
    )(
        dp_at.reshape(1).astype(i32), feedforward_input_weight, feedforward_output_weight,
        attention_output_weight,
    )
    pack, slot_token_ids = lax.optimization_barrier((pack, slot_token_ids))
    weights = lax.all_gather(pack, ("head", "dp"), axis=0, tiled=True).reshape(shards, groups, *pack.shape)

    steps = shards // 2
    packed = jnp.concatenate(
        [
            query_key_value_weight.reshape(3 * width, local_w),
            adapter_up_maps.reshape(rank2, local_w).astype(bf16),
        ],
        0,
    )
    order = jnp.stack(
        [
            2 * ((head_at // 2 + step) % steps) + (head_at + column) % 2
            for step in range(steps)
            for column in range(2)
        ]
    ).astype(i32)

    def permuted(x, source):
        return lax.ppermute(x, "head", [(source(i), i) for i in range(shards)])

    packed_z = [permuted(packed, lambda i, step=step: (i + 2 * step) % shards) for step in range(1, steps)]
    requests, slot = ask(jnp.zeros((), i32), slot_token_ids)

    wanted = exchange(requests)
    rounds = jnp.max(wanted[:, 0, LANES - 1])
    wanted, packed_z = lax.optimization_barrier((wanted, packed_z))
    found = look(wanted)
    w_own = jnp.stack([packed, *packed_z])
    w_peer = permuted(w_own, lambda i: i ^ 1)
    emb = place(found, slot)

    def again(which):
        asked, where = ask(which, slot_token_ids)
        return place(look(exchange(asked)), where)

    unused_at, emb = lax.while_loop(
        lambda state: state[0] < rounds,
        lambda state: (state[0] + 1, state[1] + again(state[0])),
        (jnp.ones((), i32), emb),
    )

    own_len = lax.dynamic_slice_in_dim(lengths, head_at, 1)
    own_label = lax.dynamic_slice_in_dim(labels, head_at, 1)
    x0, x0b, xa, q, k, v, up = call(
        functools.partial(project_kernel, shards),
        (
            shape((slots, width), f32),
            shape((slots, width), bf16),
            shape((slots, rank2), bf16),
            shape((shards, slots, LANES), bf16),
            shape((shards, slots, LANES), bf16),
            shape((shards, slots, LANES), bf16),
            shape((shards, rank2, 2 * LANES), bf16),
        ),
        [VM, VM, VM, VM, VM, ANY, ANY],
        (VM,) * 7,
        [
            pltpu.VMEM((shards // 2, width, 6 * LANES), bf16),
            pltpu.VMEM((shards // 2, rank2, 6 * LANES), bf16),
            pltpu.SemaphoreType.DMA((shards // 2, 10)),
        ],
        vmem=50,
    )(emb, positions, layer_norm_gains, layer_norm_biases, down_maps, w_own, w_peer)
    lse, ctx = call(
        functools.partial(attend_kernel, shards),
        (shape((shards, 2, slots), f32), shape((slots, width), bf16)),
        [SM, SM, VM, VM, VM],
        (VM, VM),
        [pltpu.VMEM((slots, LANES), f32)],
        vmem=40,
    )(own_len, order, q, k, v)

    dctx, loss = call(
        functools.partial(middle_kernel, shards),
        (shape((slots, width), bf16), shape((1, LANES), f32)),
        [SM, SM, VM, VM, VM, VM, VM, ANY],
        (VM, VM),
        [
            pltpu.VMEM((shards, groups // 2, 2 * local_w // groups, width), bf16),
            pltpu.VMEM((shards, groups, width // groups, units), bf16),
            pltpu.VMEM((shards, groups, units // groups, width), bf16),
            pltpu.VMEM((shards, slots, units), f32),
            pltpu.VMEM((slots, width), f32),
            pltpu.VMEM((slots, width), f32),
            pltpu.VMEM((slots, width), bf16),
            pltpu.VMEM((slots, width), f32),
            pltpu.VMEM((slots, width), bf16),
            pltpu.VMEM((slots, 2 * units), bf16),
            pltpu.SemaphoreType.DMA((shards, 5)),
        ],
        vmem=60,
    )(
        own_len, own_label, x0, ctx, layer_norm_gains, layer_norm_biases, classifier, weights
    )

    send, norm = call(
        functools.partial(gradient_kernel, shards, groups),
        (shape((devices, 2 * rank2 * width // devices // LANES, LANES), bf16), shape((1, LANES), f32)),
        [SM, SM, VM, VM, VM, VM, VM, VM, VM, VM],
        (VM, VM),
        [pltpu.VMEM((width, rank2), f32), pltpu.VMEM((slots, rank2), f32)],
        vmem=50,
    )(own_len, order, x0b, xa, q, k, v, lse, dctx, up)

    got = exchange(send)
    examples = float(devices)
    step_number = optimizer_step_count.astype(f32)
    fixes = jnp.stack([1.0 - jnp.power(beta_one, step_number), 1.0 - jnp.power(beta_two, step_number)])
    where = jnp.stack([dp_at, head_at]).astype(i32)
    rows = width // devices
    moments = [turned(x) for x in (down_first_moment, down_second_moment, up_first_moment, up_second_moment)]
    lines = rows * rank2 // LANES + 2
    many = width // groups
    slices, down_rows = call(
        early_kernel,
        (shape((4, rows, 2 * rank2), f32), shape((3, many, rank2), f32)),
        [SM] + [VM] * 8,
        (VM, VM),
        [
            pltpu.VMEM((local_w, rank2), f32),
            pltpu.VMEM((width, rank2), f32),
            pltpu.VMEM((3, many, rank2), f32),
        ],
    )(where, down_maps, adapter_up_maps, *moments, turned(down_privacy_noise), turned(up_privacy_noise))
    tile, fresh = call(
        functools.partial(direction_kernel, examples),
        (shape((devices, lines, LANES), f32), shape((3, rows, 2 * rank2), f32)),
        [SM] + [VM] * 3,
        (VM, VM),
    )(fixes, got, loss, slices)
    spread = exchange(tile)
    down_shape = shape(moments[0].shape, f32)
    up_shape = shape(moments[2].shape, f32)
    loss_mean, dm1, dm2, dw, bm1, bm2, bw, table = call(
        functools.partial(update_kernel, examples, shards),
        (
            shape((1, 1), f32), down_shape, down_shape, down_shape, up_shape, up_shape, up_shape,
            shape((2, 4), f32),
        ),
        [SM, SM] + [VM] * 4,
        (VM,) * 8,
    )(where, fixes, spread, slices, down_rows, fresh)
    return (
        loss_mean.reshape(()),
        norm[0, 0:1],
        turned(dm1),
        turned(dm2),
        turned(dw),
        turned(bm1),
        turned(bm2),
        turned(bw),
        table.T,
    )


def solution(mesh):
    placed = (
        P("dp", None),
        P("dp"),
        P("dp"),
        P(),
        P("dp", "head"),
        P(),
        P(None, None, "head"),
        P("head", None),
        P(None, "head"),
        P("head", None),
        P(),
        P(),
        P(),
        P(),
        P(None, None, "head"),
        P(None, "dp", None),
        P(None, "dp", None),
        P(None, None, ("head", "dp")),
        P(None, None, ("head", "dp")),
        P(None, "dp", None),
        P(None, None, ("head", "dp")),
    )
    return jax.shard_map(
        per_device,
        mesh=mesh,
        in_specs=placed,
        out_specs=(
            P(),
            P(("dp", "head")),
            P(None, "dp", None),
            P(None, "dp", None),
            P(None, "dp", None),
            P(None, None, ("head", "dp")),
            P(None, None, ("head", "dp")),
            P(None, None, ("head", "dp")),
            P(),
        ),
        check_vma=False,
    )
```
